32 devices in a mesh: row: 8 (over y, x, core), col: 4 (over z).
Axes of the slice: x: 2, y: 2, z: 4, core: 2. Of those that a mesh axis runs over, the one named last changes fastest.
Arguments:
- pair_map: float32 [128, 8192], P('row', 'col'), may hold values from -40 to 40
- cotangent: float32 [128, 8192], P('row', 'col'), may hold values from -50 to 50
- conv_one: float32 [3, 3, 64, 64], replicated, may hold values from -0.25 to 0.25
- conv_two: float32 [3, 3, 64, 64], replicated, may hold values from -0.25 to 0.25
- norm_gain: float32 [2, 64], replicated, may hold values from 0.5 to 2
- norm_shift: float32 [2, 64], replicated, may hold values from -2 to 2
Outputs:
- sym_out: float32 [128, 8192], P('row', 'col')
- grad_map: float32 [128, 8192], P('row', 'col')
- grad_one: float32 [3, 3, 64, 64], replicated
- grad_two: float32 [3, 3, 64, 64], replicated
- grad_gain: float32 [2, 64], replicated
- grad_shift: float32 [2, 64], replicated
The draws below stay inside these ranges and needn't reach their ends.
All inputs are finite; a program needn't handle non-finite values.
Results may differ from the reference program's by a relative error of at most 0.000086.
Values sent between devices are 32-bit elements; how exact they have to be, the bound alone decides.
No kernel may reach another device: no remote copies, remote signals or barrier semaphores. Data moves between devices by JAX's collectives and lax.ppermute only.
A program may use at most 64 MiB of HBM per device.

```python
import math
import jax
import jax.numpy as jnp
from jax import lax

CH = 64
DILATION_STEP = 16
NRES = 128


def rising_field(key, strength):
    noise_key, rough_key, offset_key = jax.random.split(key, 3)
    base = jnp.clip(jax.random.normal(noise_key, (NRES, NRES, CH), jnp.float32), -5.0, 5.0)
    ratio = 3.0
    rough = jax.random.uniform(rough_key, (NRES, NRES, 1), jnp.float32, 0.5, 1.5)
    offset = jnp.clip(jax.random.normal(offset_key, (CH,), jnp.float32) * 0.5, -1.5, 1.5)
    place = jnp.arange(NRES, dtype=jnp.float32) / NRES
    scale = jnp.exp(math.log(ratio) * (place[:, None] + place[None, :]))
    values = strength * scale[:, :, None] * rough * (base + offset)
    return values.reshape(NRES, NRES * CH)


def draw_pair_map(key, part):
    return rising_field(jax.random.fold_in(key, 11), 0.4)


def draw_cotangent(key, part):
    return rising_field(jax.random.fold_in(key, 23), 0.5)


def bell_draw(stream_key, shape, spread, limit, kind=jnp.bfloat16):
    entries = spread * jax.random.normal(stream_key, shape, jnp.float32)
    return jnp.clip(entries, min=-limit, max=limit).astype(kind)


def setup_inputs(seed: int = 0) -> dict:
    key_of = jax.random.split(jax.random.key(seed), 7)
    pair_map = draw_pair_map(jax.random.fold_in(key_of[6], 71), 0)
    cotangent = draw_cotangent(jax.random.fold_in(key_of[6], 71), 0)
    conv_one = bell_draw(key_of[2], (3, 3, CH, CH), (9 * CH) ** -0.5, 0.25, jnp.float32)
    conv_two = bell_draw(key_of[3], (3, 3, CH, CH), (9 * CH) ** -0.5, 0.25, jnp.float32)
    norm_gain = jnp.clip(jnp.exp(jax.random.uniform(key_of[4], (2, CH), jnp.float32, math.log(0.5), math.log(2.0))), 0.5, 2.0)
    norm_shift = bell_draw(key_of[5], (2, CH), 0.5, 2.0, jnp.float32)
    return dict(pair_map=pair_map, cotangent=cotangent, conv_one=conv_one, conv_two=conv_two, norm_gain=norm_gain, norm_shift=norm_shift)


def convolve(feature_field_grid, filter_weight):
    block_result = lax.conv_general_dilated(feature_field_grid[None], filter_weight, (1, 1), ((DILATION_STEP, DILATION_STEP), (DILATION_STEP, DILATION_STEP)), rhs_dilation=(DILATION_STEP, DILATION_STEP), dimension_numbers=('NHWC', 'HWIO', 'NHWC'), precision=lax.Precision.HIGHEST)
    return block_result[0]

def instance(hidden, gain_row, shift_row):
    average = lax.optimization_barrier(jnp.mean(hidden, axis=(0, 1)))
    centered = hidden - average
    variance = lax.optimization_barrier(jnp.mean(centered * centered, axis=(0, 1)))
    return centered * lax.rsqrt(variance + 1e-05) * gain_row + shift_row

def block(feature_field_grid, conv_one, conv_two, norm_gain, norm_shift):
    active = jax.nn.elu(instance(convolve(feature_field_grid, conv_one), norm_gain[0], norm_shift[0]))
    summed = feature_field_grid + instance(convolve(active, conv_two), norm_gain[1], norm_shift[1])
    output = jax.nn.elu(summed)
    return 0.5 * (output + jnp.transpose(output, (1, 0, 2)))

def reference(pair_map, cotangent, conv_one, conv_two, norm_gain, norm_shift):
    feature_field_grid = pair_map.reshape(NRES, NRES, CH)
    grad_in = cotangent.reshape(NRES, NRES, CH)
    symmetric, pullback = jax.vjp(block, feature_field_grid, conv_one, conv_two, norm_gain, norm_shift)
    grad_field, grad_first, grad_second, grad_gains, grad_shifts = pullback(grad_in)
    return (symmetric.reshape(NRES, NRES * CH), grad_field.reshape(NRES, NRES * CH), grad_first / NRES, grad_second / NRES, grad_gains / NRES, grad_shifts / NRES)
```

```python
import functools

import jax
import jax.numpy as jnp
from jax import lax
from jax.experimental import pallas as pl
from jax.experimental.pallas import tpu as pltpu
from jax.sharding import PartitionSpec as P

DILATION_STEP = 16


epsilon = 1e-05
highest = lax.Precision.HIGHEST


def extended_2(cells, sides, width):
    for axis, dim in sides:
        count = lax.axis_size(axis)
        ends = count - 1
        head = lax.slice_in_dim(cells, 0, width, axis=dim)
        tail = lax.slice_in_dim(cells, cells.shape[dim] - width, cells.shape[dim], axis=dim)
        cells = jnp.concatenate(
            [
                lax.ppermute(tail, axis, [(i, (i + 1) % count) for i in range(ends)]),
                cells,
                lax.ppermute(head, axis, [((i + 1) % count, i) for i in range(ends)]),
            ],
            axis=dim,
        )
    return cells


def extend(feature_field_patch):
    block_result = extended_2(feature_field_patch, (("row", 0), ("col", 1)), DILATION_STEP)
    return block_result


def tap_windows(extended, row_begin, column_starts, local_row_count, local_column_count):
    pieces = [
        extended[row_begin : row_begin + local_row_count, start : start + local_column_count]
        for start in column_starts
    ]
    joined = jnp.concatenate(pieces, axis=2)
    return joined.reshape(local_row_count * local_column_count, -1)


def dilated(extended, filter_weight, local_row_count, local_column_count):
    channels = filter_weight.shape[2]
    starts = [tap * DILATION_STEP for tap in range(3)]
    summed_taps = jnp.zeros(
        (local_row_count * local_column_count, filter_weight.shape[3]), jnp.float32
    )
    for filter_tap_row in range(3):
        window = tap_windows(
            extended, filter_tap_row * DILATION_STEP, starts, local_row_count, local_column_count
        )
        stacked = filter_weight[filter_tap_row].reshape(3 * channels, -1)
        summed_taps = summed_taps + jnp.dot(
            window, stacked, precision=highest, preferred_element_type=jnp.float32
        )
    return summed_taps.reshape(local_row_count, local_column_count, -1)


def dilated_back(grad_ext, filter_weight, local_row_count, local_column_count):
    channels = filter_weight.shape[3]
    starts = [(2 - tap) * DILATION_STEP for tap in range(3)]
    summed_taps = jnp.zeros(
        (local_row_count * local_column_count, filter_weight.shape[2]), jnp.float32
    )
    for filter_tap_row in range(3):
        window = tap_windows(
            grad_ext,
            (2 - filter_tap_row) * DILATION_STEP,
            starts,
            local_row_count,
            local_column_count,
        )
        stacked = jnp.transpose(filter_weight[filter_tap_row], (0, 2, 1)).reshape(3 * channels, -1)
        summed_taps = summed_taps + jnp.dot(
            window, stacked, precision=highest, preferred_element_type=jnp.float32
        )
    return summed_taps.reshape(local_row_count, local_column_count, -1)


def kernel_grad(extended, grad_tile, local_row_count, local_column_count):
    channels = extended.shape[2]
    starts = [tap * DILATION_STEP for tap in range(3)]
    grad_flat = grad_tile.reshape(-1, grad_tile.shape[2])
    tap_list = []
    for filter_tap_row in range(3):
        window = tap_windows(
            extended, filter_tap_row * DILATION_STEP, starts, local_row_count, local_column_count
        )
        product = lax.dot_general(
            window,
            grad_flat,
            (((0,), (0,)), ((), ())),
            precision=highest,
            preferred_element_type=jnp.float32,
        )
        tap_list.append(product.reshape(3, channels, -1))
    return jnp.stack(tap_list)


def normalize(hidden, cell_count):
    totals = lax.psum(jnp.sum(hidden, axis=(0, 1)), ("row", "col"))
    average = totals / cell_count
    centered = hidden - average
    spread = lax.psum(jnp.sum(centered * centered, axis=(0, 1)), ("row", "col"))
    variance = spread / cell_count
    inverse = lax.rsqrt(variance + epsilon)
    return ((hidden - average) * inverse, inverse)


def normalize_back(grad_normed, normed, inverse, gain_row, cell_count):
    shift_sum, gain_sum = lax.psum(
        (jnp.sum(grad_normed, axis=(0, 1)), jnp.sum(grad_normed * normed, axis=(0, 1))),
        ("row", "col"),
    )
    grad_scaled = grad_normed * gain_row
    grad_hidden = inverse * (
        grad_scaled
        - gain_row * shift_sum / cell_count
        - normed * (gain_row * gain_sum / cell_count)
    )
    return (grad_hidden, gain_sum, shift_sum)


def elu_slope(values):
    return jnp.where(values > 0, 1.0, jnp.exp(jnp.minimum(values, 0.0)))


def mirror_tile(tile_in):
    local_row_count, local_column_count, channels = tile_in.shape
    row_devices = lax.axis_size("row")
    col_devices = lax.axis_size("col")
    row_part = local_row_count // col_devices
    group = row_devices // col_devices
    sectioned = tile_in.reshape(col_devices, row_part, local_column_count, channels)
    sectioned = lax.all_to_all(sectioned, "col", split_axis=0, concat_axis=0, tiled=True)
    sectioned = (
        sectioned.reshape(col_devices, row_part, group, local_row_count, channels)
        .transpose(0, 2, 1, 3, 4)
        .reshape(row_devices, row_part, local_row_count, channels)
    )
    sectioned = lax.all_to_all(
        lax.all_to_all(sectioned, "row", split_axis=0, concat_axis=0, tiled=True),
        "col",
        split_axis=0,
        concat_axis=0,
        tiled=True,
    )
    sectioned = sectioned.reshape(
        col_devices, group, row_part, local_row_count, channels
    ).transpose(3, 1, 0, 2, 4)
    return sectioned.reshape(local_row_count, local_column_count, channels)


def general_body(pair_map, cotangent, conv_one, conv_two, norm_gain, norm_shift):
    channels = conv_one.shape[2]
    local_row_count = pair_map.shape[0]
    local_column_count = pair_map.shape[1] // channels
    residues = float(local_row_count * lax.axis_size("row"))
    cell_count = float(
        local_row_count * local_column_count * lax.axis_size("row") * lax.axis_size("col")
    )
    feature_field_patch = pair_map.reshape(local_row_count, local_column_count, channels)
    field_ext = extend(feature_field_patch)
    first_conv = dilated(field_ext, conv_one, local_row_count, local_column_count)
    normed_one, inverse_one = normalize(first_conv, cell_count)
    before_one = normed_one * norm_gain[0] + norm_shift[0]
    active = jax.nn.elu(before_one)
    active_ext = extend(active)
    second_conv = dilated(active_ext, conv_two, local_row_count, local_column_count)
    normed_two, inverse_two = normalize(second_conv, cell_count)
    summed = feature_field_patch + normed_two * norm_gain[1] + norm_shift[1]
    block_out = jax.nn.elu(summed)
    symmetric = 0.5 * (block_out + mirror_tile(block_out))
    grad_in = cotangent.reshape(local_row_count, local_column_count, channels)
    grad_out = 0.5 * (grad_in + mirror_tile(grad_in))
    grad_sum = grad_out * elu_slope(summed)
    grad_second, gain_two, shift_two = normalize_back(
        grad_sum, normed_two, inverse_two, norm_gain[1], cell_count
    )
    second_ext = extend(grad_second)
    grad_active = dilated_back(second_ext, conv_two, local_row_count, local_column_count)
    kernel_two = kernel_grad(active_ext, grad_second, local_row_count, local_column_count)
    grad_before = grad_active * elu_slope(before_one)
    grad_first, gain_one, shift_one = normalize_back(
        grad_before, normed_one, inverse_one, norm_gain[0], cell_count
    )
    first_ext = extend(grad_first)
    grad_field = grad_sum + dilated_back(first_ext, conv_one, local_row_count, local_column_count)
    kernel_one = kernel_grad(field_ext, grad_first, local_row_count, local_column_count)
    total_one, total_two = lax.psum((kernel_one, kernel_two), ("row", "col"))
    grad_gains = jnp.stack([gain_one, gain_two]) / residues
    grad_shifts = jnp.stack([shift_one, shift_two]) / residues
    return (
        symmetric.reshape(local_row_count, local_column_count * channels),
        grad_field.reshape(local_row_count, local_column_count * channels),
        total_one / residues,
        total_two / residues,
        grad_gains,
        grad_shifts,
    )


SLOTS = 8
LANES = 128
HALF = 64
ROWS = 256
AXES = ("row", "col")


def phase_table(devices):
    pairs = [(r, s) for r in range(DILATION_STEP) for s in range(r + 1, DILATION_STEP)]
    table = []
    taken = 0
    diagonal = DILATION_STEP // 2
    for device in range(devices):
        count = SLOTS // 2 - (1 if device < diagonal else 0)
        upper = pairs[taken : taken + count]
        taken += count
        lower = [(s, r) for r, s in upper]
        if device < diagonal:
            upper = upper + [(2 * device, 2 * device)]
            lower = lower + [(2 * device + 1, 2 * device + 1)]
        table.append(upper + lower)
    return table


def lane_low(shape):
    return lax.broadcasted_iota(jnp.int32, shape, len(shape) - 1) < HALF


def swap_halves(values):
    return pltpu.roll(values, HALF, values.ndim - 1)


def fold_halves(values):
    return values + swap_halves(values)


def twice(row):
    return jnp.concatenate([row, row], axis=1)


def exact_dot(left, right, dims):
    return lax.dot_general(
        left, right, (dims, ((), ())), precision=highest, preferred_element_type=jnp.float32
    )


def split_phases(tile_ref, scratch_ref):
    low = lane_low((DILATION_STEP, LANES))
    for t in range(DILATION_STEP // 2):
        first = tile_ref[:, t * LANES : (t + 1) * LANES]
        begin = DILATION_STEP * HALF + t * LANES
        second = tile_ref[:, begin : begin + LANES]
        row = 2 * t * DILATION_STEP
        scratch_ref[row : row + DILATION_STEP, :] = jnp.where(low, first, swap_halves(second))
        row += DILATION_STEP
        scratch_ref[row : row + DILATION_STEP, :] = jnp.where(low, swap_halves(first), second)


def join_phases(scratch_ref, tile_ref):
    low = lane_low((DILATION_STEP, LANES))
    for t in range(DILATION_STEP // 2):
        row = 2 * t * DILATION_STEP
        even = scratch_ref[row : row + DILATION_STEP, :]
        odd = scratch_ref[row + DILATION_STEP : row + 2 * DILATION_STEP, :]
        tile_ref[:, t * LANES : (t + 1) * LANES] = jnp.where(low, even, swap_halves(odd))
        begin = DILATION_STEP * HALF + t * LANES
        tile_ref[:, begin : begin + LANES] = jnp.where(low, swap_halves(even), odd)


def pack_rows(table, scratch_ref, send_ref, stride):
    for device, slots in enumerate(table):
        for k, (r, s) in enumerate(slots):
            source = s * DILATION_STEP + r
            target = device * stride + k
            send_ref[target : target + 1, :] = scratch_ref[source : source + 1, :]


def unpack_rows(table, recv_ref, scratch_ref, stride, offset):
    for device, slots in enumerate(table):
        for k, (r, s) in enumerate(slots):
            target = s * DILATION_STEP + r
            source = device * stride + offset + k
            scratch_ref[target : target + 1, :] = recv_ref[source : source + 1, :]


def slot_rows(ref, stride, devices):
    return jnp.concatenate(
        [ref[d * stride : d * stride + SLOTS, :] for d in range(devices)], axis=0
    )


def neighbours(values):
    zero = jnp.zeros((SLOTS, LANES), jnp.float32)
    ahead = jnp.concatenate([values[SLOTS:], zero], axis=0)
    behind = jnp.concatenate([zero, values[:-SLOTS]], axis=0)
    place = (lax.broadcasted_iota(jnp.int32, (ROWS, LANES), 0) // SLOTS) % 4
    low = lane_low((ROWS, LANES))
    side = jnp.where(low, jnp.where(place == 3, 0.0, ahead), jnp.where(place == 0, 0.0, behind))
    return jnp.concatenate([side, values], axis=1)


def forward_weight(weight_ref):
    zero = jnp.zeros((HALF, HALF), jnp.float32)
    taps = []
    for a in range(3):
        w = [weight_ref[a, b] for b in range(3)]
        blocks = [(zero, w[2]), (w[0], zero), (w[1], w[0]), (w[2], w[1])]
        taps.append(
            jnp.concatenate([jnp.concatenate(list(b), axis=1) for b in blocks], axis=0)
        )
    return jnp.concatenate(taps, axis=1)


def backward_weight(weight_ref):
    zero = jnp.zeros((HALF, HALF), jnp.float32)
    taps = []
    for a in range(3):
        w = [weight_ref[2 - a, 2 - b] for b in range(3)]
        taps.append(jnp.concatenate([zero, w[0], w[1], w[2]], axis=1))
        taps.append(jnp.concatenate([w[2], zero, w[0], w[1]], axis=1))
    return jnp.concatenate(taps, axis=0)


def shifted_sum(parts):
    step = 4 * SLOTS
    zero = jnp.zeros((step, LANES), jnp.float32)
    first, middle, last = (parts[:, a * LANES : (a + 1) * LANES] for a in range(3))
    return (
        middle
        + jnp.concatenate([zero, first[:-step]], axis=0)
        + jnp.concatenate([last[step:], zero], axis=0)
    )


def spread_shifts(values):
    step = 4 * SLOTS
    zero = jnp.zeros((step, LANES), jnp.float32)
    return jnp.concatenate(
        [
            jnp.concatenate([values[step:], zero], axis=0),
            values,
            jnp.concatenate([zero, values[:-step]], axis=0),
        ],
        axis=1,
    )


def kernel_rows(joined, grad):
    product = exact_dot(joined, spread_shifts(grad), ((0,), (0,)))
    pieces = []
    for a in range(3):
        part = product[:, a * LANES : (a + 1) * LANES]
        for even, odd in ((1, 2), (2, 3), (3, 0)):
            tap = part[even * HALF : (even + 1) * HALF] + swap_halves(
                part[odd * HALF : (odd + 1) * HALF]
            )
            low = lane_low((HALF // 2, LANES))
            pieces.append(jnp.where(low, tap[: HALF // 2], swap_halves(tap[HALF // 2 :])))
    return jnp.concatenate(pieces, axis=0)


def local_stats(hidden):
    count = 2.0 * ROWS
    mean = fold_halves(jnp.sum(hidden, axis=0, keepdims=True)) / count
    centered = hidden - mean
    spread = fold_halves(jnp.sum(centered * centered, axis=0, keepdims=True))
    return jnp.where(lane_low((1, LANES)), mean, spread)


def combine_stats(rows, devices):
    low = lane_low((devices, LANES))
    means = jnp.where(low, rows, swap_halves(rows))
    spreads = jnp.where(low, swap_halves(rows), rows)
    mean = jnp.sum(means, axis=0, keepdims=True) / devices
    apart = means - mean
    total = jnp.sum(spreads + (2.0 * ROWS) * (apart * apart), axis=0, keepdims=True)
    return mean, lax.rsqrt(total / (2.0 * ROWS * devices) + epsilon)


def elu_value(values):
    return jnp.where(values > 0, values, jnp.exp(jnp.minimum(values, 0.0)) - 1.0)


def pair_sums(grad, normed):
    plain = fold_halves(jnp.sum(grad, axis=0, keepdims=True))
    scaled = fold_halves(jnp.sum(grad * normed, axis=0, keepdims=True))
    return jnp.where(lane_low((1, LANES)), plain, scaled)


def split_sums(rows):
    total = jnp.sum(rows, axis=0, keepdims=True)
    other = swap_halves(total)
    low = lane_low((1, LANES))
    return jnp.where(low, total, other), jnp.where(low, other, total)


def norm_back(grad, normed, inverse, gain, shift_sum, gain_sum, cells):
    return inverse * (gain * grad - gain * shift_sum / cells - normed * (gain * gain_sum / cells))


def mirrored(values, own_mask):
    low = lane_low((SLOTS, LANES))
    tiles = [values[i * SLOTS : (i + 1) * SLOTS] for i in range(ROWS // SLOTS)]
    pieces = []
    for p in range(SLOTS):
        for c in range(4):
            even = tiles[2 * c * 4 + p // 2]
            odd = tiles[(2 * c + 1) * 4 + p // 2]
            if p % 2 == 0:
                piece = jnp.where(low, even, swap_halves(odd))
            else:
                piece = jnp.where(low, swap_halves(even), odd)
            pieces.append(jnp.where(own_mask, piece, pltpu.roll(piece, 4, 0)))
    return jnp.concatenate(pieces, axis=0)


def first_kernel(table, x_ref, send_ref, scratch_ref):
    split_phases(x_ref, scratch_ref)
    pack_rows(table, scratch_ref, send_ref, SLOTS)


def conv_one_kernel(table, x_ref, weight_ref, g_ref, hidden_ref, send_ref, scratch_ref):
    split_phases(g_ref, scratch_ref)
    stride = SLOTS + 1
    pack_rows(table, scratch_ref, send_ref, stride)
    hidden = shifted_sum(
        exact_dot(neighbours(x_ref[...]), forward_weight(weight_ref), ((1,), (0,)))
    )
    hidden_ref[...] = hidden
    stats = local_stats(hidden)
    for d in range(len(table)):
        send_ref[d * stride + SLOTS : (d + 1) * stride, :] = stats


def conv_two_kernel(
    devices, recv_ref, hidden_ref, weight_ref, gain_ref, shift_ref,
    normed_ref, inverse_ref, active_ref, second_ref, send_ref,
):
    stride = SLOTS + 1
    mean, inverse = combine_stats(recv_ref[pl.ds(SLOTS, devices, stride=stride), :], devices)
    normed = (hidden_ref[...] - mean) * inverse
    normed_ref[...] = normed
    inverse_ref[...] = inverse
    active = elu_value(normed * twice(gain_ref[0:1, :]) + twice(shift_ref[0:1, :]))
    active_ref[...] = active
    second = shifted_sum(
        exact_dot(neighbours(active), forward_weight(weight_ref), ((1,), (0,)))
    )
    second_ref[...] = second
    send_ref[...] = jnp.broadcast_to(local_stats(second), (devices, LANES))


def output_kernel(
    devices, recv_ref, second_ref, x_ref, grad_ref, gain_ref, shift_ref, own_ref,
    normed_ref, inverse_ref, sum_ref, send_ref,
):
    stride = SLOTS + 1
    mean, inverse = combine_stats(recv_ref[...], devices)
    normed = (second_ref[...] - mean) * inverse
    normed_ref[...] = normed
    inverse_ref[...] = inverse
    summed = x_ref[...] + normed * twice(gain_ref[1:2, :]) + twice(shift_ref[1:2, :])
    slope = jnp.exp(jnp.minimum(summed, 0.0))
    out = jnp.where(summed > 0, summed, slope - 1.0)
    own = own_ref[...] > 0
    symmetric = 0.5 * (out + mirrored(out, own))
    for d in range(devices):
        send_ref[d * stride : d * stride + SLOTS, :] = symmetric[d * SLOTS : (d + 1) * SLOTS]
    grad_in = slot_rows(grad_ref, stride, devices)
    grad_out = 0.5 * (grad_in + mirrored(grad_in, own))
    grad_sum = grad_out * jnp.where(summed > 0, 1.0, slope)
    sum_ref[...] = grad_sum
    sums = pair_sums(grad_sum, normed)
    for d in range(devices):
        send_ref[d * stride + SLOTS : (d + 1) * stride, :] = sums


def back_two_kernel(
    devices, recv_ref, sum_ref, normed_two_ref, inverse_two_ref, active_ref, normed_ref,
    weight_ref, gain_ref, shift_ref, before_ref, total_ref, send_ref, scratch_ref,
):
    cells = 2.0 * ROWS * devices
    shift_sum, gain_sum = split_sums(recv_ref[pl.ds(SLOTS, devices, stride=SLOTS + 1), :])
    total_ref[...] = jnp.where(lane_low((1, LANES)), shift_sum, gain_sum)
    grad_second = norm_back(
        sum_ref[...], normed_two_ref[...], inverse_two_ref[...], twice(gain_ref[1:2, :]),
        shift_sum, gain_sum, cells,
    )
    grad_active = shifted_sum(
        exact_dot(neighbours(grad_second), backward_weight(weight_ref), ((1,), (1,)))
    )
    normed = normed_ref[...]
    before = normed * twice(gain_ref[0:1, :]) + twice(shift_ref[0:1, :])
    grad_before = grad_active * jnp.where(before > 0, 1.0, jnp.exp(jnp.minimum(before, 0.0)))
    before_ref[...] = grad_before
    sums = pair_sums(grad_before, normed)
    share = ROWS * 9 // 8 // devices
    stride = share + 1
    scratch_ref[...] = kernel_rows(neighbours(active_ref[...]), grad_second)
    for d in range(devices):
        send_ref[d * stride : d * stride + share, :] = scratch_ref[d * share : (d + 1) * share, :]
        send_ref[d * stride + share : (d + 1) * stride, :] = sums


def reduce_share(ref, devices, share, stride):
    total = ref[0:share, :]
    for d in range(1, devices):
        total = total + ref[d * stride : d * stride + share, :]
    return total


def back_one_kernel(
    devices, recv_ref, before_ref, normed_ref, inverse_ref, x_ref, sum_ref, weight_ref, gain_ref,
    total_ref, two_ref, send_ref, scratch_ref,
):
    cells = 2.0 * ROWS * devices
    share = ROWS * 9 // 8 // devices
    stride = share + 1
    shift_sum, gain_sum = split_sums(recv_ref[pl.ds(share, devices, stride=stride), :])
    total_ref[...] = jnp.where(lane_low((1, LANES)), shift_sum, gain_sum)
    two_ref[...] = reduce_share(recv_ref, devices, share, stride)
    grad_first = norm_back(
        before_ref[...], normed_ref[...], inverse_ref[...], twice(gain_ref[0:1, :]),
        shift_sum, gain_sum, cells,
    )
    field = sum_ref[...] + shifted_sum(
        exact_dot(neighbours(grad_first), backward_weight(weight_ref), ((1,), (1,)))
    )
    scratch_ref[...] = kernel_rows(neighbours(x_ref[...]), grad_first)
    stride = share + SLOTS
    for d in range(devices):
        send_ref[d * stride : d * stride + SLOTS, :] = field[d * SLOTS : (d + 1) * SLOTS]
        send_ref[d * stride + SLOTS : (d + 1) * stride, :] = scratch_ref[
            d * share : (d + 1) * share, :
        ]


def share_kernel(devices, recv_ref, two_ref, send_ref):
    share = ROWS * 9 // 8 // devices
    stride = share + SLOTS
    total = recv_ref[SLOTS:stride, :]
    for d in range(1, devices):
        total = total + recv_ref[d * stride + SLOTS : (d + 1) * stride, :]
    two = two_ref[...]
    for d in range(devices):
        send_ref[2 * d * share : (2 * d + 1) * share, :] = total
        send_ref[(2 * d + 1) * share : (2 * d + 2) * share, :] = two


def last_kernel(
    table, residues, sym_recv_ref, map_recv_ref, recv_ref, total_one_ref, total_two_ref,
    sym_ref, map_ref, one_ref, two_ref, gain_ref, shift_ref, scratch_ref, rows_ref,
):
    devices = len(table)
    share = ROWS * 9 // 8 // devices
    unpack_rows(table, sym_recv_ref, scratch_ref, SLOTS + 1, 0)
    join_phases(scratch_ref, sym_ref)
    unpack_rows(table, map_recv_ref, scratch_ref, SLOTS + share, 0)
    join_phases(scratch_ref, map_ref)
    for index, out_ref in ((0, one_ref), (1, two_ref)):
        for d in range(devices):
            begin = (2 * d + index) * share
            rows_ref[d * share : (d + 1) * share, :] = recv_ref[begin : begin + share, :]
        for tap in range(9):
            block = rows_ref[tap * HALF // 2 : (tap + 1) * HALF // 2, :] / residues
            out_ref[tap, : HALF // 2, :] = block[:, :HALF]
            out_ref[tap, HALF // 2 :, :] = swap_halves(block)[:, :HALF]
    for index, total_ref in ((0, total_one_ref), (1, total_two_ref)):
        total = total_ref[...] / residues
        shift_ref[index : index + 1, :] = total[:, :HALF]
        gain_ref[index : index + 1, :] = swap_halves(total)[:, :HALF]


def call(body, shapes, scratch=()):
    return pl.pallas_call(
        body,
        out_shape=[jax.ShapeDtypeStruct(s, jnp.float32) for s in shapes],
        scratch_shapes=[pltpu.VMEM(s, jnp.float32) for s in scratch],
    )


def exchange(rows, devices):
    sent = rows.reshape(devices, 1, -1)
    received = lax.all_to_all(sent, AXES, split_axis=0, concat_axis=0, tiled=True)
    return received.reshape(-1, LANES)


def phase_body(pair_map, cotangent, conv_one, conv_two, norm_gain, norm_shift):
    devices = lax.axis_size("row") * lax.axis_size("col")
    residues = float(pair_map.shape[0] * lax.axis_size("row"))
    table = phase_table(devices)
    share = ROWS * 9 // 8 // devices
    whole, line = (ROWS, LANES), (1, LANES)
    part = functools.partial
    me = lax.axis_index("row") * lax.axis_size("col") + lax.axis_index("col")
    slot = lax.broadcasted_iota(jnp.int32, (SLOTS, LANES), 0)
    own = ((slot % 4 == 3) & (me < DILATION_STEP // 2)).astype(jnp.float32)

    (send,) = call(part(first_kernel, table), [whole], [whole])(pair_map)
    x = exchange(send, devices)
    hidden, send = call(
        part(conv_one_kernel, table), [whole, (devices * (SLOTS + 1), LANES)], [whole]
    )(x, conv_one, cotangent)
    grad_recv = exchange(send, devices)
    normed_one, inverse_one, active, second, send = call(
        part(conv_two_kernel, devices), [whole, line, whole, whole, (devices, LANES)]
    )(grad_recv, hidden, conv_two, norm_gain, norm_shift)
    recv = exchange(send, devices)
    normed_two, inverse_two, grad_sum, send = call(
        part(output_kernel, devices), [whole, line, whole, (devices * (SLOTS + 1), LANES)]
    )(recv, second, x, grad_recv, norm_gain, norm_shift, own)
    sym_recv = exchange(send, devices)
    grad_before, total_two, send = call(
        part(back_two_kernel, devices),
        [whole, line, (devices * (share + 1), LANES)],
        [(devices * share, LANES)],
    )(
        sym_recv, grad_sum, normed_two, inverse_two, active, normed_one, conv_two,
        norm_gain, norm_shift,
    )
    recv = exchange(send, devices)
    total_one, kernel_two, send = call(
        part(back_one_kernel, devices),
        [line, (share, LANES), (devices * (share + SLOTS), LANES)],
        [(devices * share, LANES)],
    )(recv, grad_before, normed_one, inverse_one, x, grad_sum, conv_one, norm_gain)
    map_recv = exchange(send, devices)
    (send,) = call(part(share_kernel, devices), [(2 * devices * share, LANES)])(
        map_recv, kernel_two
    )
    recv = exchange(send, devices)
    taps = conv_one.shape[0] * conv_one.shape[1]
    sym_out, grad_map, grad_one, grad_two, grad_gain, grad_shift = call(
        part(last_kernel, table, residues),
        [
            pair_map.shape, pair_map.shape, (taps, HALF, HALF), (taps, HALF, HALF),
            norm_gain.shape, norm_shift.shape,
        ],
        [whole, (devices * share, LANES)],
    )(sym_recv, map_recv, recv, total_one, total_two)
    return (
        sym_out,
        grad_map,
        grad_one.reshape(conv_one.shape),
        grad_two.reshape(conv_two.shape),
        grad_gain,
        grad_shift,
    )


def body(pair_map, cotangent, conv_one, conv_two, norm_gain, norm_shift):
    devices = lax.axis_size("row") * lax.axis_size("col")
    fits = (
        conv_one.shape == (3, 3, HALF, HALF)
        and pair_map.shape == (DILATION_STEP, 2 * DILATION_STEP * HALF)
        and lax.axis_size("row") == SLOTS
        and lax.axis_size("col") == 4
    )
    plan = phase_body if fits else general_body
    return plan(pair_map, cotangent, conv_one, conv_two, norm_gain, norm_shift)


def solution(mesh):
    return jax.shard_map(
        body,
        mesh=mesh,
        in_specs=(P("row", "col"), P("row", "col"), P(), P(), P(), P()),
        out_specs=(P("row", "col"), P("row", "col"), P(), P(), P(), P()),
        check_vma=False,
    )
```

```python
import functools

import jax
import jax.numpy as jnp
from jax import lax
from jax.experimental import pallas as pl
from jax.experimental.pallas import tpu as pltpu
from jax.sharding import PartitionSpec as P

DILATION_STEP = 16


epsilon = 1e-05
highest = lax.Precision.HIGHEST


def extended_2(cells, sides, width):
    for axis, dim in sides:
        count = lax.axis_size(axis)
        ends = count - 1
        head = lax.slice_in_dim(cells, 0, width, axis=dim)
        tail = lax.slice_in_dim(cells, cells.shape[dim] - width, cells.shape[dim], axis=dim)
        cells = jnp.concatenate(
            [
                lax.ppermute(tail, axis, [(i, (i + 1) % count) for i in range(ends)]),
                cells,
                lax.ppermute(head, axis, [((i + 1) % count, i) for i in range(ends)]),
            ],
            axis=dim,
        )
    return cells


def extend(feature_field_patch):
    block_result = extended_2(feature_field_patch, (("row", 0), ("col", 1)), DILATION_STEP)
    return block_result


def tap_windows(extended, row_begin, column_starts, local_row_count, local_column_count):
    pieces = [
        extended[row_begin : row_begin + local_row_count, start : start + local_column_count]
        for start in column_starts
    ]
    joined = jnp.concatenate(pieces, axis=2)
    return joined.reshape(local_row_count * local_column_count, -1)


def dilated(extended, filter_weight, local_row_count, local_column_count):
    channels = filter_weight.shape[2]
    starts = [tap * DILATION_STEP for tap in range(3)]
    summed_taps = jnp.zeros(
        (local_row_count * local_column_count, filter_weight.shape[3]), jnp.float32
    )
    for filter_tap_row in range(3):
        window = tap_windows(
            extended, filter_tap_row * DILATION_STEP, starts, local_row_count, local_column_count
        )
        stacked = filter_weight[filter_tap_row].reshape(3 * channels, -1)
        summed_taps = summed_taps + jnp.dot(
            window, stacked, precision=highest, preferred_element_type=jnp.float32
        )
    return summed_taps.reshape(local_row_count, local_column_count, -1)


def dilated_back(grad_ext, filter_weight, local_row_count, local_column_count):
    channels = filter_weight.shape[3]
    starts = [(2 - tap) * DILATION_STEP for tap in range(3)]
    summed_taps = jnp.zeros(
        (local_row_count * local_column_count, filter_weight.shape[2]), jnp.float32
    )
    for filter_tap_row in range(3):
        window = tap_windows(
            grad_ext,
            (2 - filter_tap_row) * DILATION_STEP,
            starts,
            local_row_count,
            local_column_count,
        )
        stacked = jnp.transpose(filter_weight[filter_tap_row], (0, 2, 1)).reshape(3 * channels, -1)
        summed_taps = summed_taps + jnp.dot(
            window, stacked, precision=highest, preferred_element_type=jnp.float32
        )
    return summed_taps.reshape(local_row_count, local_column_count, -1)


def kernel_grad(extended, grad_tile, local_row_count, local_column_count):
    channels = extended.shape[2]
    starts = [tap * DILATION_STEP for tap in range(3)]
    grad_flat = grad_tile.reshape(-1, grad_tile.shape[2])
    tap_list = []
    for filter_tap_row in range(3):
        window = tap_windows(
            extended, filter_tap_row * DILATION_STEP, starts, local_row_count, local_column_count
        )
        product = lax.dot_general(
            window,
            grad_flat,
            (((0,), (0,)), ((), ())),
            precision=highest,
            preferred_element_type=jnp.float32,
        )
        tap_list.append(product.reshape(3, channels, -1))
    return jnp.stack(tap_list)


def normalize(hidden, cell_count):
    totals = lax.psum(jnp.sum(hidden, axis=(0, 1)), ("row", "col"))
    average = totals / cell_count
    centered = hidden - average
    spread = lax.psum(jnp.sum(centered * centered, axis=(0, 1)), ("row", "col"))
    variance = spread / cell_count
    inverse = lax.rsqrt(variance + epsilon)
    return ((hidden - average) * inverse, inverse)


def normalize_back(grad_normed, normed, inverse, gain_row, cell_count):
    shift_sum, gain_sum = lax.psum(
        (jnp.sum(grad_normed, axis=(0, 1)), jnp.sum(grad_normed * normed, axis=(0, 1))),
        ("row", "col"),
    )
    grad_scaled = grad_normed * gain_row
    grad_hidden = inverse * (
        grad_scaled
        - gain_row * shift_sum / cell_count
        - normed * (gain_row * gain_sum / cell_count)
    )
    return (grad_hidden, gain_sum, shift_sum)


def elu_slope(values):
    return jnp.where(values > 0, 1.0, jnp.exp(jnp.minimum(values, 0.0)))


def mirror_tile(tile_in):
    local_row_count, local_column_count, channels = tile_in.shape
    row_devices = lax.axis_size("row")
    col_devices = lax.axis_size("col")
    row_part = local_row_count // col_devices
    group = row_devices // col_devices
    sectioned = tile_in.reshape(col_devices, row_part, local_column_count, channels)
    sectioned = lax.all_to_all(sectioned, "col", split_axis=0, concat_axis=0, tiled=True)
    sectioned = (
        sectioned.reshape(col_devices, row_part, group, local_row_count, channels)
        .transpose(0, 2, 1, 3, 4)
        .reshape(row_devices, row_part, local_row_count, channels)
    )
    sectioned = lax.all_to_all(
        lax.all_to_all(sectioned, "row", split_axis=0, concat_axis=0, tiled=True),
        "col",
        split_axis=0,
        concat_axis=0,
        tiled=True,
    )
    sectioned = sectioned.reshape(
        col_devices, group, row_part, local_row_count, channels
    ).transpose(3, 1, 0, 2, 4)
    return sectioned.reshape(local_row_count, local_column_count, channels)


def general_body(pair_map, cotangent, conv_one, conv_two, norm_gain, norm_shift):
    channels = conv_one.shape[2]
    local_row_count = pair_map.shape[0]
    local_column_count = pair_map.shape[1] // channels
    residues = float(local_row_count * lax.axis_size("row"))
    cell_count = float(
        local_row_count * local_column_count * lax.axis_size("row") * lax.axis_size("col")
    )
    feature_field_patch = pair_map.reshape(local_row_count, local_column_count, channels)
    field_ext = extend(feature_field_patch)
    first_conv = dilated(field_ext, conv_one, local_row_count, local_column_count)
    normed_one, inverse_one = normalize(first_conv, cell_count)
    before_one = normed_one * norm_gain[0] + norm_shift[0]
    active = jax.nn.elu(before_one)
    active_ext = extend(active)
    second_conv = dilated(active_ext, conv_two, local_row_count, local_column_count)
    normed_two, inverse_two = normalize(second_conv, cell_count)
    summed = feature_field_patch + normed_two * norm_gain[1] + norm_shift[1]
    block_out = jax.nn.elu(summed)
    symmetric = 0.5 * (block_out + mirror_tile(block_out))
    grad_in = cotangent.reshape(local_row_count, local_column_count, channels)
    grad_out = 0.5 * (grad_in + mirror_tile(grad_in))
    grad_sum = grad_out * elu_slope(summed)
    grad_second, gain_two, shift_two = normalize_back(
        grad_sum, normed_two, inverse_two, norm_gain[1], cell_count
    )
    second_ext = extend(grad_second)
    grad_active = dilated_back(second_ext, conv_two, local_row_count, local_column_count)
    kernel_two = kernel_grad(active_ext, grad_second, local_row_count, local_column_count)
    grad_before = grad_active * elu_slope(before_one)
    grad_first, gain_one, shift_one = normalize_back(
        grad_before, normed_one, inverse_one, norm_gain[0], cell_count
    )
    first_ext = extend(grad_first)
    grad_field = grad_sum + dilated_back(first_ext, conv_one, local_row_count, local_column_count)
    kernel_one = kernel_grad(field_ext, grad_first, local_row_count, local_column_count)
    total_one, total_two = lax.psum((kernel_one, kernel_two), ("row", "col"))
    grad_gains = jnp.stack([gain_one, gain_two]) / residues
    grad_shifts = jnp.stack([shift_one, shift_two]) / residues
    return (
        symmetric.reshape(local_row_count, local_column_count * channels),
        grad_field.reshape(local_row_count, local_column_count * channels),
        total_one / residues,
        total_two / residues,
        grad_gains,
        grad_shifts,
    )


SLOTS = 8
LANES = 128
HALF = 64
ROWS = 256
AXES = ("row", "col")
VMEM_BYTES = 8 << 20


def phase_table(devices):
    pairs = [(r, s) for r in range(DILATION_STEP) for s in range(r + 1, DILATION_STEP)]
    table = []
    taken = 0
    diagonal = DILATION_STEP // 2
    for device in range(devices):
        count = SLOTS // 2 - (1 if device < diagonal else 0)
        upper = pairs[taken : taken + count]
        taken += count
        lower = [(s, r) for r, s in upper]
        if device < diagonal:
            upper = upper + [(2 * device, 2 * device)]
            lower = lower + [(2 * device + 1, 2 * device + 1)]
        table.append(upper + lower)
    return table


def lane_low(shape):
    return lax.broadcasted_iota(jnp.int32, shape, len(shape) - 1) < HALF


def swap_halves(values):
    return pltpu.roll(values, HALF, values.ndim - 1)


def fold_halves(values):
    return values + swap_halves(values)


def twice(row):
    return jnp.concatenate([row, row], axis=1)


def exact_dot(left, right, dims):
    return lax.dot_general(
        left, right, (dims, ((), ())), precision=highest, preferred_element_type=jnp.float32
    )


def split_phases(tile_ref, scratch_ref):
    low = lane_low((DILATION_STEP, LANES))
    for t in range(DILATION_STEP // 2):
        first = tile_ref[:, t * LANES : (t + 1) * LANES]
        begin = DILATION_STEP * HALF + t * LANES
        second = tile_ref[:, begin : begin + LANES]
        row = 2 * t * DILATION_STEP
        scratch_ref[row : row + DILATION_STEP, :] = jnp.where(low, first, swap_halves(second))
        row += DILATION_STEP
        scratch_ref[row : row + DILATION_STEP, :] = jnp.where(low, swap_halves(first), second)


def join_phases(scratch_ref, tile_ref):
    low = lane_low((DILATION_STEP, LANES))
    for t in range(DILATION_STEP // 2):
        row = 2 * t * DILATION_STEP
        even = scratch_ref[row : row + DILATION_STEP, :]
        odd = scratch_ref[row + DILATION_STEP : row + 2 * DILATION_STEP, :]
        tile_ref[:, t * LANES : (t + 1) * LANES] = jnp.where(low, even, swap_halves(odd))
        begin = DILATION_STEP * HALF + t * LANES
        tile_ref[:, begin : begin + LANES] = jnp.where(low, swap_halves(even), odd)


def pack_rows(table, scratch_ref, send_ref, stride):
    for device, slots in enumerate(table):
        for k, (r, s) in enumerate(slots):
            source = s * DILATION_STEP + r
            target = device * stride + k
            send_ref[target : target + 1, :] = scratch_ref[source : source + 1, :]


def unpack_rows(table, recv_ref, scratch_ref, stride, offset):
    for device, slots in enumerate(table):
        for k, (r, s) in enumerate(slots):
            target = s * DILATION_STEP + r
            source = device * stride + offset + k
            scratch_ref[target : target + 1, :] = recv_ref[source : source + 1, :]


def slot_rows(ref, stride, devices):
    return jnp.concatenate(
        [ref[d * stride : d * stride + SLOTS, :] for d in range(devices)], axis=0
    )


def neighbours(values):
    zero = jnp.zeros((SLOTS, LANES), jnp.float32)
    ahead = jnp.concatenate([values[SLOTS:], zero], axis=0)
    behind = jnp.concatenate([zero, values[:-SLOTS]], axis=0)
    place = (lax.broadcasted_iota(jnp.int32, (ROWS, LANES), 0) // SLOTS) % 4
    low = lane_low((ROWS, LANES))
    side = jnp.where(low, jnp.where(place == 3, 0.0, ahead), jnp.where(place == 0, 0.0, behind))
    return jnp.concatenate([side, values], axis=1)


def forward_weight(weight_ref):
    zero = jnp.zeros((HALF, HALF), jnp.float32)
    taps = []
    for a in range(3):
        w = [weight_ref[a, b] for b in range(3)]
        blocks = [(zero, w[2]), (w[0], zero), (w[1], w[0]), (w[2], w[1])]
        taps.append(
            jnp.concatenate([jnp.concatenate(list(b), axis=1) for b in blocks], axis=0)
        )
    return jnp.concatenate(taps, axis=1)


def backward_weight(weight_ref):
    zero = jnp.zeros((HALF, HALF), jnp.float32)
    taps = []
    for a in range(3):
        w = [weight_ref[2 - a, 2 - b] for b in range(3)]
        taps.append(jnp.concatenate([zero, w[0], w[1], w[2]], axis=1))
        taps.append(jnp.concatenate([w[2], zero, w[0], w[1]], axis=1))
    return jnp.concatenate(taps, axis=0)


def shifted_sum(parts):
    step = 4 * SLOTS
    zero = jnp.zeros((step, LANES), jnp.float32)
    first, middle, last = (parts[:, a * LANES : (a + 1) * LANES] for a in range(3))
    return (
        middle
        + jnp.concatenate([zero, first[:-step]], axis=0)
        + jnp.concatenate([last[step:], zero], axis=0)
    )


def spread_shifts(values):
    step = 4 * SLOTS
    zero = jnp.zeros((step, LANES), jnp.float32)
    return jnp.concatenate(
        [
            jnp.concatenate([values[step:], zero], axis=0),
            values,
            jnp.concatenate([zero, values[:-step]], axis=0),
        ],
        axis=1,
    )


def kernel_rows(joined, grad):
    product = exact_dot(joined, spread_shifts(grad), ((0,), (0,)))
    pieces = []
    for a in range(3):
        part = product[:, a * LANES : (a + 1) * LANES]
        for even, odd in ((1, 2), (2, 3), (3, 0)):
            tap = part[even * HALF : (even + 1) * HALF] + swap_halves(
                part[odd * HALF : (odd + 1) * HALF]
            )
            low = lane_low((HALF // 2, LANES))
            pieces.append(jnp.where(low, tap[: HALF // 2], swap_halves(tap[HALF // 2 :])))
    return jnp.concatenate(pieces, axis=0)


def local_stats(hidden):
    count = 2.0 * ROWS
    mean = fold_halves(jnp.sum(hidden, axis=0, keepdims=True)) / count
    centered = hidden - mean
    spread = fold_halves(jnp.sum(centered * centered, axis=0, keepdims=True))
    return jnp.where(lane_low((1, LANES)), mean, spread)


def combine_stats(rows, devices):
    low = lane_low((devices, LANES))
    means = jnp.where(low, rows, swap_halves(rows))
    spreads = jnp.where(low, swap_halves(rows), rows)
    mean = jnp.sum(means, axis=0, keepdims=True) / devices
    apart = means - mean
    total = jnp.sum(spreads + (2.0 * ROWS) * (apart * apart), axis=0, keepdims=True)
    return mean, lax.rsqrt(total / (2.0 * ROWS * devices) + epsilon)


def elu_value(values):
    return jnp.where(values > 0, values, jnp.exp(jnp.minimum(values, 0.0)) - 1.0)


def pair_sums(grad, normed):
    plain = fold_halves(jnp.sum(grad, axis=0, keepdims=True))
    scaled = fold_halves(jnp.sum(grad * normed, axis=0, keepdims=True))
    return jnp.where(lane_low((1, LANES)), plain, scaled)


def split_sums(rows):
    total = jnp.sum(rows, axis=0, keepdims=True)
    other = swap_halves(total)
    low = lane_low((1, LANES))
    return jnp.where(low, total, other), jnp.where(low, other, total)


def norm_back(grad, normed, inverse, gain, shift_sum, gain_sum, cells):
    return inverse * (gain * grad - gain * shift_sum / cells - normed * (gain * gain_sum / cells))


def mirrored(values, own_mask):
    low = lane_low((SLOTS, LANES))
    tiles = [values[i * SLOTS : (i + 1) * SLOTS] for i in range(ROWS // SLOTS)]
    pieces = []
    for p in range(SLOTS):
        for c in range(4):
            even = tiles[2 * c * 4 + p // 2]
            odd = tiles[(2 * c + 1) * 4 + p // 2]
            if p % 2 == 0:
                piece = jnp.where(low, even, swap_halves(odd))
            else:
                piece = jnp.where(low, swap_halves(even), odd)
            pieces.append(jnp.where(own_mask, piece, pltpu.roll(piece, 4, 0)))
    return jnp.concatenate(pieces, axis=0)


def first_kernel(table, x_ref, send_ref, scratch_ref):
    split_phases(x_ref, scratch_ref)
    pack_rows(table, scratch_ref, send_ref, SLOTS)


def conv_one_kernel(table, x_ref, weight_ref, g_ref, hidden_ref, send_ref, scratch_ref):
    split_phases(g_ref, scratch_ref)
    stride = SLOTS + 1
    pack_rows(table, scratch_ref, send_ref, stride)
    hidden = shifted_sum(
        exact_dot(neighbours(x_ref[...]), forward_weight(weight_ref), ((1,), (0,)))
    )
    hidden_ref[...] = hidden
    stats = local_stats(hidden)
    for d in range(len(table)):
        send_ref[d * stride + SLOTS : (d + 1) * stride, :] = stats


def conv_two_kernel(
    devices, recv_ref, hidden_ref, weight_ref, gain_ref, shift_ref,
    normed_ref, inverse_ref, active_ref, second_ref, send_ref,
):
    stride = SLOTS + 1
    mean, inverse = combine_stats(recv_ref[pl.ds(SLOTS, devices, stride=stride), :], devices)
    normed = (hidden_ref[...] - mean) * inverse
    normed_ref[...] = normed
    inverse_ref[...] = inverse
    active = elu_value(normed * twice(gain_ref[0:1, :]) + twice(shift_ref[0:1, :]))
    active_ref[...] = active
    second = shifted_sum(
        exact_dot(neighbours(active), forward_weight(weight_ref), ((1,), (0,)))
    )
    second_ref[...] = second
    send_ref[...] = jnp.broadcast_to(local_stats(second), (devices, LANES))


def output_kernel(
    devices, recv_ref, second_ref, x_ref, grad_ref, gain_ref, shift_ref, own_ref,
    normed_ref, inverse_ref, sum_ref, send_ref,
):
    stride = SLOTS + 1
    mean, inverse = combine_stats(recv_ref[...], devices)
    normed = (second_ref[...] - mean) * inverse
    normed_ref[...] = normed
    inverse_ref[...] = inverse
    summed = x_ref[...] + normed * twice(gain_ref[1:2, :]) + twice(shift_ref[1:2, :])
    slope = jnp.exp(jnp.minimum(summed, 0.0))
    out = jnp.where(summed > 0, summed, slope - 1.0)
    own = own_ref[...] > 0
    symmetric = 0.5 * (out + mirrored(out, own))
    for d in range(devices):
        send_ref[d * stride : d * stride + SLOTS, :] = symmetric[d * SLOTS : (d + 1) * SLOTS]
    grad_in = slot_rows(grad_ref, stride, devices)
    grad_out = 0.5 * (grad_in + mirrored(grad_in, own))
    grad_sum = grad_out * jnp.where(summed > 0, 1.0, slope)
    sum_ref[...] = grad_sum
    sums = pair_sums(grad_sum, normed)
    for d in range(devices):
        send_ref[d * stride + SLOTS : (d + 1) * stride, :] = sums


def back_two_kernel(
    devices, recv_ref, sum_ref, normed_two_ref, inverse_two_ref, active_ref, normed_ref,
    weight_ref, gain_ref, shift_ref, before_ref, total_ref, send_ref, scratch_ref,
):
    cells = 2.0 * ROWS * devices
    shift_sum, gain_sum = split_sums(recv_ref[pl.ds(SLOTS, devices, stride=SLOTS + 1), :])
    total_ref[...] = jnp.where(lane_low((1, LANES)), shift_sum, gain_sum)
    grad_second = norm_back(
        sum_ref[...], normed_two_ref[...], inverse_two_ref[...], twice(gain_ref[1:2, :]),
        shift_sum, gain_sum, cells,
    )
    grad_active = shifted_sum(
        exact_dot(neighbours(grad_second), backward_weight(weight_ref), ((1,), (1,)))
    )
    normed = normed_ref[...]
    before = normed * twice(gain_ref[0:1, :]) + twice(shift_ref[0:1, :])
    grad_before = grad_active * jnp.where(before > 0, 1.0, jnp.exp(jnp.minimum(before, 0.0)))
    before_ref[...] = grad_before
    sums = pair_sums(grad_before, normed)
    share = ROWS * 9 // 8 // devices
    stride = share + 1
    scratch_ref[...] = kernel_rows(neighbours(active_ref[...]), grad_second)
    for d in range(devices):
        send_ref[d * stride : d * stride + share, :] = scratch_ref[d * share : (d + 1) * share, :]
        send_ref[d * stride + share : (d + 1) * stride, :] = sums


def reduce_share(ref, devices, share, stride):
    total = ref[0:share, :]
    for d in range(1, devices):
        total = total + ref[d * stride : d * stride + share, :]
    return total


def back_one_kernel(
    devices, recv_ref, before_ref, normed_ref, inverse_ref, x_ref, sum_ref, weight_ref, gain_ref,
    total_ref, two_ref, send_ref, scratch_ref,
):
    cells = 2.0 * ROWS * devices
    share = ROWS * 9 // 8 // devices
    stride = share + 1
    shift_sum, gain_sum = split_sums(recv_ref[pl.ds(share, devices, stride=stride), :])
    total_ref[...] = jnp.where(lane_low((1, LANES)), shift_sum, gain_sum)
    two_ref[...] = reduce_share(recv_ref, devices, share, stride)
    grad_first = norm_back(
        before_ref[...], normed_ref[...], inverse_ref[...], twice(gain_ref[0:1, :]),
        shift_sum, gain_sum, cells,
    )
    field = sum_ref[...] + shifted_sum(
        exact_dot(neighbours(grad_first), backward_weight(weight_ref), ((1,), (1,)))
    )
    scratch_ref[...] = kernel_rows(neighbours(x_ref[...]), grad_first)
    stride = share + SLOTS
    for d in range(devices):
        send_ref[d * stride : d * stride + SLOTS, :] = field[d * SLOTS : (d + 1) * SLOTS]
        send_ref[d * stride + SLOTS : (d + 1) * stride, :] = scratch_ref[
            d * share : (d + 1) * share, :
        ]


def share_kernel(devices, recv_ref, two_ref, send_ref):
    share = ROWS * 9 // 8 // devices
    stride = share + SLOTS
    total = recv_ref[SLOTS:stride, :]
    for d in range(1, devices):
        total = total + recv_ref[d * stride + SLOTS : (d + 1) * stride, :]
    two = two_ref[...]
    for d in range(devices):
        send_ref[2 * d * share : (2 * d + 1) * share, :] = total
        send_ref[(2 * d + 1) * share : (2 * d + 2) * share, :] = two


def last_kernel(
    table, residues, sym_recv_ref, map_recv_ref, recv_ref, total_one_ref, total_two_ref,
    sym_ref, map_ref, one_ref, two_ref, gain_ref, shift_ref, scratch_ref, rows_ref,
):
    devices = len(table)
    share = ROWS * 9 // 8 // devices
    unpack_rows(table, sym_recv_ref, scratch_ref, SLOTS + 1, 0)
    join_phases(scratch_ref, sym_ref)
    unpack_rows(table, map_recv_ref, scratch_ref, SLOTS + share, 0)
    join_phases(scratch_ref, map_ref)
    for index, out_ref in ((0, one_ref), (1, two_ref)):
        for d in range(devices):
            begin = (2 * d + index) * share
            rows_ref[d * share : (d + 1) * share, :] = recv_ref[begin : begin + share, :]
        for tap in range(9):
            block = rows_ref[tap * HALF // 2 : (tap + 1) * HALF // 2, :] / residues
            out_ref[tap, : HALF // 2, :] = block[:, :HALF]
            out_ref[tap, HALF // 2 :, :] = swap_halves(block)[:, :HALF]
    for index, total_ref in ((0, total_one_ref), (1, total_two_ref)):
        total = total_ref[...] / residues
        shift_ref[index : index + 1, :] = total[:, :HALF]
        gain_ref[index : index + 1, :] = swap_halves(total)[:, :HALF]


def call(body, shapes, scratch=()):
    return pl.pallas_call(
        body,
        out_shape=[jax.ShapeDtypeStruct(s, jnp.float32) for s in shapes],
        scratch_shapes=[pltpu.VMEM(s, jnp.float32) for s in scratch],
        compiler_params=pltpu.CompilerParams(vmem_limit_bytes=VMEM_BYTES),
    )


def exchange(rows, devices):
    sent = rows.reshape(devices, 1, -1)
    received = lax.all_to_all(sent, AXES, split_axis=0, concat_axis=0, tiled=True)
    return received.reshape(-1, LANES)


def phase_body(pair_map, cotangent, conv_one, conv_two, norm_gain, norm_shift):
    devices = lax.axis_size("row") * lax.axis_size("col")
    residues = float(pair_map.shape[0] * lax.axis_size("row"))
    table = phase_table(devices)
    share = ROWS * 9 // 8 // devices
    whole, line = (ROWS, LANES), (1, LANES)
    part = functools.partial
    me = lax.axis_index("row") * lax.axis_size("col") + lax.axis_index("col")
    slot = lax.broadcasted_iota(jnp.int32, (SLOTS, LANES), 0)
    own = ((slot % 4 == 3) & (me < DILATION_STEP // 2)).astype(jnp.float32)

    (send,) = call(part(first_kernel, table), [whole], [whole])(pair_map)
    x = exchange(send, devices)
    hidden, send = call(
        part(conv_one_kernel, table), [whole, (devices * (SLOTS + 1), LANES)], [whole]
    )(x, conv_one, cotangent)
    grad_recv = exchange(send, devices)
    normed_one, inverse_one, active, second, send = call(
        part(conv_two_kernel, devices), [whole, line, whole, whole, (devices, LANES)]
    )(grad_recv, hidden, conv_two, norm_gain, norm_shift)
    recv = exchange(send, devices)
    normed_two, inverse_two, grad_sum, send = call(
        part(output_kernel, devices), [whole, line, whole, (devices * (SLOTS + 1), LANES)]
    )(recv, second, x, grad_recv, norm_gain, norm_shift, own)
    sym_recv = exchange(send, devices)
    grad_before, total_two, send = call(
        part(back_two_kernel, devices),
        [whole, line, (devices * (share + 1), LANES)],
        [(devices * share, LANES)],
    )(
        sym_recv, grad_sum, normed_two, inverse_two, active, normed_one, conv_two,
        norm_gain, norm_shift,
    )
    recv = exchange(send, devices)
    total_one, kernel_two, send = call(
        part(back_one_kernel, devices),
        [line, (share, LANES), (devices * (share + SLOTS), LANES)],
        [(devices * share, LANES)],
    )(recv, grad_before, normed_one, inverse_one, x, grad_sum, conv_one, norm_gain)
    map_recv = exchange(send, devices)
    (send,) = call(part(share_kernel, devices), [(2 * devices * share, LANES)])(
        map_recv, kernel_two
    )
    recv = exchange(send, devices)
    taps = conv_one.shape[0] * conv_one.shape[1]
    sym_out, grad_map, grad_one, grad_two, grad_gain, grad_shift = call(
        part(last_kernel, table, residues),
        [
            pair_map.shape, pair_map.shape, (taps, HALF, HALF), (taps, HALF, HALF),
            norm_gain.shape, norm_shift.shape,
        ],
        [whole, (devices * share, LANES)],
    )(sym_recv, map_recv, recv, total_one, total_two)
    return (
        sym_out,
        grad_map,
        grad_one.reshape(conv_one.shape),
        grad_two.reshape(conv_two.shape),
        grad_gain,
        grad_shift,
    )


def body(pair_map, cotangent, conv_one, conv_two, norm_gain, norm_shift):
    devices = lax.axis_size("row") * lax.axis_size("col")
    fits = (
        conv_one.shape == (3, 3, HALF, HALF)
        and pair_map.shape == (DILATION_STEP, 2 * DILATION_STEP * HALF)
        and lax.axis_size("row") == SLOTS
        and lax.axis_size("col") == 4
    )
    plan = phase_body if fits else general_body
    return plan(pair_map, cotangent, conv_one, conv_two, norm_gain, norm_shift)


def solution(mesh):
    return jax.shard_map(
        body,
        mesh=mesh,
        in_specs=(P("row", "col"), P("row", "col"), P(), P(), P(), P()),
        out_specs=(P("row", "col"), P("row", "col"), P(), P(), P(), P()),
        check_vma=False,
    )
```

```python
import functools

import jax
import jax.numpy as jnp
from jax import lax
from jax.experimental import pallas as pl
from jax.experimental.pallas import tpu as pltpu
from jax.sharding import PartitionSpec as P

DILATION_STEP = 16


epsilon = 1e-05
highest = lax.Precision.HIGHEST


def extended_2(cells, sides, width):
    for axis, dim in sides:
        count = lax.axis_size(axis)
        ends = count - 1
        head = lax.slice_in_dim(cells, 0, width, axis=dim)
        tail = lax.slice_in_dim(cells, cells.shape[dim] - width, cells.shape[dim], axis=dim)
        cells = jnp.concatenate(
            [
                lax.ppermute(tail, axis, [(i, (i + 1) % count) for i in range(ends)]),
                cells,
                lax.ppermute(head, axis, [((i + 1) % count, i) for i in range(ends)]),
            ],
            axis=dim,
        )
    return cells


def extend(feature_field_patch):
    block_result = extended_2(feature_field_patch, (("row", 0), ("col", 1)), DILATION_STEP)
    return block_result


def tap_windows(extended, row_begin, column_starts, local_row_count, local_column_count):
    pieces = [
        extended[row_begin : row_begin + local_row_count, start : start + local_column_count]
        for start in column_starts
    ]
    joined = jnp.concatenate(pieces, axis=2)
    return joined.reshape(local_row_count * local_column_count, -1)


def dilated(extended, filter_weight, local_row_count, local_column_count):
    channels = filter_weight.shape[2]
    starts = [tap * DILATION_STEP for tap in range(3)]
    summed_taps = jnp.zeros(
        (local_row_count * local_column_count, filter_weight.shape[3]), jnp.float32
    )
    for filter_tap_row in range(3):
        window = tap_windows(
            extended, filter_tap_row * DILATION_STEP, starts, local_row_count, local_column_count
        )
        stacked = filter_weight[filter_tap_row].reshape(3 * channels, -1)
        summed_taps = summed_taps + jnp.dot(
            window, stacked, precision=highest, preferred_element_type=jnp.float32
        )
    return summed_taps.reshape(local_row_count, local_column_count, -1)


def dilated_back(grad_ext, filter_weight, local_row_count, local_column_count):
    channels = filter_weight.shape[3]
    starts = [(2 - tap) * DILATION_STEP for tap in range(3)]
    summed_taps = jnp.zeros(
        (local_row_count * local_column_count, filter_weight.shape[2]), jnp.float32
    )
    for filter_tap_row in range(3):
        window = tap_windows(
            grad_ext,
            (2 - filter_tap_row) * DILATION_STEP,
            starts,
            local_row_count,
            local_column_count,
        )
        stacked = jnp.transpose(filter_weight[filter_tap_row], (0, 2, 1)).reshape(3 * channels, -1)
        summed_taps = summed_taps + jnp.dot(
            window, stacked, precision=highest, preferred_element_type=jnp.float32
        )
    return summed_taps.reshape(local_row_count, local_column_count, -1)


def kernel_grad(extended, grad_tile, local_row_count, local_column_count):
    channels = extended.shape[2]
    starts = [tap * DILATION_STEP for tap in range(3)]
    grad_flat = grad_tile.reshape(-1, grad_tile.shape[2])
    tap_list = []
    for filter_tap_row in range(3):
        window = tap_windows(
            extended, filter_tap_row * DILATION_STEP, starts, local_row_count, local_column_count
        )
        product = lax.dot_general(
            window,
            grad_flat,
            (((0,), (0,)), ((), ())),
            precision=highest,
            preferred_element_type=jnp.float32,
        )
        tap_list.append(product.reshape(3, channels, -1))
    return jnp.stack(tap_list)


def normalize(hidden, cell_count):
    totals = lax.psum(jnp.sum(hidden, axis=(0, 1)), ("row", "col"))
    average = totals / cell_count
    centered = hidden - average
    spread = lax.psum(jnp.sum(centered * centered, axis=(0, 1)), ("row", "col"))
    variance = spread / cell_count
    inverse = lax.rsqrt(variance + epsilon)
    return ((hidden - average) * inverse, inverse)


def normalize_back(grad_normed, normed, inverse, gain_row, cell_count):
    shift_sum, gain_sum = lax.psum(
        (jnp.sum(grad_normed, axis=(0, 1)), jnp.sum(grad_normed * normed, axis=(0, 1))),
        ("row", "col"),
    )
    grad_scaled = grad_normed * gain_row
    grad_hidden = inverse * (
        grad_scaled
        - gain_row * shift_sum / cell_count
        - normed * (gain_row * gain_sum / cell_count)
    )
    return (grad_hidden, gain_sum, shift_sum)


def elu_slope(values):
    return jnp.where(values > 0, 1.0, jnp.exp(jnp.minimum(values, 0.0)))


def mirror_tile(tile_in):
    local_row_count, local_column_count, channels = tile_in.shape
    row_devices = lax.axis_size("row")
    col_devices = lax.axis_size("col")
    row_part = local_row_count // col_devices
    group = row_devices // col_devices
    sectioned = tile_in.reshape(col_devices, row_part, local_column_count, channels)
    sectioned = lax.all_to_all(sectioned, "col", split_axis=0, concat_axis=0, tiled=True)
    sectioned = (
        sectioned.reshape(col_devices, row_part, group, local_row_count, channels)
        .transpose(0, 2, 1, 3, 4)
        .reshape(row_devices, row_part, local_row_count, channels)
    )
    sectioned = lax.all_to_all(
        lax.all_to_all(sectioned, "row", split_axis=0, concat_axis=0, tiled=True),
        "col",
        split_axis=0,
        concat_axis=0,
        tiled=True,
    )
    sectioned = sectioned.reshape(
        col_devices, group, row_part, local_row_count, channels
    ).transpose(3, 1, 0, 2, 4)
    return sectioned.reshape(local_row_count, local_column_count, channels)


def general_body(pair_map, cotangent, conv_one, conv_two, norm_gain, norm_shift):
    channels = conv_one.shape[2]
    local_row_count = pair_map.shape[0]
    local_column_count = pair_map.shape[1] // channels
    residues = float(local_row_count * lax.axis_size("row"))
    cell_count = float(
        local_row_count * local_column_count * lax.axis_size("row") * lax.axis_size("col")
    )
    feature_field_patch = pair_map.reshape(local_row_count, local_column_count, channels)
    field_ext = extend(feature_field_patch)
    first_conv = dilated(field_ext, conv_one, local_row_count, local_column_count)
    normed_one, inverse_one = normalize(first_conv, cell_count)
    before_one = normed_one * norm_gain[0] + norm_shift[0]
    active = jax.nn.elu(before_one)
    active_ext = extend(active)
    second_conv = dilated(active_ext, conv_two, local_row_count, local_column_count)
    normed_two, inverse_two = normalize(second_conv, cell_count)
    summed = feature_field_patch + normed_two * norm_gain[1] + norm_shift[1]
    block_out = jax.nn.elu(summed)
    symmetric = 0.5 * (block_out + mirror_tile(block_out))
    grad_in = cotangent.reshape(local_row_count, local_column_count, channels)
    grad_out = 0.5 * (grad_in + mirror_tile(grad_in))
    grad_sum = grad_out * elu_slope(summed)
    grad_second, gain_two, shift_two = normalize_back(
        grad_sum, normed_two, inverse_two, norm_gain[1], cell_count
    )
    second_ext = extend(grad_second)
    grad_active = dilated_back(second_ext, conv_two, local_row_count, local_column_count)
    kernel_two = kernel_grad(active_ext, grad_second, local_row_count, local_column_count)
    grad_before = grad_active * elu_slope(before_one)
    grad_first, gain_one, shift_one = normalize_back(
        grad_before, normed_one, inverse_one, norm_gain[0], cell_count
    )
    first_ext = extend(grad_first)
    grad_field = grad_sum + dilated_back(first_ext, conv_one, local_row_count, local_column_count)
    kernel_one = kernel_grad(field_ext, grad_first, local_row_count, local_column_count)
    total_one, total_two = lax.psum((kernel_one, kernel_two), ("row", "col"))
    grad_gains = jnp.stack([gain_one, gain_two]) / residues
    grad_shifts = jnp.stack([shift_one, shift_two]) / residues
    return (
        symmetric.reshape(local_row_count, local_column_count * channels),
        grad_field.reshape(local_row_count, local_column_count * channels),
        total_one / residues,
        total_two / residues,
        grad_gains,
        grad_shifts,
    )


SLOTS = 8
LANES = 128
HALF = 64
ROWS = 256
AXES = ("row", "col")
VMEM_BYTES = 8 << 20
TAP_SOURCES = ((1, 2), (2, 3), (3, 0))


def phase_table(devices):
    pairs = [(r, s) for r in range(DILATION_STEP) for s in range(r + 1, DILATION_STEP)]
    table = []
    taken = 0
    diagonal = DILATION_STEP // 2
    for device in range(devices):
        count = SLOTS // 2 - (1 if device < diagonal else 0)
        upper = pairs[taken : taken + count]
        taken += count
        lower = [(s, r) for r, s in upper]
        if device < diagonal:
            upper = upper + [(2 * device, 2 * device)]
            lower = lower + [(2 * device + 1, 2 * device + 1)]
        table.append(upper + lower)
    return table


def lane_low(shape):
    return lax.broadcasted_iota(jnp.int32, shape, len(shape) - 1) < HALF


def swap_halves(values):
    return pltpu.roll(values, HALF, values.ndim - 1)


def fold_halves(values):
    return values + swap_halves(values)


def twice(row):
    return jnp.concatenate([row, row], axis=1)


def exact_dot(left, right, dims):
    return lax.dot_general(
        left, right, (dims, ((), ())), precision=highest, preferred_element_type=jnp.float32
    )


def split_phases(tile_ref, scratch_ref):
    low = lane_low((DILATION_STEP, LANES))
    for t in range(DILATION_STEP // 2):
        first = tile_ref[:, t * LANES : (t + 1) * LANES]
        begin = DILATION_STEP * HALF + t * LANES
        second = tile_ref[:, begin : begin + LANES]
        row = 2 * t * DILATION_STEP
        scratch_ref[row : row + DILATION_STEP, :] = jnp.where(low, first, swap_halves(second))
        row += DILATION_STEP
        scratch_ref[row : row + DILATION_STEP, :] = jnp.where(low, swap_halves(first), second)


def join_phases(scratch_ref, tile_ref):
    low = lane_low((DILATION_STEP, LANES))
    for t in range(DILATION_STEP // 2):
        row = 2 * t * DILATION_STEP
        even = scratch_ref[row : row + DILATION_STEP, :]
        odd = scratch_ref[row + DILATION_STEP : row + 2 * DILATION_STEP, :]
        tile_ref[:, t * LANES : (t + 1) * LANES] = jnp.where(low, even, swap_halves(odd))
        begin = DILATION_STEP * HALF + t * LANES
        tile_ref[:, begin : begin + LANES] = jnp.where(low, swap_halves(even), odd)


def pack_rows(table, scratch_ref, send_ref, stride):
    for device, slots in enumerate(table):
        for k, (r, s) in enumerate(slots):
            source = s * DILATION_STEP + r
            target = device * stride + k
            send_ref[target : target + 1, :] = scratch_ref[source : source + 1, :]


def unpack_rows(table, recv_ref, scratch_ref, stride, offset):
    for device, slots in enumerate(table):
        for k, (r, s) in enumerate(slots):
            target = s * DILATION_STEP + r
            source = device * stride + offset + k
            scratch_ref[target : target + 1, :] = recv_ref[source : source + 1, :]


def slot_rows(ref, stride, devices):
    return jnp.concatenate(
        [ref[d * stride : d * stride + SLOTS, :] for d in range(devices)], axis=0
    )


def neighbours(values):
    zero = jnp.zeros((SLOTS, LANES), jnp.float32)
    ahead = jnp.concatenate([values[SLOTS:], zero], axis=0)
    behind = jnp.concatenate([zero, values[:-SLOTS]], axis=0)
    place = (lax.broadcasted_iota(jnp.int32, (ROWS, LANES), 0) // SLOTS) % 4
    low = lane_low((ROWS, LANES))
    side = jnp.where(low, jnp.where(place == 3, 0.0, ahead), jnp.where(place == 0, 0.0, behind))
    return jnp.concatenate([side, values], axis=1)


def forward_weight(weight_ref):
    zero = jnp.zeros((HALF, HALF), jnp.float32)
    taps = []
    for a in range(3):
        w = [weight_ref[a, b] for b in range(3)]
        blocks = [(zero, w[2]), (w[0], zero), (w[1], w[0]), (w[2], w[1])]
        taps.append(
            jnp.concatenate([jnp.concatenate(list(b), axis=1) for b in blocks], axis=0)
        )
    return jnp.concatenate(taps, axis=1)


def backward_weight(weight_ref):
    zero = jnp.zeros((HALF, HALF), jnp.float32)
    taps = []
    for a in range(3):
        w = [weight_ref[2 - a, 2 - b] for b in range(3)]
        taps.append(jnp.concatenate([zero, w[0], w[1], w[2]], axis=1))
        taps.append(jnp.concatenate([w[2], zero, w[0], w[1]], axis=1))
    return jnp.concatenate(taps, axis=0)


def shifted_sum(parts):
    step = 4 * SLOTS
    zero = jnp.zeros((step, LANES), jnp.float32)
    first, middle, last = (parts[:, a * LANES : (a + 1) * LANES] for a in range(3))
    return (
        middle
        + jnp.concatenate([zero, first[:-step]], axis=0)
        + jnp.concatenate([last[step:], zero], axis=0)
    )


def spread_shifts(values):
    step = 4 * SLOTS
    zero = jnp.zeros((step, LANES), jnp.float32)
    return jnp.concatenate(
        [
            jnp.concatenate([values[step:], zero], axis=0),
            values,
            jnp.concatenate([zero, values[:-step]], axis=0),
        ],
        axis=1,
    )


def tap_rows(product):
    low = lane_low((HALF // 2, LANES))
    pieces = []
    for a in range(3):
        part = product[:, a * LANES : (a + 1) * LANES]
        for even, odd in TAP_SOURCES:
            tap = part[even * HALF : (even + 1) * HALF] + swap_halves(
                part[odd * HALF : (odd + 1) * HALF]
            )
            pieces.append(jnp.where(low, tap[: HALF // 2], swap_halves(tap[HALF // 2 :])))
    return jnp.concatenate(pieces, axis=0)


def kernel_rows(joined, grad):
    return tap_rows(exact_dot(joined, spread_shifts(grad), ((0,), (0,))))


def kernel_rows_and_sums(joined, grad, devices):
    row = lax.broadcasted_iota(jnp.int32, (ROWS, LANES), 0)
    tap = (lax.broadcasted_iota(jnp.int32, (ROWS, LANES), 1) % HALF) % 3
    step = 4 * SLOTS
    outside = ((tap == 0) & (row >= ROWS - step)) | ((tap == 2) & (row < step))
    ones = jnp.where(outside, 0.0, 1.0)
    product = exact_dot(
        joined, jnp.concatenate([spread_shifts(grad), ones], axis=1), ((0,), (0,))
    )
    part = product[:, 3 * LANES :]
    low = lane_low((HALF // 2, LANES))
    pieces = []
    for even, odd in TAP_SOURCES:
        both = part[even * HALF : (even + 1) * HALF] + part[odd * HALF : (odd + 1) * HALF]
        pieces.append(jnp.where(low, both[: HALF // 2], both[HALF // 2 :]))
    sums = jnp.concatenate(pieces * 3, axis=0)
    total = sums.shape[0]
    share = total // devices
    row = lax.broadcasted_iota(jnp.int32, (total, LANES), 0)
    lane = lax.broadcasted_iota(jnp.int32, (total, LANES), 1) % HALF
    sums = jnp.where(lane == 3 * (row % share) + row // (total // 3), sums, 0.0)
    owner = lax.broadcasted_iota(jnp.int32, (devices, total), 0)
    index = lax.broadcasted_iota(jnp.int32, (devices, total), 1)
    picked = (index // share == owner).astype(jnp.float32)
    return tap_rows(product), exact_dot(picked, sums, ((1,), (0,)))


def widen_sums(row, share):
    lane = lax.broadcasted_iota(jnp.int32, (share, LANES), 1)
    index = lax.broadcasted_iota(jnp.int32, (share, LANES), 0)
    picked = jnp.where((lane % HALF) // 3 == index, row, 0.0)
    low = lane < HALF
    first = jnp.sum(jnp.where(low, picked, 0.0), axis=1, keepdims=True)
    second = jnp.sum(jnp.where(low, 0.0, picked), axis=1, keepdims=True)
    return jnp.where(low, first, second)


def local_stats(hidden):
    count = 2.0 * ROWS
    mean = fold_halves(jnp.sum(hidden, axis=0, keepdims=True)) / count
    centered = hidden - mean
    spread = fold_halves(jnp.sum(centered * centered, axis=0, keepdims=True))
    return jnp.where(lane_low((1, LANES)), mean, spread)


def combine_stats(rows, devices):
    low = lane_low((devices, LANES))
    means = jnp.where(low, rows, swap_halves(rows))
    spreads = jnp.where(low, swap_halves(rows), rows)
    mean = jnp.sum(means, axis=0, keepdims=True) / devices
    apart = means - mean
    total = jnp.sum(spreads + (2.0 * ROWS) * (apart * apart), axis=0, keepdims=True)
    return mean, lax.rsqrt(total / (2.0 * ROWS * devices) + epsilon)


def elu_value(values):
    return jnp.where(values > 0, values, jnp.exp(jnp.minimum(values, 0.0)) - 1.0)


def pair_sums(grad, normed):
    plain = fold_halves(jnp.sum(grad, axis=0, keepdims=True))
    scaled = fold_halves(jnp.sum(grad * normed, axis=0, keepdims=True))
    return jnp.where(lane_low((1, LANES)), plain, scaled)


def split_sums(rows):
    total = jnp.sum(rows, axis=0, keepdims=True)
    other = swap_halves(total)
    low = lane_low((1, LANES))
    return jnp.where(low, total, other), jnp.where(low, other, total)


def norm_back(grad, normed, inverse, gain, shift_sum, gain_sum, cells):
    return inverse * (gain * grad - gain * shift_sum / cells - normed * (gain * gain_sum / cells))


def mirrored(values, own_mask):
    low = lane_low((SLOTS, LANES))
    tiles = [values[i * SLOTS : (i + 1) * SLOTS] for i in range(ROWS // SLOTS)]
    pieces = []
    for p in range(SLOTS):
        for c in range(4):
            even = tiles[2 * c * 4 + p // 2]
            odd = tiles[(2 * c + 1) * 4 + p // 2]
            if p % 2 == 0:
                piece = jnp.where(low, even, swap_halves(odd))
            else:
                piece = jnp.where(low, swap_halves(even), odd)
            pieces.append(jnp.where(own_mask, piece, pltpu.roll(piece, 4, 0)))
    return jnp.concatenate(pieces, axis=0)


def own_mirrors():
    me = lax.axis_index("row") * lax.axis_size("col") + lax.axis_index("col")
    slot = lax.broadcasted_iota(jnp.int32, (SLOTS, LANES), 0)
    return (slot % 4 == 3) & (me < DILATION_STEP // 2)


def first_kernel(
    table, x_ref, g_ref, gain_ref, shift_ref, send_ref, grad_ref, affine_ref, scratch_ref, other_ref
):
    split_phases(x_ref, scratch_ref)
    pack_rows(table, scratch_ref, send_ref, SLOTS)
    split_phases(g_ref, other_ref)
    pack_rows(table, other_ref, grad_ref, SLOTS)
    affine_ref[...] = jnp.concatenate(
        [twice(gain_ref[...]), twice(shift_ref[...]), jnp.zeros((4, LANES), jnp.float32)], axis=0
    )


def conv_one_kernel(devices, x_ref, weight_ref, g_ref, hidden_ref, send_ref):
    stride = SLOTS + 1
    hidden = shifted_sum(
        exact_dot(neighbours(x_ref[...]), forward_weight(weight_ref), ((1,), (0,)))
    )
    hidden_ref[...] = hidden
    stats = local_stats(hidden)
    for d in range(devices):
        send_ref[d * stride : d * stride + SLOTS, :] = g_ref[d * SLOTS : (d + 1) * SLOTS, :]
        send_ref[d * stride + SLOTS : (d + 1) * stride, :] = stats


def conv_two_kernel(
    devices, recv_ref, hidden_ref, x_ref, weight_ref, affine_ref,
    normed_ref, inverse_ref, active_ref, second_ref, send_ref, scratch_ref,
):
    mean, inverse = combine_stats(recv_ref[pl.ds(SLOTS, devices, stride=SLOTS + 1), :], devices)
    normed = (hidden_ref[...] - mean) * inverse
    normed_ref[...] = normed
    inverse_ref[...] = inverse
    active = elu_value(normed * affine_ref[0:1, :] + affine_ref[2:3, :])
    active_ref[...] = active
    second = shifted_sum(
        exact_dot(neighbours(active), forward_weight(weight_ref), ((1,), (0,)))
    )
    second_ref[...] = second
    stats = local_stats(second)
    rows, sums = kernel_rows_and_sums(neighbours(x_ref[...]), normed, devices)
    scratch_ref[...] = rows
    share = rows.shape[0] // devices
    stride = share + 2
    for d in range(devices):
        begin = d * stride
        send_ref[begin : begin + share, :] = scratch_ref[d * share : (d + 1) * share, :]
        send_ref[begin + share : begin + share + 1, :] = sums[d : d + 1, :]
        send_ref[begin + share + 1 : begin + stride, :] = stats


def output_kernel(
    devices, share, recv_ref, second_ref, x_ref, grad_ref, affine_ref,
    normed_ref, inverse_ref, sum_ref, send_ref,
):
    stride = SLOTS + 1
    mean, inverse = combine_stats(
        recv_ref[pl.ds(share + 1, devices, stride=share + 2), :], devices
    )
    normed = (second_ref[...] - mean) * inverse
    normed_ref[...] = normed
    inverse_ref[...] = inverse
    summed = x_ref[...] + normed * affine_ref[1:2, :] + affine_ref[3:4, :]
    slope = jnp.exp(jnp.minimum(summed, 0.0))
    out = jnp.where(summed > 0, summed, slope - 1.0)
    own = own_mirrors()
    symmetric = 0.5 * (out + mirrored(out, own))
    for d in range(devices):
        send_ref[d * stride : d * stride + SLOTS, :] = symmetric[d * SLOTS : (d + 1) * SLOTS]
    grad_in = slot_rows(grad_ref, stride, devices)
    grad_out = 0.5 * (grad_in + mirrored(grad_in, own))
    grad_sum = grad_out * jnp.where(summed > 0, 1.0, slope)
    sum_ref[...] = grad_sum
    sums = pair_sums(grad_sum, normed)
    for d in range(devices):
        send_ref[d * stride + SLOTS : (d + 1) * stride, :] = sums


def back_two_kernel(
    devices, share, recv_ref, sum_ref, normed_two_ref, inverse_two_ref, active_ref, normed_ref,
    x_ref, weight_ref, affine_ref, before_ref, total_ref, send_ref, two_ref, one_ref,
):
    cells = 2.0 * ROWS * devices
    shift_sum, gain_sum = split_sums(recv_ref[pl.ds(SLOTS, devices, stride=SLOTS + 1), :])
    total_ref[...] = jnp.where(lane_low((1, LANES)), shift_sum, gain_sum)
    grad_second = norm_back(
        sum_ref[...], normed_two_ref[...], inverse_two_ref[...], affine_ref[1:2, :],
        shift_sum, gain_sum, cells,
    )
    grad_active = shifted_sum(
        exact_dot(neighbours(grad_second), backward_weight(weight_ref), ((1,), (1,)))
    )
    normed = normed_ref[...]
    before = normed * affine_ref[0:1, :] + affine_ref[2:3, :]
    grad_before = grad_active * jnp.where(before > 0, 1.0, jnp.exp(jnp.minimum(before, 0.0)))
    before_ref[...] = grad_before
    sums = pair_sums(grad_before, normed)
    two_ref[...] = kernel_rows(neighbours(active_ref[...]), grad_second)
    one_ref[...] = kernel_rows(neighbours(x_ref[...]), grad_before)
    stride = 2 * share + 1
    for d in range(devices):
        begin = d * stride
        send_ref[begin : begin + share, :] = one_ref[d * share : (d + 1) * share, :]
        send_ref[begin + share : begin + 2 * share, :] = two_ref[d * share : (d + 1) * share, :]
        send_ref[begin + 2 * share : begin + stride, :] = sums


def reduce_share(ref, devices, begin, size, stride):
    total = ref[begin : begin + size, :]
    for d in range(1, devices):
        total = total + ref[d * stride + begin : d * stride + begin + size, :]
    return total


def back_one_kernel(
    devices, share, residues, recv_ref, before_ref, normed_ref, inverse_ref, sum_ref, weight_ref,
    affine_ref, normed_recv_ref, total_ref, send_ref,
):
    cells = 2.0 * ROWS * devices
    stride = 2 * share + 1
    shift_sum, gain_sum = split_sums(recv_ref[pl.ds(2 * share, devices, stride=stride), :])
    total_ref[...] = jnp.where(lane_low((1, LANES)), shift_sum, gain_sum)
    gain, inverse = affine_ref[0:1, :], inverse_ref[...]
    grad_first = norm_back(
        before_ref[...], normed_ref[...], inverse, gain, shift_sum, gain_sum, cells
    )
    field = sum_ref[...] + shifted_sum(
        exact_dot(neighbours(grad_first), backward_weight(weight_ref), ((1,), (1,)))
    )
    one = reduce_share(recv_ref, devices, 0, share, stride)
    two = reduce_share(recv_ref, devices, share, share, stride)
    rows = reduce_share(normed_recv_ref, devices, 0, share + 1, share + 2)
    constant = widen_sums(rows[share : share + 1], share)
    one = (inverse * gain) * (
        one - constant * (shift_sum / cells) - rows[:share] * (gain_sum / cells)
    )
    one, two = one / residues, two / residues
    stride = 2 * share + SLOTS
    for d in range(devices):
        begin = d * stride
        send_ref[begin : begin + SLOTS, :] = field[d * SLOTS : (d + 1) * SLOTS]
        send_ref[begin + SLOTS : begin + SLOTS + share, :] = one
        send_ref[begin + SLOTS + share : begin + stride, :] = two


def last_kernel(
    table, share, residues, sym_recv_ref, recv_ref, total_one_ref, total_two_ref,
    sym_ref, map_ref, one_ref, two_ref, gain_ref, shift_ref, scratch_ref, rows_ref,
):
    stride = 2 * share + SLOTS
    unpack_rows(table, sym_recv_ref, scratch_ref, SLOTS + 1, 0)
    join_phases(scratch_ref, sym_ref)
    unpack_rows(table, recv_ref, scratch_ref, stride, 0)
    join_phases(scratch_ref, map_ref)
    for index, out_ref in ((0, one_ref), (1, two_ref)):
        for d in range(len(table)):
            begin = d * stride + SLOTS + index * share
            rows_ref[d * share : (d + 1) * share, :] = recv_ref[begin : begin + share, :]
        for tap in range(9):
            block = rows_ref[tap * HALF // 2 : (tap + 1) * HALF // 2, :]
            out_ref[tap, : HALF // 2, :] = block[:, :HALF]
            out_ref[tap, HALF // 2 :, :] = swap_halves(block)[:, :HALF]
    for index, total_ref in ((0, total_one_ref), (1, total_two_ref)):
        total = total_ref[...] / residues
        shift_ref[index : index + 1, :] = total[:, :HALF]
        gain_ref[index : index + 1, :] = swap_halves(total)[:, :HALF]


def call(body, shapes, scratch=()):
    return pl.pallas_call(
        body,
        out_shape=[jax.ShapeDtypeStruct(s, jnp.float32) for s in shapes],
        scratch_shapes=[pltpu.VMEM(s, jnp.float32) for s in scratch],
        compiler_params=pltpu.CompilerParams(vmem_limit_bytes=VMEM_BYTES),
    )


def exchange(rows, devices):
    sent = rows.reshape(devices, 1, -1)
    received = lax.all_to_all(sent, AXES, split_axis=0, concat_axis=0, tiled=True)
    return received.reshape(-1, LANES)


def phase_body(pair_map, cotangent, conv_one, conv_two, norm_gain, norm_shift):
    devices = lax.axis_size("row") * lax.axis_size("col")
    residues = float(pair_map.shape[0] * lax.axis_size("row"))
    table = phase_table(devices)
    share = ROWS * 9 // 8 // devices
    whole, line, rows = (ROWS, LANES), (1, LANES), (devices * share, LANES)
    part = functools.partial

    def wide(count):
        return (devices * count, LANES)

    inputs = (pair_map, cotangent, norm_gain, norm_shift)
    send, grad_sent, affine = call(
        part(first_kernel, table), [whole, whole, (SLOTS, LANES)], [whole, whole]
    )(*(pltpu.with_memory_space_constraint(v, pltpu.HBM) for v in inputs))
    x = exchange(send, devices)
    hidden, send = call(part(conv_one_kernel, devices), [whole, wide(SLOTS + 1)])(
        x, conv_one, grad_sent
    )
    grad_recv = exchange(send, devices)
    normed_one, inverse_one, active, second, send = call(
        part(conv_two_kernel, devices), [whole, line, whole, whole, wide(share + 2)], [rows]
    )(grad_recv, hidden, x, conv_two, affine)
    normed_recv = exchange(send, devices)
    normed_two, inverse_two, grad_sum, send = call(
        part(output_kernel, devices, share), [whole, line, whole, wide(SLOTS + 1)]
    )(normed_recv, second, x, grad_recv, affine)
    sym_recv = exchange(send, devices)
    grad_before, total_two, send = call(
        part(back_two_kernel, devices, share), [whole, line, wide(2 * share + 1)], [rows, rows]
    )(
        sym_recv, grad_sum, normed_two, inverse_two, active, normed_one, x, conv_two, affine
    )
    recv = exchange(send, devices)
    total_one, send = call(
        part(back_one_kernel, devices, share, residues), [line, wide(2 * share + SLOTS)]
    )(recv, grad_before, normed_one, inverse_one, grad_sum, conv_one, affine, normed_recv)
    recv = exchange(send, devices)
    taps = conv_one.shape[0] * conv_one.shape[1]
    sym_out, grad_map, grad_one, grad_two, grad_gain, grad_shift = call(
        part(last_kernel, table, share, residues),
        [
            pair_map.shape, pair_map.shape, (taps, HALF, HALF), (taps, HALF, HALF),
            norm_gain.shape, norm_shift.shape,
        ],
        [whole, rows],
    )(sym_recv, recv, total_one, total_two)
    return (
        sym_out,
        grad_map,
        grad_one.reshape(conv_one.shape),
        grad_two.reshape(conv_two.shape),
        grad_gain,
        grad_shift,
    )


def body(pair_map, cotangent, conv_one, conv_two, norm_gain, norm_shift):
    devices = lax.axis_size("row") * lax.axis_size("col")
    fits = (
        conv_one.shape == (3, 3, HALF, HALF)
        and pair_map.shape == (DILATION_STEP, 2 * DILATION_STEP * HALF)
        and lax.axis_size("row") == SLOTS
        and lax.axis_size("col") == 4
    )
    plan = phase_body if fits else general_body
    return plan(pair_map, cotangent, conv_one, conv_two, norm_gain, norm_shift)


def solution(mesh):
    return jax.shard_map(
        body,
        mesh=mesh,
        in_specs=(P("row", "col"), P("row", "col"), P(), P(), P(), P()),
        out_specs=(P("row", "col"), P("row", "col"), P(), P(), P(), P()),
        check_vma=False,
    )
```

```python
import functools

import jax
import jax.numpy as jnp
from jax import lax
from jax.experimental import pallas as pl
from jax.experimental.pallas import tpu as pltpu
from jax.sharding import PartitionSpec as P

DILATION_STEP = 16


epsilon = 1e-05
highest = lax.Precision.HIGHEST


def extended_2(cells, sides, width):
    for axis, dim in sides:
        count = lax.axis_size(axis)
        ends = count - 1
        head = lax.slice_in_dim(cells, 0, width, axis=dim)
        tail = lax.slice_in_dim(cells, cells.shape[dim] - width, cells.shape[dim], axis=dim)
        cells = jnp.concatenate(
            [
                lax.ppermute(tail, axis, [(i, (i + 1) % count) for i in range(ends)]),
                cells,
                lax.ppermute(head, axis, [((i + 1) % count, i) for i in range(ends)]),
            ],
            axis=dim,
        )
    return cells


def extend(feature_field_patch):
    block_result = extended_2(feature_field_patch, (("row", 0), ("col", 1)), DILATION_STEP)
    return block_result


def tap_windows(extended, row_begin, column_starts, local_row_count, local_column_count):
    pieces = [
        extended[row_begin : row_begin + local_row_count, start : start + local_column_count]
        for start in column_starts
    ]
    joined = jnp.concatenate(pieces, axis=2)
    return joined.reshape(local_row_count * local_column_count, -1)


def dilated(extended, filter_weight, local_row_count, local_column_count):
    channels = filter_weight.shape[2]
    starts = [tap * DILATION_STEP for tap in range(3)]
    summed_taps = jnp.zeros(
        (local_row_count * local_column_count, filter_weight.shape[3]), jnp.float32
    )
    for filter_tap_row in range(3):
        window = tap_windows(
            extended, filter_tap_row * DILATION_STEP, starts, local_row_count, local_column_count
        )
        stacked = filter_weight[filter_tap_row].reshape(3 * channels, -1)
        summed_taps = summed_taps + jnp.dot(
            window, stacked, precision=highest, preferred_element_type=jnp.float32
        )
    return summed_taps.reshape(local_row_count, local_column_count, -1)


def dilated_back(grad_ext, filter_weight, local_row_count, local_column_count):
    channels = filter_weight.shape[3]
    starts = [(2 - tap) * DILATION_STEP for tap in range(3)]
    summed_taps = jnp.zeros(
        (local_row_count * local_column_count, filter_weight.shape[2]), jnp.float32
    )
    for filter_tap_row in range(3):
        window = tap_windows(
            grad_ext,
            (2 - filter_tap_row) * DILATION_STEP,
            starts,
            local_row_count,
            local_column_count,
        )
        stacked = jnp.transpose(filter_weight[filter_tap_row], (0, 2, 1)).reshape(3 * channels, -1)
        summed_taps = summed_taps + jnp.dot(
            window, stacked, precision=highest, preferred_element_type=jnp.float32
        )
    return summed_taps.reshape(local_row_count, local_column_count, -1)


def kernel_grad(extended, grad_tile, local_row_count, local_column_count):
    channels = extended.shape[2]
    starts = [tap * DILATION_STEP for tap in range(3)]
    grad_flat = grad_tile.reshape(-1, grad_tile.shape[2])
    tap_list = []
    for filter_tap_row in range(3):
        window = tap_windows(
            extended, filter_tap_row * DILATION_STEP, starts, local_row_count, local_column_count
        )
        product = lax.dot_general(
            window,
            grad_flat,
            (((0,), (0,)), ((), ())),
            precision=highest,
            preferred_element_type=jnp.float32,
        )
        tap_list.append(product.reshape(3, channels, -1))
    return jnp.stack(tap_list)


def normalize(hidden, cell_count):
    totals = lax.psum(jnp.sum(hidden, axis=(0, 1)), ("row", "col"))
    average = totals / cell_count
    centered = hidden - average
    spread = lax.psum(jnp.sum(centered * centered, axis=(0, 1)), ("row", "col"))
    variance = spread / cell_count
    inverse = lax.rsqrt(variance + epsilon)
    return ((hidden - average) * inverse, inverse)


def normalize_back(grad_normed, normed, inverse, gain_row, cell_count):
    shift_sum, gain_sum = lax.psum(
        (jnp.sum(grad_normed, axis=(0, 1)), jnp.sum(grad_normed * normed, axis=(0, 1))),
        ("row", "col"),
    )
    grad_scaled = grad_normed * gain_row
    grad_hidden = inverse * (
        grad_scaled
        - gain_row * shift_sum / cell_count
        - normed * (gain_row * gain_sum / cell_count)
    )
    return (grad_hidden, gain_sum, shift_sum)


def elu_slope(values):
    return jnp.where(values > 0, 1.0, jnp.exp(jnp.minimum(values, 0.0)))


def mirror_tile(tile_in):
    local_row_count, local_column_count, channels = tile_in.shape
    row_devices = lax.axis_size("row")
    col_devices = lax.axis_size("col")
    row_part = local_row_count // col_devices
    group = row_devices // col_devices
    sectioned = tile_in.reshape(col_devices, row_part, local_column_count, channels)
    sectioned = lax.all_to_all(sectioned, "col", split_axis=0, concat_axis=0, tiled=True)
    sectioned = (
        sectioned.reshape(col_devices, row_part, group, local_row_count, channels)
        .transpose(0, 2, 1, 3, 4)
        .reshape(row_devices, row_part, local_row_count, channels)
    )
    sectioned = lax.all_to_all(
        lax.all_to_all(sectioned, "row", split_axis=0, concat_axis=0, tiled=True),
        "col",
        split_axis=0,
        concat_axis=0,
        tiled=True,
    )
    sectioned = sectioned.reshape(
        col_devices, group, row_part, local_row_count, channels
    ).transpose(3, 1, 0, 2, 4)
    return sectioned.reshape(local_row_count, local_column_count, channels)


def general_body(pair_map, cotangent, conv_one, conv_two, norm_gain, norm_shift):
    channels = conv_one.shape[2]
    local_row_count = pair_map.shape[0]
    local_column_count = pair_map.shape[1] // channels
    residues = float(local_row_count * lax.axis_size("row"))
    cell_count = float(
        local_row_count * local_column_count * lax.axis_size("row") * lax.axis_size("col")
    )
    feature_field_patch = pair_map.reshape(local_row_count, local_column_count, channels)
    field_ext = extend(feature_field_patch)
    first_conv = dilated(field_ext, conv_one, local_row_count, local_column_count)
    normed_one, inverse_one = normalize(first_conv, cell_count)
    before_one = normed_one * norm_gain[0] + norm_shift[0]
    active = jax.nn.elu(before_one)
    active_ext = extend(active)
    second_conv = dilated(active_ext, conv_two, local_row_count, local_column_count)
    normed_two, inverse_two = normalize(second_conv, cell_count)
    summed = feature_field_patch + normed_two * norm_gain[1] + norm_shift[1]
    block_out = jax.nn.elu(summed)
    symmetric = 0.5 * (block_out + mirror_tile(block_out))
    grad_in = cotangent.reshape(local_row_count, local_column_count, channels)
    grad_out = 0.5 * (grad_in + mirror_tile(grad_in))
    grad_sum = grad_out * elu_slope(summed)
    grad_second, gain_two, shift_two = normalize_back(
        grad_sum, normed_two, inverse_two, norm_gain[1], cell_count
    )
    second_ext = extend(grad_second)
    grad_active = dilated_back(second_ext, conv_two, local_row_count, local_column_count)
    kernel_two = kernel_grad(active_ext, grad_second, local_row_count, local_column_count)
    grad_before = grad_active * elu_slope(before_one)
    grad_first, gain_one, shift_one = normalize_back(
        grad_before, normed_one, inverse_one, norm_gain[0], cell_count
    )
    first_ext = extend(grad_first)
    grad_field = grad_sum + dilated_back(first_ext, conv_one, local_row_count, local_column_count)
    kernel_one = kernel_grad(field_ext, grad_first, local_row_count, local_column_count)
    total_one, total_two = lax.psum((kernel_one, kernel_two), ("row", "col"))
    grad_gains = jnp.stack([gain_one, gain_two]) / residues
    grad_shifts = jnp.stack([shift_one, shift_two]) / residues
    return (
        symmetric.reshape(local_row_count, local_column_count * channels),
        grad_field.reshape(local_row_count, local_column_count * channels),
        total_one / residues,
        total_two / residues,
        grad_gains,
        grad_shifts,
    )


SLOTS = 8
LANES = 128
HALF = 64
ROWS = 256
AXES = ("row", "col")
VMEM_BYTES = 8 << 20
TAP_SOURCES = ((1, 2), (2, 3), (3, 0))


def phase_table(devices):
    pairs = [(r, s) for r in range(DILATION_STEP) for s in range(r + 1, DILATION_STEP)]
    table = []
    taken = 0
    diagonal = DILATION_STEP // 2
    for device in range(devices):
        count = SLOTS // 2 - (1 if device < diagonal else 0)
        upper = pairs[taken : taken + count]
        taken += count
        lower = [(s, r) for r, s in upper]
        if device < diagonal:
            upper = upper + [(2 * device, 2 * device)]
            lower = lower + [(2 * device + 1, 2 * device + 1)]
        table.append(upper + lower)
    return table


def lane_low(shape):
    return lax.broadcasted_iota(jnp.int32, shape, len(shape) - 1) < HALF


def swap_halves(values):
    return pltpu.roll(values, HALF, values.ndim - 1)


def fold_halves(values):
    return values + swap_halves(values)


def twice(row):
    return jnp.concatenate([row, row], axis=1)


def close_dot(left, right, dims):
    return lax.dot_general(
        left, right, (dims, ((), ())), precision=lax.Precision.HIGH, preferred_element_type=jnp.float32
    )


def split_phases(tile_ref, scratch_ref):
    low = lane_low((DILATION_STEP, LANES))
    for t in range(DILATION_STEP // 2):
        first = tile_ref[:, t * LANES : (t + 1) * LANES]
        begin = DILATION_STEP * HALF + t * LANES
        second = tile_ref[:, begin : begin + LANES]
        row = 2 * t * DILATION_STEP
        scratch_ref[row : row + DILATION_STEP, :] = jnp.where(low, first, swap_halves(second))
        row += DILATION_STEP
        scratch_ref[row : row + DILATION_STEP, :] = jnp.where(low, swap_halves(first), second)


def join_phases(scratch_ref, tile_ref):
    low = lane_low((DILATION_STEP, LANES))
    for t in range(DILATION_STEP // 2):
        row = 2 * t * DILATION_STEP
        even = scratch_ref[row : row + DILATION_STEP, :]
        odd = scratch_ref[row + DILATION_STEP : row + 2 * DILATION_STEP, :]
        tile_ref[:, t * LANES : (t + 1) * LANES] = jnp.where(low, even, swap_halves(odd))
        begin = DILATION_STEP * HALF + t * LANES
        tile_ref[:, begin : begin + LANES] = jnp.where(low, swap_halves(even), odd)


def pack_rows(table, scratch_ref, send_ref, stride):
    for device, slots in enumerate(table):
        for k, (r, s) in enumerate(slots):
            source = s * DILATION_STEP + r
            target = device * stride + k
            send_ref[target : target + 1, :] = scratch_ref[source : source + 1, :]


def unpack_rows(table, recv_ref, scratch_ref, stride, offset):
    for device, slots in enumerate(table):
        for k, (r, s) in enumerate(slots):
            target = s * DILATION_STEP + r
            source = device * stride + offset + k
            scratch_ref[target : target + 1, :] = recv_ref[source : source + 1, :]


def slot_rows(ref, stride, devices):
    return jnp.concatenate(
        [ref[d * stride : d * stride + SLOTS, :] for d in range(devices)], axis=0
    )


def neighbours(values):
    zero = jnp.zeros((SLOTS, LANES), jnp.float32)
    ahead = jnp.concatenate([values[SLOTS:], zero], axis=0)
    behind = jnp.concatenate([zero, values[:-SLOTS]], axis=0)
    place = (lax.broadcasted_iota(jnp.int32, (ROWS, LANES), 0) // SLOTS) % 4
    low = lane_low((ROWS, LANES))
    side = jnp.where(low, jnp.where(place == 3, 0.0, ahead), jnp.where(place == 0, 0.0, behind))
    return jnp.concatenate([side, values], axis=1)


def forward_weight(weight_ref):
    zero = jnp.zeros((HALF, HALF), jnp.float32)
    taps = []
    for a in range(3):
        w = [weight_ref[a, b] for b in range(3)]
        blocks = [(zero, w[2]), (w[0], zero), (w[1], w[0]), (w[2], w[1])]
        taps.append(
            jnp.concatenate([jnp.concatenate(list(b), axis=1) for b in blocks], axis=0)
        )
    return jnp.concatenate(taps, axis=1)


def backward_weight(weight_ref):
    zero = jnp.zeros((HALF, HALF), jnp.float32)
    taps = []
    for a in range(3):
        w = [weight_ref[2 - a, 2 - b] for b in range(3)]
        taps.append(jnp.concatenate([zero, w[0], w[1], w[2]], axis=1))
        taps.append(jnp.concatenate([w[2], zero, w[0], w[1]], axis=1))
    return jnp.concatenate(taps, axis=0)


def shifted_sum(parts):
    step = 4 * SLOTS
    zero = jnp.zeros((step, LANES), jnp.float32)
    first, middle, last = (parts[:, a * LANES : (a + 1) * LANES] for a in range(3))
    return (
        middle
        + jnp.concatenate([zero, first[:-step]], axis=0)
        + jnp.concatenate([last[step:], zero], axis=0)
    )


def spread_shifts(values):
    step = 4 * SLOTS
    zero = jnp.zeros((step, LANES), jnp.float32)
    return jnp.concatenate(
        [
            jnp.concatenate([values[step:], zero], axis=0),
            values,
            jnp.concatenate([zero, values[:-step]], axis=0),
        ],
        axis=1,
    )


def tap_rows(product):
    low = lane_low((HALF // 2, LANES))
    pieces = []
    for a in range(3):
        part = product[:, a * LANES : (a + 1) * LANES]
        for even, odd in TAP_SOURCES:
            tap = part[even * HALF : (even + 1) * HALF] + swap_halves(
                part[odd * HALF : (odd + 1) * HALF]
            )
            pieces.append(jnp.where(low, tap[: HALF // 2], swap_halves(tap[HALF // 2 :])))
    return jnp.concatenate(pieces, axis=0)


def kernel_rows(joined, grad):
    return tap_rows(close_dot(joined, spread_shifts(grad), ((0,), (0,))))


def kernel_rows_and_sums(joined, grad, devices):
    row = lax.broadcasted_iota(jnp.int32, (ROWS, LANES), 0)
    tap = (lax.broadcasted_iota(jnp.int32, (ROWS, LANES), 1) % HALF) % 3
    step = 4 * SLOTS
    outside = ((tap == 0) & (row >= ROWS - step)) | ((tap == 2) & (row < step))
    ones = jnp.where(outside, 0.0, 1.0)
    product = close_dot(
        joined, jnp.concatenate([spread_shifts(grad), ones], axis=1), ((0,), (0,))
    )
    part = product[:, 3 * LANES :]
    low = lane_low((HALF // 2, LANES))
    pieces = []
    for even, odd in TAP_SOURCES:
        both = part[even * HALF : (even + 1) * HALF] + part[odd * HALF : (odd + 1) * HALF]
        pieces.append(jnp.where(low, both[: HALF // 2], both[HALF // 2 :]))
    sums = jnp.concatenate(pieces * 3, axis=0)
    total = sums.shape[0]
    share = total // devices
    row = lax.broadcasted_iota(jnp.int32, (total, LANES), 0)
    lane = lax.broadcasted_iota(jnp.int32, (total, LANES), 1) % HALF
    sums = jnp.where(lane == 3 * (row % share) + row // (total // 3), sums, 0.0)
    owner = lax.broadcasted_iota(jnp.int32, (devices, total), 0)
    index = lax.broadcasted_iota(jnp.int32, (devices, total), 1)
    picked = (index // share == owner).astype(jnp.float32)
    return tap_rows(product), close_dot(picked, sums, ((1,), (0,)))


def widen_sums(row, share):
    lane = lax.broadcasted_iota(jnp.int32, (share, LANES), 1)
    index = lax.broadcasted_iota(jnp.int32, (share, LANES), 0)
    picked = jnp.where((lane % HALF) // 3 == index, row, 0.0)
    low = lane < HALF
    first = jnp.sum(jnp.where(low, picked, 0.0), axis=1, keepdims=True)
    second = jnp.sum(jnp.where(low, 0.0, picked), axis=1, keepdims=True)
    return jnp.where(low, first, second)


def local_stats(hidden):
    count = 2.0 * ROWS
    mean = fold_halves(jnp.sum(hidden, axis=0, keepdims=True)) / count
    centered = hidden - mean
    spread = fold_halves(jnp.sum(centered * centered, axis=0, keepdims=True))
    return jnp.where(lane_low((1, LANES)), mean, spread)


def combine_stats(rows, devices):
    low = lane_low((devices, LANES))
    means = jnp.where(low, rows, swap_halves(rows))
    spreads = jnp.where(low, swap_halves(rows), rows)
    mean = jnp.sum(means, axis=0, keepdims=True) / devices
    apart = means - mean
    total = jnp.sum(spreads + (2.0 * ROWS) * (apart * apart), axis=0, keepdims=True)
    return mean, lax.rsqrt(total / (2.0 * ROWS * devices) + epsilon)


def elu_value(values):
    return jnp.where(values > 0, values, jnp.exp(jnp.minimum(values, 0.0)) - 1.0)


def pair_sums(grad, normed):
    plain = fold_halves(jnp.sum(grad, axis=0, keepdims=True))
    scaled = fold_halves(jnp.sum(grad * normed, axis=0, keepdims=True))
    return jnp.where(lane_low((1, LANES)), plain, scaled)


def split_sums(rows):
    total = jnp.sum(rows, axis=0, keepdims=True)
    other = swap_halves(total)
    low = lane_low((1, LANES))
    return jnp.where(low, total, other), jnp.where(low, other, total)


def norm_back(grad, normed, inverse, gain, shift_sum, gain_sum, cells):
    return inverse * (gain * grad - gain * shift_sum / cells - normed * (gain * gain_sum / cells))


def mirrored(values, own_mask):
    low = lane_low((SLOTS, LANES))
    tiles = [values[i * SLOTS : (i + 1) * SLOTS] for i in range(ROWS // SLOTS)]
    pieces = []
    for p in range(SLOTS):
        for c in range(4):
            even = tiles[2 * c * 4 + p // 2]
            odd = tiles[(2 * c + 1) * 4 + p // 2]
            if p % 2 == 0:
                piece = jnp.where(low, even, swap_halves(odd))
            else:
                piece = jnp.where(low, swap_halves(even), odd)
            pieces.append(jnp.where(own_mask, piece, pltpu.roll(piece, 4, 0)))
    return jnp.concatenate(pieces, axis=0)


def own_mirrors():
    me = lax.axis_index("row") * lax.axis_size("col") + lax.axis_index("col")
    slot = lax.broadcasted_iota(jnp.int32, (SLOTS, LANES), 0)
    return (slot % 4 == 3) & (me < DILATION_STEP // 2)


def first_kernel(
    table, x_ref, g_ref, gain_ref, shift_ref, send_ref, grad_ref, affine_ref, scratch_ref, other_ref
):
    split_phases(x_ref, scratch_ref)
    pack_rows(table, scratch_ref, send_ref, SLOTS)
    split_phases(g_ref, other_ref)
    pack_rows(table, other_ref, grad_ref, SLOTS)
    affine_ref[...] = jnp.concatenate(
        [twice(gain_ref[...]), twice(shift_ref[...]), jnp.zeros((4, LANES), jnp.float32)], axis=0
    )


def conv_one_kernel(devices, x_ref, weight_ref, g_ref, hidden_ref, send_ref):
    stride = SLOTS + 1
    hidden = shifted_sum(
        close_dot(neighbours(x_ref[...]), forward_weight(weight_ref), ((1,), (0,)))
    )
    hidden_ref[...] = hidden
    stats = local_stats(hidden)
    for d in range(devices):
        send_ref[d * stride : d * stride + SLOTS, :] = g_ref[d * SLOTS : (d + 1) * SLOTS, :]
        send_ref[d * stride + SLOTS : (d + 1) * stride, :] = stats


def conv_two_kernel(
    devices, recv_ref, hidden_ref, x_ref, weight_ref, affine_ref,
    normed_ref, inverse_ref, active_ref, second_ref, send_ref, scratch_ref,
):
    mean, inverse = combine_stats(recv_ref[pl.ds(SLOTS, devices, stride=SLOTS + 1), :], devices)
    normed = (hidden_ref[...] - mean) * inverse
    normed_ref[...] = normed
    inverse_ref[...] = inverse
    active = elu_value(normed * affine_ref[0:1, :] + affine_ref[2:3, :])
    active_ref[...] = active
    second = shifted_sum(
        close_dot(neighbours(active), forward_weight(weight_ref), ((1,), (0,)))
    )
    second_ref[...] = second
    stats = local_stats(second)
    rows, sums = kernel_rows_and_sums(neighbours(x_ref[...]), normed, devices)
    scratch_ref[...] = rows
    share = rows.shape[0] // devices
    stride = share + 2
    for d in range(devices):
        begin = d * stride
        send_ref[begin : begin + share, :] = scratch_ref[d * share : (d + 1) * share, :]
        send_ref[begin + share : begin + share + 1, :] = sums[d : d + 1, :]
        send_ref[begin + share + 1 : begin + stride, :] = stats


def output_kernel(
    devices, share, recv_ref, second_ref, x_ref, grad_ref, affine_ref,
    normed_ref, inverse_ref, sum_ref, send_ref,
):
    stride = SLOTS + 1
    mean, inverse = combine_stats(
        recv_ref[pl.ds(share + 1, devices, stride=share + 2), :], devices
    )
    normed = (second_ref[...] - mean) * inverse
    normed_ref[...] = normed
    inverse_ref[...] = inverse
    summed = x_ref[...] + normed * affine_ref[1:2, :] + affine_ref[3:4, :]
    slope = jnp.exp(jnp.minimum(summed, 0.0))
    out = jnp.where(summed > 0, summed, slope - 1.0)
    own = own_mirrors()
    symmetric = 0.5 * (out + mirrored(out, own))
    for d in range(devices):
        send_ref[d * stride : d * stride + SLOTS, :] = symmetric[d * SLOTS : (d + 1) * SLOTS]
    grad_in = slot_rows(grad_ref, stride, devices)
    grad_out = 0.5 * (grad_in + mirrored(grad_in, own))
    grad_sum = grad_out * jnp.where(summed > 0, 1.0, slope)
    sum_ref[...] = grad_sum
    sums = pair_sums(grad_sum, normed)
    for d in range(devices):
        send_ref[d * stride + SLOTS : (d + 1) * stride, :] = sums


def back_two_kernel(
    devices, share, recv_ref, sum_ref, normed_two_ref, inverse_two_ref, active_ref, normed_ref,
    x_ref, weight_ref, affine_ref, before_ref, total_ref, send_ref, two_ref, one_ref,
):
    cells = 2.0 * ROWS * devices
    shift_sum, gain_sum = split_sums(recv_ref[pl.ds(SLOTS, devices, stride=SLOTS + 1), :])
    total_ref[...] = jnp.where(lane_low((1, LANES)), shift_sum, gain_sum)
    grad_second = norm_back(
        sum_ref[...], normed_two_ref[...], inverse_two_ref[...], affine_ref[1:2, :],
        shift_sum, gain_sum, cells,
    )
    grad_active = shifted_sum(
        close_dot(neighbours(grad_second), backward_weight(weight_ref), ((1,), (1,)))
    )
    normed = normed_ref[...]
    before = normed * affine_ref[0:1, :] + affine_ref[2:3, :]
    grad_before = grad_active * jnp.where(before > 0, 1.0, jnp.exp(jnp.minimum(before, 0.0)))
    before_ref[...] = grad_before
    sums = pair_sums(grad_before, normed)
    two_ref[...] = kernel_rows(neighbours(active_ref[...]), grad_second)
    one_ref[...] = kernel_rows(neighbours(x_ref[...]), grad_before)
    stride = 2 * share + 1
    for d in range(devices):
        begin = d * stride
        send_ref[begin : begin + share, :] = one_ref[d * share : (d + 1) * share, :]
        send_ref[begin + share : begin + 2 * share, :] = two_ref[d * share : (d + 1) * share, :]
        send_ref[begin + 2 * share : begin + stride, :] = sums


def reduce_share(ref, devices, begin, size, stride):
    total = ref[begin : begin + size, :]
    for d in range(1, devices):
        total = total + ref[d * stride + begin : d * stride + begin + size, :]
    return total


def owner_core(device):
    return device // 4 % 2


def back_one_kernel(
    devices, share, residues, recv_ref, before_ref, normed_ref, inverse_ref, sum_ref, weight_ref,
    affine_ref, normed_recv_ref, total_ref, send_ref,
):
    cells = 2.0 * ROWS * devices
    stride = 2 * share + 1
    shift_sum, gain_sum = split_sums(recv_ref[pl.ds(2 * share, devices, stride=stride), :])
    total_ref[...] = jnp.where(lane_low((1, LANES)), shift_sum, gain_sum)
    gain, inverse = affine_ref[0:1, :], inverse_ref[...]
    grad_first = norm_back(
        before_ref[...], normed_ref[...], inverse, gain, shift_sum, gain_sum, cells
    )
    field = sum_ref[...] + shifted_sum(
        close_dot(neighbours(grad_first), backward_weight(weight_ref), ((1,), (1,)))
    )
    one = reduce_share(recv_ref, devices, 0, share, stride)
    two = reduce_share(recv_ref, devices, share, share, stride)
    rows = reduce_share(normed_recv_ref, devices, 0, share + 1, share + 2)
    constant = widen_sums(rows[share : share + 1], share)
    one = (inverse * gain) * (
        one - constant * (shift_sum / cells) - rows[:share] * (gain_sum / cells)
    )
    one, two = one / residues, two / residues
    stride = share + SLOTS
    for d in range(devices):
        begin = d * stride
        send_ref[begin : begin + SLOTS, :] = field[d * SLOTS : (d + 1) * SLOTS]
        send_ref[begin + SLOTS : begin + stride, :] = two if owner_core(d) else one


def map_kernel(
    table, share, residues, sym_recv_ref, recv_ref, total_one_ref, total_two_ref,
    sym_ref, map_ref, gain_ref, shift_ref, scratch_ref, other_ref,
):
    unpack_rows(table, sym_recv_ref, scratch_ref, SLOTS + 1, 0)
    join_phases(scratch_ref, sym_ref)
    unpack_rows(table, recv_ref, other_ref, share + SLOTS, 0)
    join_phases(other_ref, map_ref)
    for index, total_ref in ((0, total_one_ref), (1, total_two_ref)):
        total = total_ref[...] / residues
        shift_ref[index : index + 1, :] = total[:, :HALF]
        gain_ref[index : index + 1, :] = swap_halves(total)[:, :HALF]


def grad_kernel(devices, share, mine_ref, partner_ref, one_ref, two_ref, first_ref, second_ref):
    stride = share + SLOTS
    for source_ref, rows_ref in ((mine_ref, first_ref), (partner_ref, second_ref)):
        for d in range(devices):
            begin = d * stride + SLOTS
            rows_ref[d * share : (d + 1) * share, :] = source_ref[begin : begin + share, :]
    even = lax.axis_index("row") % 2 == 0
    for tap in range(9):
        begin = tap * HALF // 2
        mine = first_ref[begin : begin + HALF // 2, :]
        partner = second_ref[begin : begin + HALF // 2, :]
        one, two = jnp.where(even, mine, partner), jnp.where(even, partner, mine)
        for block, out_ref in ((one, one_ref), (two, two_ref)):
            out_ref[tap, : HALF // 2, :] = block[:, :HALF]
            out_ref[tap, HALF // 2 :, :] = swap_halves(block)[:, :HALF]


def call(body, shapes, scratch=(), cost=None):
    return pl.pallas_call(
        body,
        out_shape=[jax.ShapeDtypeStruct(s, jnp.float32) for s in shapes],
        scratch_shapes=[pltpu.VMEM(s, jnp.float32) for s in scratch],
        compiler_params=pltpu.CompilerParams(vmem_limit_bytes=VMEM_BYTES),
        cost_estimate=cost,
    )


def exchange(rows, devices):
    sent = rows.reshape(devices, 1, -1)
    received = lax.all_to_all(sent, AXES, split_axis=0, concat_axis=0, tiled=True)
    return received.reshape(-1, LANES)


def phase_body(pair_map, cotangent, conv_one, conv_two, norm_gain, norm_shift):
    devices = lax.axis_size("row") * lax.axis_size("col")
    residues = float(pair_map.shape[0] * lax.axis_size("row"))
    table = phase_table(devices)
    share = ROWS * 9 // 8 // devices
    whole, line, rows = (ROWS, LANES), (1, LANES), (devices * share, LANES)
    part = functools.partial

    def wide(count):
        return (devices * count, LANES)

    inputs = (pair_map, cotangent, norm_gain, norm_shift)
    send, grad_sent, affine = call(
        part(first_kernel, table), [whole, whole, (SLOTS, LANES)], [whole, whole]
    )(*(pltpu.with_memory_space_constraint(v, pltpu.HBM) for v in inputs))
    x = exchange(send, devices)
    hidden, send = call(part(conv_one_kernel, devices), [whole, wide(SLOTS + 1)])(
        x, conv_one, grad_sent
    )
    grad_recv = exchange(send, devices)
    normed_one, inverse_one, active, second, send = call(
        part(conv_two_kernel, devices), [whole, line, whole, whole, wide(share + 2)], [rows]
    )(grad_recv, hidden, x, conv_two, affine)
    normed_recv = exchange(send, devices)
    normed_two, inverse_two, grad_sum, send = call(
        part(output_kernel, devices, share), [whole, line, whole, wide(SLOTS + 1)]
    )(normed_recv, second, x, grad_recv, affine)
    sym_recv = exchange(send, devices)
    grad_before, total_two, send = call(
        part(back_two_kernel, devices, share), [whole, line, wide(2 * share + 1)], [rows, rows]
    )(
        sym_recv, grad_sum, normed_two, inverse_two, active, normed_one, x, conv_two, affine
    )
    recv = exchange(send, devices)
    total_one, send = call(
        part(back_one_kernel, devices, share, residues), [line, wide(share + SLOTS)]
    )(recv, grad_before, normed_one, inverse_one, grad_sum, conv_one, affine, normed_recv)
    recv = exchange(send, devices)
    taps = conv_one.shape[0] * conv_one.shape[1]
    cores = [(i, i ^ 1) for i in range(lax.axis_size("row"))]
    partner = lax.ppermute(recv, "row", cores)
    sym_out, grad_map, grad_gain, grad_shift = call(
        part(map_kernel, table, share, residues),
        [pair_map.shape, pair_map.shape, norm_gain.shape, norm_shift.shape],
        [whole, whole],
        pl.CostEstimate(flops=4 << 20, bytes_accessed=4 << 20, transcendentals=0),
    )(sym_recv, recv, total_one, total_two)
    grad_one, grad_two = call(
        part(grad_kernel, devices, share), [(taps, HALF, HALF)] * 2, [rows, rows]
    )(recv, partner)
    return (
        sym_out,
        grad_map,
        grad_one.reshape(conv_one.shape),
        grad_two.reshape(conv_two.shape),
        grad_gain,
        grad_shift,
    )


def body(pair_map, cotangent, conv_one, conv_two, norm_gain, norm_shift):
    devices = lax.axis_size("row") * lax.axis_size("col")
    fits = (
        conv_one.shape == (3, 3, HALF, HALF)
        and pair_map.shape == (DILATION_STEP, 2 * DILATION_STEP * HALF)
        and lax.axis_size("row") == SLOTS
        and lax.axis_size("col") == 4
    )
    plan = phase_body if fits else general_body
    return plan(pair_map, cotangent, conv_one, conv_two, norm_gain, norm_shift)


def solution(mesh):
    return jax.shard_map(
        body,
        mesh=mesh,
        in_specs=(P("row", "col"), P("row", "col"), P(), P(), P(), P()),
        out_specs=(P("row", "col"), P("row", "col"), P(), P(), P(), P()),
        check_vma=False,
    )
```

```python
import functools

import jax
import jax.numpy as jnp
from jax import lax
from jax.experimental import pallas as pl
from jax.experimental.pallas import tpu as pltpu
from jax.sharding import PartitionSpec as P

DILATION_STEP = 16


epsilon = 1e-05
highest = lax.Precision.HIGHEST


def extended_2(cells, sides, width):
    for axis, dim in sides:
        count = lax.axis_size(axis)
        ends = count - 1
        head = lax.slice_in_dim(cells, 0, width, axis=dim)
        tail = lax.slice_in_dim(cells, cells.shape[dim] - width, cells.shape[dim], axis=dim)
        cells = jnp.concatenate(
            [
                lax.ppermute(tail, axis, [(i, (i + 1) % count) for i in range(ends)]),
                cells,
                lax.ppermute(head, axis, [((i + 1) % count, i) for i in range(ends)]),
            ],
            axis=dim,
        )
    return cells


def extend(feature_field_patch):
    block_result = extended_2(feature_field_patch, (("row", 0), ("col", 1)), DILATION_STEP)
    return block_result


def tap_windows(extended, row_begin, column_starts, local_row_count, local_column_count):
    pieces = [
        extended[row_begin : row_begin + local_row_count, start : start + local_column_count]
        for start in column_starts
    ]
    joined = jnp.concatenate(pieces, axis=2)
    return joined.reshape(local_row_count * local_column_count, -1)


def dilated(extended, filter_weight, local_row_count, local_column_count):
    channels = filter_weight.shape[2]
    starts = [tap * DILATION_STEP for tap in range(3)]
    summed_taps = jnp.zeros(
        (local_row_count * local_column_count, filter_weight.shape[3]), jnp.float32
    )
    for filter_tap_row in range(3):
        window = tap_windows(
            extended, filter_tap_row * DILATION_STEP, starts, local_row_count, local_column_count
        )
        stacked = filter_weight[filter_tap_row].reshape(3 * channels, -1)
        summed_taps = summed_taps + jnp.dot(
            window, stacked, precision=highest, preferred_element_type=jnp.float32
        )
    return summed_taps.reshape(local_row_count, local_column_count, -1)


def dilated_back(grad_ext, filter_weight, local_row_count, local_column_count):
    channels = filter_weight.shape[3]
    starts = [(2 - tap) * DILATION_STEP for tap in range(3)]
    summed_taps = jnp.zeros(
        (local_row_count * local_column_count, filter_weight.shape[2]), jnp.float32
    )
    for filter_tap_row in range(3):
        window = tap_windows(
            grad_ext,
            (2 - filter_tap_row) * DILATION_STEP,
            starts,
            local_row_count,
            local_column_count,
        )
        stacked = jnp.transpose(filter_weight[filter_tap_row], (0, 2, 1)).reshape(3 * channels, -1)
        summed_taps = summed_taps + jnp.dot(
            window, stacked, precision=highest, preferred_element_type=jnp.float32
        )
    return summed_taps.reshape(local_row_count, local_column_count, -1)


def kernel_grad(extended, grad_tile, local_row_count, local_column_count):
    channels = extended.shape[2]
    starts = [tap * DILATION_STEP for tap in range(3)]
    grad_flat = grad_tile.reshape(-1, grad_tile.shape[2])
    tap_list = []
    for filter_tap_row in range(3):
        window = tap_windows(
            extended, filter_tap_row * DILATION_STEP, starts, local_row_count, local_column_count
        )
        product = lax.dot_general(
            window,
            grad_flat,
            (((0,), (0,)), ((), ())),
            precision=highest,
            preferred_element_type=jnp.float32,
        )
        tap_list.append(product.reshape(3, channels, -1))
    return jnp.stack(tap_list)


def normalize(hidden, cell_count):
    totals = lax.psum(jnp.sum(hidden, axis=(0, 1)), ("row", "col"))
    average = totals / cell_count
    centered = hidden - average
    spread = lax.psum(jnp.sum(centered * centered, axis=(0, 1)), ("row", "col"))
    variance = spread / cell_count
    inverse = lax.rsqrt(variance + epsilon)
    return ((hidden - average) * inverse, inverse)


def normalize_back(grad_normed, normed, inverse, gain_row, cell_count):
    shift_sum, gain_sum = lax.psum(
        (jnp.sum(grad_normed, axis=(0, 1)), jnp.sum(grad_normed * normed, axis=(0, 1))),
        ("row", "col"),
    )
    grad_scaled = grad_normed * gain_row
    grad_hidden = inverse * (
        grad_scaled
        - gain_row * shift_sum / cell_count
        - normed * (gain_row * gain_sum / cell_count)
    )
    return (grad_hidden, gain_sum, shift_sum)


def elu_slope(values):
    return jnp.where(values > 0, 1.0, jnp.exp(jnp.minimum(values, 0.0)))


def mirror_tile(tile_in):
    local_row_count, local_column_count, channels = tile_in.shape
    row_devices = lax.axis_size("row")
    col_devices = lax.axis_size("col")
    row_part = local_row_count // col_devices
    group = row_devices // col_devices
    sectioned = tile_in.reshape(col_devices, row_part, local_column_count, channels)
    sectioned = lax.all_to_all(sectioned, "col", split_axis=0, concat_axis=0, tiled=True)
    sectioned = (
        sectioned.reshape(col_devices, row_part, group, local_row_count, channels)
        .transpose(0, 2, 1, 3, 4)
        .reshape(row_devices, row_part, local_row_count, channels)
    )
    sectioned = lax.all_to_all(
        lax.all_to_all(sectioned, "row", split_axis=0, concat_axis=0, tiled=True),
        "col",
        split_axis=0,
        concat_axis=0,
        tiled=True,
    )
    sectioned = sectioned.reshape(
        col_devices, group, row_part, local_row_count, channels
    ).transpose(3, 1, 0, 2, 4)
    return sectioned.reshape(local_row_count, local_column_count, channels)


def general_body(pair_map, cotangent, conv_one, conv_two, norm_gain, norm_shift):
    channels = conv_one.shape[2]
    local_row_count = pair_map.shape[0]
    local_column_count = pair_map.shape[1] // channels
    residues = float(local_row_count * lax.axis_size("row"))
    cell_count = float(
        local_row_count * local_column_count * lax.axis_size("row") * lax.axis_size("col")
    )
    feature_field_patch = pair_map.reshape(local_row_count, local_column_count, channels)
    field_ext = extend(feature_field_patch)
    first_conv = dilated(field_ext, conv_one, local_row_count, local_column_count)
    normed_one, inverse_one = normalize(first_conv, cell_count)
    before_one = normed_one * norm_gain[0] + norm_shift[0]
    active = jax.nn.elu(before_one)
    active_ext = extend(active)
    second_conv = dilated(active_ext, conv_two, local_row_count, local_column_count)
    normed_two, inverse_two = normalize(second_conv, cell_count)
    summed = feature_field_patch + normed_two * norm_gain[1] + norm_shift[1]
    block_out = jax.nn.elu(summed)
    symmetric = 0.5 * (block_out + mirror_tile(block_out))
    grad_in = cotangent.reshape(local_row_count, local_column_count, channels)
    grad_out = 0.5 * (grad_in + mirror_tile(grad_in))
    grad_sum = grad_out * elu_slope(summed)
    grad_second, gain_two, shift_two = normalize_back(
        grad_sum, normed_two, inverse_two, norm_gain[1], cell_count
    )
    second_ext = extend(grad_second)
    grad_active = dilated_back(second_ext, conv_two, local_row_count, local_column_count)
    kernel_two = kernel_grad(active_ext, grad_second, local_row_count, local_column_count)
    grad_before = grad_active * elu_slope(before_one)
    grad_first, gain_one, shift_one = normalize_back(
        grad_before, normed_one, inverse_one, norm_gain[0], cell_count
    )
    first_ext = extend(grad_first)
    grad_field = grad_sum + dilated_back(first_ext, conv_one, local_row_count, local_column_count)
    kernel_one = kernel_grad(field_ext, grad_first, local_row_count, local_column_count)
    total_one, total_two = lax.psum((kernel_one, kernel_two), ("row", "col"))
    grad_gains = jnp.stack([gain_one, gain_two]) / residues
    grad_shifts = jnp.stack([shift_one, shift_two]) / residues
    return (
        symmetric.reshape(local_row_count, local_column_count * channels),
        grad_field.reshape(local_row_count, local_column_count * channels),
        total_one / residues,
        total_two / residues,
        grad_gains,
        grad_shifts,
    )


SLOTS = 8
LANES = 128
HALF = 64
ROWS = 256
AXES = ("row", "col")
VMEM_BYTES = 8 << 20
TAP_SOURCES = ((1, 2), (2, 3), (3, 0))


def phase_table(devices):
    pairs = [(r, s) for r in range(DILATION_STEP) for s in range(r + 1, DILATION_STEP)]
    table = []
    taken = 0
    diagonal = DILATION_STEP // 2
    for device in range(devices):
        count = SLOTS // 2 - (1 if device < diagonal else 0)
        upper = pairs[taken : taken + count]
        taken += count
        lower = [(s, r) for r, s in upper]
        if device < diagonal:
            upper = upper + [(2 * device, 2 * device)]
            lower = lower + [(2 * device + 1, 2 * device + 1)]
        table.append(upper + lower)
    return table


def lane_low(shape):
    return lax.broadcasted_iota(jnp.int32, shape, len(shape) - 1) < HALF


def swap_halves(values):
    return pltpu.roll(values, HALF, values.ndim - 1)


def fold_halves(values):
    return values + swap_halves(values)


def twice(row):
    return jnp.concatenate([row, row], axis=1)


def close_dot(left, right, dims):
    return lax.dot_general(
        left, right, (dims, ((), ())), precision=lax.Precision.HIGH, preferred_element_type=jnp.float32
    )


def split_phases(tile_ref, scratch_ref):
    low = lane_low((DILATION_STEP, LANES))
    for t in range(DILATION_STEP // 2):
        first = tile_ref[:, t * LANES : (t + 1) * LANES]
        begin = DILATION_STEP * HALF + t * LANES
        second = tile_ref[:, begin : begin + LANES]
        row = 2 * t * DILATION_STEP
        scratch_ref[row : row + DILATION_STEP, :] = jnp.where(low, first, swap_halves(second))
        row += DILATION_STEP
        scratch_ref[row : row + DILATION_STEP, :] = jnp.where(low, swap_halves(first), second)


def join_phases(scratch_ref, tile_ref):
    low = lane_low((DILATION_STEP, LANES))
    for t in range(DILATION_STEP // 2):
        row = 2 * t * DILATION_STEP
        even = scratch_ref[row : row + DILATION_STEP, :]
        odd = scratch_ref[row + DILATION_STEP : row + 2 * DILATION_STEP, :]
        tile_ref[:, t * LANES : (t + 1) * LANES] = jnp.where(low, even, swap_halves(odd))
        begin = DILATION_STEP * HALF + t * LANES
        tile_ref[:, begin : begin + LANES] = jnp.where(low, swap_halves(even), odd)


def pack_rows(table, scratch_ref, send_ref, stride):
    for device, slots in enumerate(table):
        for k, (r, s) in enumerate(slots):
            source = s * DILATION_STEP + r
            target = device * stride + k
            send_ref[target : target + 1, :] = scratch_ref[source : source + 1, :]


def unpack_rows(table, recv_ref, scratch_ref, stride, offset):
    for device, slots in enumerate(table):
        for k, (r, s) in enumerate(slots):
            target = s * DILATION_STEP + r
            source = device * stride + offset + k
            scratch_ref[target : target + 1, :] = recv_ref[source : source + 1, :]


def slot_rows(ref, stride, devices):
    return jnp.concatenate(
        [ref[d * stride : d * stride + SLOTS, :] for d in range(devices)], axis=0
    )


def neighbours(values):
    zero = jnp.zeros((SLOTS, LANES), jnp.float32)
    ahead = jnp.concatenate([values[SLOTS:], zero], axis=0)
    behind = jnp.concatenate([zero, values[:-SLOTS]], axis=0)
    place = (lax.broadcasted_iota(jnp.int32, (ROWS, LANES), 0) // SLOTS) % 4
    low = lane_low((ROWS, LANES))
    side = jnp.where(low, jnp.where(place == 3, 0.0, ahead), jnp.where(place == 0, 0.0, behind))
    return jnp.concatenate([side, values], axis=1)


def forward_weight(weight_ref):
    zero = jnp.zeros((HALF, HALF), jnp.float32)
    taps = []
    for a in range(3):
        w = [weight_ref[a, b] for b in range(3)]
        blocks = [(zero, w[2]), (w[0], zero), (w[1], w[0]), (w[2], w[1])]
        taps.append(
            jnp.concatenate([jnp.concatenate(list(b), axis=1) for b in blocks], axis=0)
        )
    return jnp.concatenate(taps, axis=1)


def backward_weight(weight_ref):
    zero = jnp.zeros((HALF, HALF), jnp.float32)
    taps = []
    for a in range(3):
        w = [weight_ref[2 - a, 2 - b] for b in range(3)]
        taps.append(jnp.concatenate([zero, w[0], w[1], w[2]], axis=1))
        taps.append(jnp.concatenate([w[2], zero, w[0], w[1]], axis=1))
    return jnp.concatenate(taps, axis=0)


def shifted_sum(parts):
    step = 4 * SLOTS
    zero = jnp.zeros((step, LANES), jnp.float32)
    first, middle, last = (parts[:, a * LANES : (a + 1) * LANES] for a in range(3))
    return (
        middle
        + jnp.concatenate([zero, first[:-step]], axis=0)
        + jnp.concatenate([last[step:], zero], axis=0)
    )


def spread_shifts(values):
    step = 4 * SLOTS
    zero = jnp.zeros((step, LANES), jnp.float32)
    return jnp.concatenate(
        [
            jnp.concatenate([values[step:], zero], axis=0),
            values,
            jnp.concatenate([zero, values[:-step]], axis=0),
        ],
        axis=1,
    )


def tap_rows(product):
    low = lane_low((HALF // 2, LANES))
    pieces = []
    for a in range(3):
        part = product[:, a * LANES : (a + 1) * LANES]
        for even, odd in TAP_SOURCES:
            tap = part[even * HALF : (even + 1) * HALF] + swap_halves(
                part[odd * HALF : (odd + 1) * HALF]
            )
            pieces.append(jnp.where(low, tap[: HALF // 2], swap_halves(tap[HALF // 2 :])))
    return jnp.concatenate(pieces, axis=0)


def kernel_rows(joined, grad):
    return tap_rows(close_dot(joined, spread_shifts(grad), ((0,), (0,))))


def kernel_rows_and_sums(joined, grad, devices):
    row = lax.broadcasted_iota(jnp.int32, (ROWS, LANES), 0)
    tap = (lax.broadcasted_iota(jnp.int32, (ROWS, LANES), 1) % HALF) % 3
    step = 4 * SLOTS
    outside = ((tap == 0) & (row >= ROWS - step)) | ((tap == 2) & (row < step))
    ones = jnp.where(outside, 0.0, 1.0)
    product = close_dot(
        joined, jnp.concatenate([spread_shifts(grad), ones], axis=1), ((0,), (0,))
    )
    part = product[:, 3 * LANES :]
    low = lane_low((HALF // 2, LANES))
    pieces = []
    for even, odd in TAP_SOURCES:
        both = part[even * HALF : (even + 1) * HALF] + part[odd * HALF : (odd + 1) * HALF]
        pieces.append(jnp.where(low, both[: HALF // 2], both[HALF // 2 :]))
    sums = jnp.concatenate(pieces * 3, axis=0)
    total = sums.shape[0]
    share = total // devices
    row = lax.broadcasted_iota(jnp.int32, (total, LANES), 0)
    lane = lax.broadcasted_iota(jnp.int32, (total, LANES), 1) % HALF
    sums = jnp.where(lane == 3 * (row % share) + row // (total // 3), sums, 0.0)
    owner = lax.broadcasted_iota(jnp.int32, (devices, total), 0)
    index = lax.broadcasted_iota(jnp.int32, (devices, total), 1)
    picked = (index // share == owner).astype(jnp.float32)
    return tap_rows(product), close_dot(picked, sums, ((1,), (0,)))


def widen_sums(row, share):
    lane = lax.broadcasted_iota(jnp.int32, (share, LANES), 1)
    index = lax.broadcasted_iota(jnp.int32, (share, LANES), 0)
    picked = jnp.where((lane % HALF) // 3 == index, row, 0.0)
    low = lane < HALF
    first = jnp.sum(jnp.where(low, picked, 0.0), axis=1, keepdims=True)
    second = jnp.sum(jnp.where(low, 0.0, picked), axis=1, keepdims=True)
    return jnp.where(low, first, second)


def local_stats(hidden):
    count = 2.0 * ROWS
    mean = fold_halves(jnp.sum(hidden, axis=0, keepdims=True)) / count
    centered = hidden - mean
    spread = fold_halves(jnp.sum(centered * centered, axis=0, keepdims=True))
    return jnp.where(lane_low((1, LANES)), mean, spread)


def combine_stats(rows, devices):
    low = lane_low((devices, LANES))
    means = jnp.where(low, rows, swap_halves(rows))
    spreads = jnp.where(low, swap_halves(rows), rows)
    mean = jnp.sum(means, axis=0, keepdims=True) / devices
    apart = means - mean
    total = jnp.sum(spreads + (2.0 * ROWS) * (apart * apart), axis=0, keepdims=True)
    return mean, lax.rsqrt(total / (2.0 * ROWS * devices) + epsilon)


def elu_value(values):
    return jnp.where(values > 0, values, jnp.exp(jnp.minimum(values, 0.0)) - 1.0)


def pair_sums(grad, normed):
    plain = fold_halves(jnp.sum(grad, axis=0, keepdims=True))
    scaled = fold_halves(jnp.sum(grad * normed, axis=0, keepdims=True))
    return jnp.where(lane_low((1, LANES)), plain, scaled)


def split_sums(rows):
    total = jnp.sum(rows, axis=0, keepdims=True)
    other = swap_halves(total)
    low = lane_low((1, LANES))
    return jnp.where(low, total, other), jnp.where(low, other, total)


def norm_back(grad, normed, inverse, gain, shift_sum, gain_sum, cells):
    return inverse * (gain * grad - gain * shift_sum / cells - normed * (gain * gain_sum / cells))


def mirrored(values, own_mask):
    low = lane_low((SLOTS, LANES))
    tiles = [values[i * SLOTS : (i + 1) * SLOTS] for i in range(ROWS // SLOTS)]
    pieces = []
    for p in range(SLOTS):
        for c in range(4):
            even = tiles[2 * c * 4 + p // 2]
            odd = tiles[(2 * c + 1) * 4 + p // 2]
            if p % 2 == 0:
                piece = jnp.where(low, even, swap_halves(odd))
            else:
                piece = jnp.where(low, swap_halves(even), odd)
            pieces.append(jnp.where(own_mask, piece, pltpu.roll(piece, 4, 0)))
    return jnp.concatenate(pieces, axis=0)


def own_mirrors():
    me = lax.axis_index("row") * lax.axis_size("col") + lax.axis_index("col")
    slot = lax.broadcasted_iota(jnp.int32, (SLOTS, LANES), 0)
    return (slot % 4 == 3) & (me < DILATION_STEP // 2)


def first_kernel(
    table, x_ref, g_ref, gain_ref, shift_ref, send_ref, grad_ref, affine_ref, scratch_ref, other_ref
):
    split_phases(x_ref, scratch_ref)
    pack_rows(table, scratch_ref, send_ref, SLOTS)
    split_phases(g_ref, other_ref)
    pack_rows(table, other_ref, grad_ref, SLOTS)
    affine_ref[...] = jnp.concatenate(
        [twice(gain_ref[...]), twice(shift_ref[...]), jnp.zeros((4, LANES), jnp.float32)], axis=0
    )


def conv_one_kernel(devices, x_ref, weight_ref, g_ref, hidden_ref, send_ref):
    stride = SLOTS + 1
    hidden = shifted_sum(
        close_dot(neighbours(x_ref[...]), forward_weight(weight_ref), ((1,), (0,)))
    )
    hidden_ref[...] = hidden
    stats = local_stats(hidden)
    for d in range(devices):
        send_ref[d * stride : d * stride + SLOTS, :] = g_ref[d * SLOTS : (d + 1) * SLOTS, :]
        send_ref[d * stride + SLOTS : (d + 1) * stride, :] = stats


def conv_two_kernel(
    devices, recv_ref, hidden_ref, x_ref, weight_ref, affine_ref,
    normed_ref, inverse_ref, active_ref, second_ref, send_ref, scratch_ref,
):
    mean, inverse = combine_stats(recv_ref[pl.ds(SLOTS, devices, stride=SLOTS + 1), :], devices)
    normed = (hidden_ref[...] - mean) * inverse
    normed_ref[...] = normed
    inverse_ref[...] = inverse
    active = elu_value(normed * affine_ref[0:1, :] + affine_ref[2:3, :])
    active_ref[...] = active
    second = shifted_sum(
        close_dot(neighbours(active), forward_weight(weight_ref), ((1,), (0,)))
    )
    second_ref[...] = second
    stats = local_stats(second)
    rows, sums = kernel_rows_and_sums(neighbours(x_ref[...]), normed, devices)
    scratch_ref[...] = rows
    share = rows.shape[0] // devices
    stride = share + 2
    for d in range(devices):
        begin = d * stride
        send_ref[begin : begin + share, :] = scratch_ref[d * share : (d + 1) * share, :]
        send_ref[begin + share : begin + share + 1, :] = sums[d : d + 1, :]
        send_ref[begin + share + 1 : begin + stride, :] = stats


def output_kernel(
    devices, share, recv_ref, second_ref, x_ref, grad_ref, affine_ref,
    normed_ref, inverse_ref, sum_ref, send_ref,
):
    stride = SLOTS + 1
    mean, inverse = combine_stats(
        recv_ref[pl.ds(share + 1, devices, stride=share + 2), :], devices
    )
    normed = (second_ref[...] - mean) * inverse
    normed_ref[...] = normed
    inverse_ref[...] = inverse
    summed = x_ref[...] + normed * affine_ref[1:2, :] + affine_ref[3:4, :]
    slope = jnp.exp(jnp.minimum(summed, 0.0))
    out = jnp.where(summed > 0, summed, slope - 1.0)
    own = own_mirrors()
    symmetric = 0.5 * (out + mirrored(out, own))
    for d in range(devices):
        send_ref[d * stride : d * stride + SLOTS, :] = symmetric[d * SLOTS : (d + 1) * SLOTS]
    grad_in = slot_rows(grad_ref, stride, devices)
    grad_out = 0.5 * (grad_in + mirrored(grad_in, own))
    grad_sum = grad_out * jnp.where(summed > 0, 1.0, slope)
    sum_ref[...] = grad_sum
    sums = pair_sums(grad_sum, normed)
    for d in range(devices):
        send_ref[d * stride + SLOTS : (d + 1) * stride, :] = sums


def back_two_kernel(
    devices, recv_ref, sum_ref, normed_two_ref, inverse_two_ref, active_ref, normed_ref,
    x_ref, weight_ref, affine_ref, before_ref, total_ref, sums_ref, keep_ref, give_ref,
):
    cells = 2.0 * ROWS * devices
    shift_sum, gain_sum = split_sums(recv_ref[pl.ds(SLOTS, devices, stride=SLOTS + 1), :])
    total_ref[...] = jnp.where(lane_low((1, LANES)), shift_sum, gain_sum)
    grad_second = norm_back(
        sum_ref[...], normed_two_ref[...], inverse_two_ref[...], affine_ref[1:2, :],
        shift_sum, gain_sum, cells,
    )
    grad_active = shifted_sum(
        close_dot(neighbours(grad_second), backward_weight(weight_ref), ((1,), (1,)))
    )
    normed = normed_ref[...]
    before = normed * affine_ref[0:1, :] + affine_ref[2:3, :]
    grad_before = grad_active * jnp.where(before > 0, 1.0, jnp.exp(jnp.minimum(before, 0.0)))
    before_ref[...] = grad_before
    sums_ref[...] = pair_sums(grad_before, normed)
    two = kernel_rows(neighbours(active_ref[...]), grad_second)
    one = kernel_rows(neighbours(x_ref[...]), grad_before)
    even = lax.axis_index("row") % 2 == 0
    keep_ref[...] = jnp.where(even, one, two)
    give_ref[...] = jnp.where(even, two, one)


def pair_kernel(devices, share, keep_ref, got_ref, sums_ref, before_exchange_ref, send_ref):
    del before_exchange_ref
    stride = share + 1
    sums = sums_ref[...]
    for d in range(devices):
        rows = slice(d * share, (d + 1) * share)
        send_ref[d * stride : d * stride + share, :] = keep_ref[rows, :] + got_ref[rows, :]
        send_ref[d * stride + share : (d + 1) * stride, :] = sums


def constant_kernel(devices, share, recv_ref, weight_ref, rows_ref, constant_ref, joined_ref):
    rows = reduce_share(recv_ref, range(devices), 0, share + 1, share + 2)
    rows_ref[...] = rows[:share]
    constant_ref[...] = widen_sums(rows[share : share + 1], share)
    joined_ref[...] = backward_weight(weight_ref)


def reduce_share(ref, sources, begin, size, stride):
    total = None
    for d in sources:
        rows = ref[d * stride + begin : d * stride + begin + size, :]
        total = rows if total is None else total + rows
    return total


def owner_core(device):
    return device // 4 % 2


def back_one_kernel(
    devices, share, residues, recv_ref, before_ref, normed_ref, inverse_ref, sum_ref, joined_ref,
    affine_ref, rows_ref, constant_ref, total_ref, send_ref,
):
    cells = 2.0 * ROWS * devices
    stride = share + 1
    shift_sum, gain_sum = split_sums(recv_ref[pl.ds(share, devices, stride=stride), :])
    total_ref[...] = jnp.where(lane_low((1, LANES)), shift_sum, gain_sum)
    gain, inverse = affine_ref[0:1, :], inverse_ref[...]
    grad_first = norm_back(
        before_ref[...], normed_ref[...], inverse, gain, shift_sum, gain_sum, cells
    )
    field = sum_ref[...] + shifted_sum(
        close_dot(neighbours(grad_first), joined_ref[...], ((1,), (1,)))
    )
    sources = range(devices)
    one = reduce_share(recv_ref, [d for d in sources if not owner_core(d)], 0, share, stride)
    two = reduce_share(recv_ref, [d for d in sources if owner_core(d)], 0, share, stride)
    one = (inverse * gain) * (
        one - constant_ref[...] * (shift_sum / cells) - rows_ref[...] * (gain_sum / cells)
    )
    one, two = one / residues, two / residues
    stride = share + SLOTS
    for d in range(devices):
        begin = d * stride
        send_ref[begin : begin + SLOTS, :] = field[d * SLOTS : (d + 1) * SLOTS]
        send_ref[begin + SLOTS : begin + stride, :] = two if owner_core(d) else one


def map_kernel(
    table, share, residues, sym_recv_ref, recv_ref, total_one_ref, total_two_ref,
    sym_ref, map_ref, gain_ref, shift_ref, scratch_ref, other_ref,
):
    unpack_rows(table, sym_recv_ref, scratch_ref, SLOTS + 1, 0)
    join_phases(scratch_ref, sym_ref)
    unpack_rows(table, recv_ref, other_ref, share + SLOTS, 0)
    join_phases(other_ref, map_ref)
    for index, total_ref in ((0, total_one_ref), (1, total_two_ref)):
        total = total_ref[...] / residues
        shift_ref[index : index + 1, :] = total[:, :HALF]
        gain_ref[index : index + 1, :] = swap_halves(total)[:, :HALF]


def grad_kernel(devices, share, mine_ref, partner_ref, one_ref, two_ref, first_ref, second_ref):
    stride = share + SLOTS
    for source_ref, rows_ref in ((mine_ref, first_ref), (partner_ref, second_ref)):
        for d in range(devices):
            begin = d * stride + SLOTS
            rows_ref[d * share : (d + 1) * share, :] = source_ref[begin : begin + share, :]
    even = lax.axis_index("row") % 2 == 0
    for tap in range(9):
        begin = tap * HALF // 2
        mine = first_ref[begin : begin + HALF // 2, :]
        partner = second_ref[begin : begin + HALF // 2, :]
        one, two = jnp.where(even, mine, partner), jnp.where(even, partner, mine)
        for block, out_ref in ((one, one_ref), (two, two_ref)):
            out_ref[tap, : HALF // 2, :] = block[:, :HALF]
            out_ref[tap, HALF // 2 :, :] = swap_halves(block)[:, :HALF]


def call(body, shapes, scratch=(), cost=None):
    return pl.pallas_call(
        body,
        out_shape=[jax.ShapeDtypeStruct(s, jnp.float32) for s in shapes],
        scratch_shapes=[pltpu.VMEM(s, jnp.float32) for s in scratch],
        compiler_params=pltpu.CompilerParams(vmem_limit_bytes=VMEM_BYTES),
        cost_estimate=cost,
    )


def exchange(rows, devices):
    sent = rows.reshape(devices, 1, -1)
    received = lax.all_to_all(sent, AXES, split_axis=0, concat_axis=0, tiled=True)
    return received.reshape(-1, LANES)


def phase_body(pair_map, cotangent, conv_one, conv_two, norm_gain, norm_shift):
    devices = lax.axis_size("row") * lax.axis_size("col")
    residues = float(pair_map.shape[0] * lax.axis_size("row"))
    table = phase_table(devices)
    share = ROWS * 9 // 8 // devices
    whole, line, rows = (ROWS, LANES), (1, LANES), (devices * share, LANES)
    part = functools.partial

    def wide(count):
        return (devices * count, LANES)

    inputs = (pair_map, cotangent, norm_gain, norm_shift)
    send, grad_sent, affine = call(
        part(first_kernel, table), [whole, whole, (SLOTS, LANES)], [whole, whole]
    )(*(pltpu.with_memory_space_constraint(v, pltpu.HBM) for v in inputs))
    x = exchange(send, devices)
    hidden, send = call(part(conv_one_kernel, devices), [whole, wide(SLOTS + 1)])(
        x, conv_one, grad_sent
    )
    grad_recv = exchange(send, devices)
    normed_one, inverse_one, active, second, send = call(
        part(conv_two_kernel, devices), [whole, line, whole, whole, wide(share + 2)], [rows]
    )(grad_recv, hidden, x, conv_two, affine)
    normed_recv = exchange(send, devices)
    normed_two, inverse_two, grad_sum, send = call(
        part(output_kernel, devices, share), [whole, line, whole, wide(SLOTS + 1)]
    )(normed_recv, second, x, grad_recv, affine)
    sym_recv = exchange(send, devices)
    cores = [(i, i ^ 1) for i in range(lax.axis_size("row"))]
    cost = pl.CostEstimate(flops=4 << 20, bytes_accessed=4 << 20, transcendentals=0)
    grad_before, total_two, sums, keep, give = call(
        part(back_two_kernel, devices), [whole, line, line, rows, rows]
    )(
        sym_recv, grad_sum, normed_two, inverse_two, active, normed_one, x, conv_two, affine
    )
    got = lax.ppermute(give, "row", cores)
    normed_rows, constant, joined = call(
        part(constant_kernel, devices, share),
        [(share, LANES), (share, LANES), (3 * LANES, 2 * LANES)],
        cost=cost,
    )(normed_recv, conv_one)
    (send,) = call(part(pair_kernel, devices, share), [wide(share + 1)])(
        keep, got, sums, constant
    )
    recv = exchange(send, devices)
    total_one, send = call(
        part(back_one_kernel, devices, share, residues), [line, wide(share + SLOTS)]
    )(
        recv, grad_before, normed_one, inverse_one, grad_sum, joined, affine, normed_rows, constant
    )
    recv = exchange(send, devices)
    taps = conv_one.shape[0] * conv_one.shape[1]
    partner = lax.ppermute(recv, "row", cores)
    sym_out, grad_map, grad_gain, grad_shift = call(
        part(map_kernel, table, share, residues),
        [pair_map.shape, pair_map.shape, norm_gain.shape, norm_shift.shape],
        [whole, whole],
        cost,
    )(sym_recv, recv, total_one, total_two)
    grad_one, grad_two = call(
        part(grad_kernel, devices, share), [(taps, HALF, HALF)] * 2, [rows, rows]
    )(recv, partner)
    return (
        sym_out,
        grad_map,
        grad_one.reshape(conv_one.shape),
        grad_two.reshape(conv_two.shape),
        grad_gain,
        grad_shift,
    )


def body(pair_map, cotangent, conv_one, conv_two, norm_gain, norm_shift):
    devices = lax.axis_size("row") * lax.axis_size("col")
    fits = (
        conv_one.shape == (3, 3, HALF, HALF)
        and pair_map.shape == (DILATION_STEP, 2 * DILATION_STEP * HALF)
        and lax.axis_size("row") == SLOTS
        and lax.axis_size("col") == 4
    )
    plan = phase_body if fits else general_body
    return plan(pair_map, cotangent, conv_one, conv_two, norm_gain, norm_shift)


def solution(mesh):
    return jax.shard_map(
        body,
        mesh=mesh,
        in_specs=(P("row", "col"), P("row", "col"), P(), P(), P(), P()),
        out_specs=(P("row", "col"), P("row", "col"), P(), P(), P(), P()),
        check_vma=False,
    )
```

```python
import functools

import jax
import jax.numpy as jnp
from jax import lax
from jax.experimental import pallas as pl
from jax.experimental.pallas import tpu as pltpu
from jax.sharding import PartitionSpec as P

DILATION_STEP = 16


epsilon = 1e-05
highest = lax.Precision.HIGHEST


def extended_2(cells, sides, width):
    for axis, dim in sides:
        count = lax.axis_size(axis)
        ends = count - 1
        head = lax.slice_in_dim(cells, 0, width, axis=dim)
        tail = lax.slice_in_dim(cells, cells.shape[dim] - width, cells.shape[dim], axis=dim)
        cells = jnp.concatenate(
            [
                lax.ppermute(tail, axis, [(i, (i + 1) % count) for i in range(ends)]),
                cells,
                lax.ppermute(head, axis, [((i + 1) % count, i) for i in range(ends)]),
            ],
            axis=dim,
        )
    return cells


def extend(feature_field_patch):
    block_result = extended_2(feature_field_patch, (("row", 0), ("col", 1)), DILATION_STEP)
    return block_result


def tap_windows(extended, row_begin, column_starts, local_row_count, local_column_count):
    pieces = [
        extended[row_begin : row_begin + local_row_count, start : start + local_column_count]
        for start in column_starts
    ]
    joined = jnp.concatenate(pieces, axis=2)
    return joined.reshape(local_row_count * local_column_count, -1)


def dilated(extended, filter_weight, local_row_count, local_column_count):
    channels = filter_weight.shape[2]
    starts = [tap * DILATION_STEP for tap in range(3)]
    summed_taps = jnp.zeros(
        (local_row_count * local_column_count, filter_weight.shape[3]), jnp.float32
    )
    for filter_tap_row in range(3):
        window = tap_windows(
            extended, filter_tap_row * DILATION_STEP, starts, local_row_count, local_column_count
        )
        stacked = filter_weight[filter_tap_row].reshape(3 * channels, -1)
        summed_taps = summed_taps + jnp.dot(
            window, stacked, precision=highest, preferred_element_type=jnp.float32
        )
    return summed_taps.reshape(local_row_count, local_column_count, -1)


def dilated_back(grad_ext, filter_weight, local_row_count, local_column_count):
    channels = filter_weight.shape[3]
    starts = [(2 - tap) * DILATION_STEP for tap in range(3)]
    summed_taps = jnp.zeros(
        (local_row_count * local_column_count, filter_weight.shape[2]), jnp.float32
    )
    for filter_tap_row in range(3):
        window = tap_windows(
            grad_ext,
            (2 - filter_tap_row) * DILATION_STEP,
            starts,
            local_row_count,
            local_column_count,
        )
        stacked = jnp.transpose(filter_weight[filter_tap_row], (0, 2, 1)).reshape(3 * channels, -1)
        summed_taps = summed_taps + jnp.dot(
            window, stacked, precision=highest, preferred_element_type=jnp.float32
        )
    return summed_taps.reshape(local_row_count, local_column_count, -1)


def kernel_grad(extended, grad_tile, local_row_count, local_column_count):
    channels = extended.shape[2]
    starts = [tap * DILATION_STEP for tap in range(3)]
    grad_flat = grad_tile.reshape(-1, grad_tile.shape[2])
    tap_list = []
    for filter_tap_row in range(3):
        window = tap_windows(
            extended, filter_tap_row * DILATION_STEP, starts, local_row_count, local_column_count
        )
        product = lax.dot_general(
            window,
            grad_flat,
            (((0,), (0,)), ((), ())),
            precision=highest,
            preferred_element_type=jnp.float32,
        )
        tap_list.append(product.reshape(3, channels, -1))
    return jnp.stack(tap_list)


def normalize(hidden, cell_count):
    totals = lax.psum(jnp.sum(hidden, axis=(0, 1)), ("row", "col"))
    average = totals / cell_count
    centered = hidden - average
    spread = lax.psum(jnp.sum(centered * centered, axis=(0, 1)), ("row", "col"))
    variance = spread / cell_count
    inverse = lax.rsqrt(variance + epsilon)
    return ((hidden - average) * inverse, inverse)


def normalize_back(grad_normed, normed, inverse, gain_row, cell_count):
    shift_sum, gain_sum = lax.psum(
        (jnp.sum(grad_normed, axis=(0, 1)), jnp.sum(grad_normed * normed, axis=(0, 1))),
        ("row", "col"),
    )
    grad_scaled = grad_normed * gain_row
    grad_hidden = inverse * (
        grad_scaled
        - gain_row * shift_sum / cell_count
        - normed * (gain_row * gain_sum / cell_count)
    )
    return (grad_hidden, gain_sum, shift_sum)


def elu_slope(values):
    return jnp.where(values > 0, 1.0, jnp.exp(jnp.minimum(values, 0.0)))


def mirror_tile(tile_in):
    local_row_count, local_column_count, channels = tile_in.shape
    row_devices = lax.axis_size("row")
    col_devices = lax.axis_size("col")
    row_part = local_row_count // col_devices
    group = row_devices // col_devices
    sectioned = tile_in.reshape(col_devices, row_part, local_column_count, channels)
    sectioned = lax.all_to_all(sectioned, "col", split_axis=0, concat_axis=0, tiled=True)
    sectioned = (
        sectioned.reshape(col_devices, row_part, group, local_row_count, channels)
        .transpose(0, 2, 1, 3, 4)
        .reshape(row_devices, row_part, local_row_count, channels)
    )
    sectioned = lax.all_to_all(
        lax.all_to_all(sectioned, "row", split_axis=0, concat_axis=0, tiled=True),
        "col",
        split_axis=0,
        concat_axis=0,
        tiled=True,
    )
    sectioned = sectioned.reshape(
        col_devices, group, row_part, local_row_count, channels
    ).transpose(3, 1, 0, 2, 4)
    return sectioned.reshape(local_row_count, local_column_count, channels)


def general_body(pair_map, cotangent, conv_one, conv_two, norm_gain, norm_shift):
    channels = conv_one.shape[2]
    local_row_count = pair_map.shape[0]
    local_column_count = pair_map.shape[1] // channels
    residues = float(local_row_count * lax.axis_size("row"))
    cell_count = float(
        local_row_count * local_column_count * lax.axis_size("row") * lax.axis_size("col")
    )
    feature_field_patch = pair_map.reshape(local_row_count, local_column_count, channels)
    field_ext = extend(feature_field_patch)
    first_conv = dilated(field_ext, conv_one, local_row_count, local_column_count)
    normed_one, inverse_one = normalize(first_conv, cell_count)
    before_one = normed_one * norm_gain[0] + norm_shift[0]
    active = jax.nn.elu(before_one)
    active_ext = extend(active)
    second_conv = dilated(active_ext, conv_two, local_row_count, local_column_count)
    normed_two, inverse_two = normalize(second_conv, cell_count)
    summed = feature_field_patch + normed_two * norm_gain[1] + norm_shift[1]
    block_out = jax.nn.elu(summed)
    symmetric = 0.5 * (block_out + mirror_tile(block_out))
    grad_in = cotangent.reshape(local_row_count, local_column_count, channels)
    grad_out = 0.5 * (grad_in + mirror_tile(grad_in))
    grad_sum = grad_out * elu_slope(summed)
    grad_second, gain_two, shift_two = normalize_back(
        grad_sum, normed_two, inverse_two, norm_gain[1], cell_count
    )
    second_ext = extend(grad_second)
    grad_active = dilated_back(second_ext, conv_two, local_row_count, local_column_count)
    kernel_two = kernel_grad(active_ext, grad_second, local_row_count, local_column_count)
    grad_before = grad_active * elu_slope(before_one)
    grad_first, gain_one, shift_one = normalize_back(
        grad_before, normed_one, inverse_one, norm_gain[0], cell_count
    )
    first_ext = extend(grad_first)
    grad_field = grad_sum + dilated_back(first_ext, conv_one, local_row_count, local_column_count)
    kernel_one = kernel_grad(field_ext, grad_first, local_row_count, local_column_count)
    total_one, total_two = lax.psum((kernel_one, kernel_two), ("row", "col"))
    grad_gains = jnp.stack([gain_one, gain_two]) / residues
    grad_shifts = jnp.stack([shift_one, shift_two]) / residues
    return (
        symmetric.reshape(local_row_count, local_column_count * channels),
        grad_field.reshape(local_row_count, local_column_count * channels),
        total_one / residues,
        total_two / residues,
        grad_gains,
        grad_shifts,
    )


SLOTS = 8
LANES = 128
HALF = 64
ROWS = 256
AXES = ("row", "col")
VMEM_BYTES = 8 << 20
TAP_SOURCES = ((1, 2), (2, 3), (3, 0))


def phase_table(devices):
    pairs = [(r, s) for r in range(DILATION_STEP) for s in range(r + 1, DILATION_STEP)]
    table = []
    taken = 0
    diagonal = DILATION_STEP // 2
    for device in range(devices):
        count = SLOTS // 2 - (1 if device < diagonal else 0)
        upper = pairs[taken : taken + count]
        taken += count
        lower = [(s, r) for r, s in upper]
        if device < diagonal:
            upper = upper + [(2 * device, 2 * device)]
            lower = lower + [(2 * device + 1, 2 * device + 1)]
        table.append(upper + lower)
    return table


def device_index():
    return lax.axis_index("row") * lax.axis_size("col") + lax.axis_index("col")


def lane_low(shape):
    return lax.broadcasted_iota(jnp.int32, shape, len(shape) - 1) < HALF


def swap_halves(values):
    return pltpu.roll(values, HALF, values.ndim - 1)


def fold_halves(values):
    return values + swap_halves(values)


def twice(row):
    return jnp.concatenate([row, row], axis=1)


def two_parts(values):
    high = values.astype(jnp.bfloat16)
    return high, (values - high.astype(jnp.float32)).astype(jnp.bfloat16)


def close_dot(left, right, dims):
    if dims[0] == (0,):
        left, dims = left.T, ((1,), dims[1])
    left_high, left_low = two_parts(left)
    right_high, right_low = two_parts(right)
    return lax.dot_general(
        jnp.concatenate([left_high, left_high, left_low], axis=1),
        jnp.concatenate([right_high, right_low, right_high], axis=dims[1][0]),
        (dims, ((), ())),
        preferred_element_type=jnp.float32,
    )


def split_phases(tile_ref, scratch_ref):
    low = lane_low((DILATION_STEP, LANES))
    for t in range(DILATION_STEP // 2):
        first = tile_ref[:, t * LANES : (t + 1) * LANES]
        begin = DILATION_STEP * HALF + t * LANES
        second = tile_ref[:, begin : begin + LANES]
        row = 2 * t * DILATION_STEP
        scratch_ref[row : row + DILATION_STEP, :] = jnp.where(low, first, swap_halves(second))
        row += DILATION_STEP
        scratch_ref[row : row + DILATION_STEP, :] = jnp.where(low, swap_halves(first), second)


def join_phases(scratch_ref, tile_ref):
    low = lane_low((DILATION_STEP, LANES))
    for t in range(DILATION_STEP // 2):
        row = 2 * t * DILATION_STEP
        even = scratch_ref[row : row + DILATION_STEP, :]
        odd = scratch_ref[row + DILATION_STEP : row + 2 * DILATION_STEP, :]
        tile_ref[:, t * LANES : (t + 1) * LANES] = jnp.where(low, even, swap_halves(odd))
        begin = DILATION_STEP * HALF + t * LANES
        tile_ref[:, begin : begin + LANES] = jnp.where(low, swap_halves(even), odd)


def pack_rows(table, scratch_ref, send_ref, stride):
    for device, slots in enumerate(table):
        for k, (r, s) in enumerate(slots):
            source = s * DILATION_STEP + r
            target = device * stride + k
            send_ref[target : target + 1, :] = scratch_ref[source : source + 1, :]


def unpack_rows(table, recv_ref, scratch_ref, stride, offset):
    for device, slots in enumerate(table):
        for k, (r, s) in enumerate(slots):
            target = s * DILATION_STEP + r
            source = device * stride + offset + k
            scratch_ref[target : target + 1, :] = recv_ref[source : source + 1, :]


def slot_rows(ref, stride, devices):
    return jnp.concatenate(
        [ref[d * stride : d * stride + SLOTS, :] for d in range(devices)], axis=0
    )


def neighbours(values):
    zero = jnp.zeros((SLOTS, LANES), jnp.float32)
    ahead = jnp.concatenate([values[SLOTS:], zero], axis=0)
    behind = jnp.concatenate([zero, values[:-SLOTS]], axis=0)
    place = (lax.broadcasted_iota(jnp.int32, (ROWS, LANES), 0) >> 3) & 3
    low = lane_low((ROWS, LANES))
    side = jnp.where(low, jnp.where(place == 3, 0.0, ahead), jnp.where(place == 0, 0.0, behind))
    return jnp.concatenate([side, values], axis=1)


def forward_weight(weight_ref):
    zero = jnp.zeros((HALF, HALF), jnp.float32)
    taps = []
    for a in range(3):
        w = [weight_ref[a, b] for b in range(3)]
        blocks = [(zero, w[2]), (w[0], zero), (w[1], w[0]), (w[2], w[1])]
        taps.append(
            jnp.concatenate([jnp.concatenate(list(b), axis=1) for b in blocks], axis=0)
        )
    return jnp.concatenate(taps, axis=1)


def backward_weight(weight_ref):
    zero = jnp.zeros((HALF, HALF), jnp.float32)
    taps = []
    for a in range(3):
        w = [weight_ref[2 - a, 2 - b] for b in range(3)]
        taps.append(jnp.concatenate([zero, w[0], w[1], w[2]], axis=1))
        taps.append(jnp.concatenate([w[2], zero, w[0], w[1]], axis=1))
    return jnp.concatenate(taps, axis=0)


def shifted_sum(parts):
    step = 4 * SLOTS
    zero = jnp.zeros((step, LANES), jnp.float32)
    first, middle, last = (parts[:, a * LANES : (a + 1) * LANES] for a in range(3))
    return (
        middle
        + jnp.concatenate([zero, first[:-step]], axis=0)
        + jnp.concatenate([last[step:], zero], axis=0)
    )


def spread_shifts(values):
    step = 4 * SLOTS
    zero = jnp.zeros((step, LANES), jnp.float32)
    return jnp.concatenate(
        [
            jnp.concatenate([values[step:], zero], axis=0),
            values,
            jnp.concatenate([zero, values[:-step]], axis=0),
        ],
        axis=1,
    )


def tap_rows(product):
    quarter = HALF // 2
    low = lane_low((quarter, LANES))
    pieces = []
    for a in range(3):
        part = product[:, a * LANES : (a + 1) * LANES]
        for even, odd in TAP_SOURCES:
            first = part[even * HALF : (even + 1) * HALF]
            second = part[odd * HALF : (odd + 1) * HALF]
            kept = jnp.where(low, first[:quarter], second[quarter:])
            moved = jnp.where(low, first[quarter:], second[:quarter])
            pieces.append(kept + swap_halves(moved))
    return jnp.concatenate(pieces, axis=0)


def kernel_rows(joined, grad):
    return tap_rows(close_dot(joined, spread_shifts(grad), ((0,), (0,))))


def kernel_rows_and_sums(joined, grad, devices):
    row = lax.broadcasted_iota(jnp.int32, (ROWS, LANES), 0)
    tap = (lax.broadcasted_iota(jnp.int32, (ROWS, LANES), 1) & (HALF - 1)) >> 4
    step = 4 * SLOTS
    outside = ((tap == 0) & (row >= ROWS - step)) | ((tap == 2) & (row < step))
    ones = jnp.where(outside, 0.0, 1.0)
    product = close_dot(
        joined, jnp.concatenate([spread_shifts(grad), ones], axis=1), ((0,), (0,))
    )
    part = product[:, 3 * LANES :]
    quarter = HALF // 2
    low = lane_low((quarter, LANES))
    row = lax.broadcasted_iota(jnp.int32, (quarter, LANES), 0) & 15
    lane = lax.broadcasted_iota(jnp.int32, (quarter, LANES), 1) & (HALF - 1)
    pieces = []
    for even, odd in TAP_SOURCES:
        both = part[even * HALF : (even + 1) * HALF] + part[odd * HALF : (odd + 1) * HALF]
        pieces.append(jnp.where(low, both[:quarter], both[quarter:]))
    sums = jnp.concatenate(
        [jnp.where(lane - 16 * a == row, piece, 0.0) for a in range(3) for piece in pieces], axis=0
    )
    total = sums.shape[0]
    share = total // devices
    first = share * lax.broadcasted_iota(jnp.int32, (devices, total), 0)
    index = lax.broadcasted_iota(jnp.int32, (devices, total), 1)
    picked = jnp.where((index >= first) & (index < first + share), 1.0, 0.0)
    return tap_rows(product), close_dot(picked, sums, ((1,), (0,)))


def widen_sums(row, share):
    lane = lax.broadcasted_iota(jnp.int32, (share, LANES), 1)
    index = lax.broadcasted_iota(jnp.int32, (share, LANES), 0) + share * device_index()
    picked = jnp.where(lane & 15 == index & 15, row, 0.0)
    low = lane < HALF
    first = jnp.sum(jnp.where(low, picked, 0.0), axis=1, keepdims=True)
    second = jnp.sum(jnp.where(low, 0.0, picked), axis=1, keepdims=True)
    return jnp.where(low, first, second)


def local_stats(hidden):
    count = 2.0 * ROWS
    mean = fold_halves(jnp.sum(hidden, axis=0, keepdims=True)) / count
    centered = hidden - mean
    spread = fold_halves(jnp.sum(centered * centered, axis=0, keepdims=True))
    return jnp.where(lane_low((1, LANES)), mean, spread)


def combine_stats(rows, devices):
    low = lane_low((devices, LANES))
    means = jnp.where(low, rows, swap_halves(rows))
    spreads = jnp.where(low, swap_halves(rows), rows)
    mean = jnp.sum(means, axis=0, keepdims=True) / devices
    apart = means - mean
    total = jnp.sum(spreads + (2.0 * ROWS) * (apart * apart), axis=0, keepdims=True)
    return mean, lax.rsqrt(total / (2.0 * ROWS * devices) + epsilon)


def elu_value(values):
    return jnp.where(values > 0, values, jnp.exp(jnp.minimum(values, 0.0)) - 1.0)


def pair_sums(grad, normed):
    plain = fold_halves(jnp.sum(grad, axis=0, keepdims=True))
    scaled = fold_halves(jnp.sum(grad * normed, axis=0, keepdims=True))
    return jnp.where(lane_low((1, LANES)), plain, scaled)


def split_sums(rows):
    total = jnp.sum(rows, axis=0, keepdims=True)
    other = swap_halves(total)
    low = lane_low((1, LANES))
    return jnp.where(low, total, other), jnp.where(low, other, total)


def norm_back(grad, normed, inverse, gain, shift_sum, gain_sum, cells):
    return inverse * (gain * grad - gain * shift_sum / cells - normed * (gain * gain_sum / cells))


def mirrored(values, own_mask):
    low = lane_low((SLOTS, LANES))
    tiles = [values[i * SLOTS : (i + 1) * SLOTS] for i in range(ROWS // SLOTS)]
    pieces = []
    for p in range(SLOTS):
        for c in range(4):
            even = tiles[2 * c * 4 + p // 2]
            odd = tiles[(2 * c + 1) * 4 + p // 2]
            if p % 2 == 0:
                piece = jnp.where(low, even, swap_halves(odd))
            else:
                piece = jnp.where(low, swap_halves(even), odd)
            pieces.append(jnp.where(own_mask, piece, pltpu.roll(piece, 4, 0)))
    return jnp.concatenate(pieces, axis=0)


def own_mirrors():
    me = device_index()
    slot = lax.broadcasted_iota(jnp.int32, (SLOTS, LANES), 0)
    return (slot & 3 == 3) & (me < DILATION_STEP // 2)


def first_kernel(
    table, x_ref, g_ref, gain_ref, shift_ref, send_ref, grad_ref, affine_ref, scratch_ref, other_ref
):
    split_phases(x_ref, scratch_ref)
    pack_rows(table, scratch_ref, send_ref, SLOTS)
    split_phases(g_ref, other_ref)
    pack_rows(table, other_ref, grad_ref, SLOTS)
    affine_ref[...] = jnp.concatenate(
        [twice(gain_ref[...]), twice(shift_ref[...]), jnp.zeros((4, LANES), jnp.float32)], axis=0
    )


def conv_one_kernel(devices, x_ref, weight_ref, g_ref, hidden_ref, send_ref):
    stride = SLOTS + 1
    hidden = shifted_sum(
        close_dot(neighbours(x_ref[...]), forward_weight(weight_ref), ((1,), (0,)))
    )
    hidden_ref[...] = hidden
    stats = local_stats(hidden)
    for d in range(devices):
        send_ref[d * stride : d * stride + SLOTS, :] = g_ref[d * SLOTS : (d + 1) * SLOTS, :]
        send_ref[d * stride + SLOTS : (d + 1) * stride, :] = stats


def conv_two_kernel(
    devices, recv_ref, hidden_ref, x_ref, weight_ref, affine_ref,
    normed_ref, inverse_ref, active_ref, second_ref, send_ref, scratch_ref,
):
    mean, inverse = combine_stats(recv_ref[pl.ds(SLOTS, devices, stride=SLOTS + 1), :], devices)
    normed = (hidden_ref[...] - mean) * inverse
    normed_ref[...] = normed
    inverse_ref[...] = inverse
    active = elu_value(normed * affine_ref[0:1, :] + affine_ref[2:3, :])
    active_ref[...] = active
    second = shifted_sum(
        close_dot(neighbours(active), forward_weight(weight_ref), ((1,), (0,)))
    )
    second_ref[...] = second
    stats = local_stats(second)
    rows, sums = kernel_rows_and_sums(neighbours(x_ref[...]), normed, devices)
    scratch_ref[...] = rows
    share = rows.shape[0] // devices
    stride = share + 2
    for d in range(devices):
        begin = d * stride
        send_ref[begin : begin + share, :] = scratch_ref[d * share : (d + 1) * share, :]
        send_ref[begin + share : begin + share + 1, :] = sums[d : d + 1, :]
        send_ref[begin + share + 1 : begin + stride, :] = stats


def output_kernel(
    devices, share, recv_ref, second_ref, x_ref, grad_ref, affine_ref,
    normed_ref, inverse_ref, sum_ref, send_ref,
):
    stride = SLOTS + 1
    mean, inverse = combine_stats(
        recv_ref[pl.ds(share + 1, devices, stride=share + 2), :], devices
    )
    normed = (second_ref[...] - mean) * inverse
    normed_ref[...] = normed
    inverse_ref[...] = inverse
    summed = x_ref[...] + normed * affine_ref[1:2, :] + affine_ref[3:4, :]
    slope = jnp.exp(jnp.minimum(summed, 0.0))
    out = jnp.where(summed > 0, summed, slope - 1.0)
    own = own_mirrors()
    symmetric = 0.5 * (out + mirrored(out, own))
    for d in range(devices):
        send_ref[d * stride : d * stride + SLOTS, :] = symmetric[d * SLOTS : (d + 1) * SLOTS]
    grad_in = slot_rows(grad_ref, stride, devices)
    grad_out = 0.5 * (grad_in + mirrored(grad_in, own))
    grad_sum = grad_out * jnp.where(summed > 0, 1.0, slope)
    sum_ref[...] = grad_sum
    sums = pair_sums(grad_sum, normed)
    for d in range(devices):
        send_ref[d * stride + SLOTS : (d + 1) * stride, :] = sums


def back_two_kernel(
    devices, recv_ref, sum_ref, normed_two_ref, inverse_two_ref, active_ref, normed_ref,
    x_ref, weight_ref, affine_ref, before_ref, total_ref, sums_ref, second_ref, give_ref,
):
    cells = 2.0 * ROWS * devices
    shift_sum, gain_sum = split_sums(recv_ref[pl.ds(SLOTS, devices, stride=SLOTS + 1), :])
    total_ref[...] = jnp.where(lane_low((1, LANES)), shift_sum, gain_sum)
    grad_second = norm_back(
        sum_ref[...], normed_two_ref[...], inverse_two_ref[...], affine_ref[1:2, :],
        shift_sum, gain_sum, cells,
    )
    grad_active = shifted_sum(
        close_dot(neighbours(grad_second), backward_weight(weight_ref), ((1,), (1,)))
    )
    normed = normed_ref[...]
    before = normed * affine_ref[0:1, :] + affine_ref[2:3, :]
    grad_before = grad_active * jnp.where(before > 0, 1.0, jnp.exp(jnp.minimum(before, 0.0)))
    before_ref[...] = grad_before
    sums_ref[...] = pair_sums(grad_before, normed)
    second_ref[...] = grad_second
    even = first_core()
    give_ref[...] = kernel_rows(
        neighbours(jnp.where(even, active_ref[...], x_ref[...])),
        jnp.where(even, grad_second, grad_before),
    )


def first_core():
    return lax.axis_index("row") & 1 == 0


def pair_kernel(devices, share, keep_ref, got_ref, sums_ref, send_ref):
    stride = share + 1
    sums = sums_ref[...]
    for d in range(devices):
        rows = slice(d * share, (d + 1) * share)
        send_ref[d * stride : d * stride + share, :] = keep_ref[rows, :] + got_ref[rows, :]
        send_ref[d * stride + share : (d + 1) * stride, :] = sums


def keep_kernel(
    devices, share, recv_ref, weight_ref, before_ref, x_ref, second_ref, active_ref,
    keep_ref, rows_ref, constant_ref, joined_ref,
):
    even = first_core()
    keep_ref[...] = kernel_rows(
        neighbours(jnp.where(even, x_ref[...], active_ref[...])),
        jnp.where(even, before_ref[...], second_ref[...]),
    )
    rows = reduce_share(recv_ref, range(devices), 0, share + 1, share + 2)
    rows_ref[...] = rows[:share]
    constant_ref[...] = widen_sums(rows[share : share + 1], share)
    joined_ref[...] = backward_weight(weight_ref)


def reduce_share(ref, sources, begin, size, stride):
    total = None
    for d in sources:
        rows = ref[d * stride + begin : d * stride + begin + size, :]
        total = rows if total is None else total + rows
    return total


def owner_core(device):
    return device // 4 % 2


def back_one_kernel(
    devices, share, residues, recv_ref, before_ref, normed_ref, inverse_ref, sum_ref, joined_ref,
    affine_ref, rows_ref, constant_ref, total_ref, send_ref,
):
    cells = 2.0 * ROWS * devices
    stride = share + 1
    shift_sum, gain_sum = split_sums(recv_ref[pl.ds(share, devices, stride=stride), :])
    total_ref[...] = jnp.where(lane_low((1, LANES)), shift_sum, gain_sum)
    gain, inverse = affine_ref[0:1, :], inverse_ref[...]
    grad_first = norm_back(
        before_ref[...], normed_ref[...], inverse, gain, shift_sum, gain_sum, cells
    )
    field = sum_ref[...] + shifted_sum(
        close_dot(neighbours(grad_first), joined_ref[...], ((1,), (1,)))
    )
    sources = range(devices)
    one = reduce_share(recv_ref, [d for d in sources if not owner_core(d)], 0, share, stride)
    two = reduce_share(recv_ref, [d for d in sources if owner_core(d)], 0, share, stride)
    one = (inverse * gain) * (
        one - constant_ref[...] * (shift_sum / cells) - rows_ref[...] * (gain_sum / cells)
    )
    one, two = one / residues, two / residues
    stride = share + SLOTS
    for d in range(devices):
        begin = d * stride
        send_ref[begin : begin + SLOTS, :] = field[d * SLOTS : (d + 1) * SLOTS]
        send_ref[begin + SLOTS : begin + stride, :] = two if owner_core(d) else one


def map_kernel(
    table, share, residues, sym_recv_ref, recv_ref, total_one_ref, total_two_ref,
    sym_ref, map_ref, gain_ref, shift_ref, scratch_ref, other_ref,
):
    unpack_rows(table, sym_recv_ref, scratch_ref, SLOTS + 1, 0)
    join_phases(scratch_ref, sym_ref)
    unpack_rows(table, recv_ref, other_ref, share + SLOTS, 0)
    join_phases(other_ref, map_ref)
    for index, total_ref in ((0, total_one_ref), (1, total_two_ref)):
        total = total_ref[...] / residues
        shift_ref[index : index + 1, :] = total[:, :HALF]
        gain_ref[index : index + 1, :] = swap_halves(total)[:, :HALF]


def grad_kernel(devices, share, mine_ref, partner_ref, one_ref, two_ref, first_ref, second_ref):
    stride = share + SLOTS
    for source_ref, rows_ref in ((mine_ref, first_ref), (partner_ref, second_ref)):
        for d in range(devices):
            begin = d * stride + SLOTS
            rows_ref[d * share : (d + 1) * share, :] = source_ref[begin : begin + share, :]
    even = first_core()
    for tap in range(9):
        begin = tap * HALF // 2
        mine = first_ref[begin : begin + HALF // 2, :]
        partner = second_ref[begin : begin + HALF // 2, :]
        one, two = jnp.where(even, mine, partner), jnp.where(even, partner, mine)
        for block, out_ref in ((one, one_ref), (two, two_ref)):
            out_ref[tap, : HALF // 2, :] = block[:, :HALF]
            out_ref[tap, HALF // 2 :, :] = swap_halves(block)[:, :HALF]


def call(body, shapes, scratch=(), cost=None):
    return pl.pallas_call(
        body,
        out_shape=[jax.ShapeDtypeStruct(s, jnp.float32) for s in shapes],
        scratch_shapes=[pltpu.VMEM(s, jnp.float32) for s in scratch],
        compiler_params=pltpu.CompilerParams(vmem_limit_bytes=VMEM_BYTES),
        cost_estimate=cost,
    )


def exchange(rows, devices):
    sent = rows.reshape(devices, 1, -1)
    received = lax.all_to_all(sent, AXES, split_axis=0, concat_axis=0, tiled=True)
    return received.reshape(-1, LANES)


def phase_body(pair_map, cotangent, conv_one, conv_two, norm_gain, norm_shift):
    devices = lax.axis_size("row") * lax.axis_size("col")
    residues = float(pair_map.shape[0] * lax.axis_size("row"))
    table = phase_table(devices)
    share = ROWS * 9 // 8 // devices
    whole, line, rows = (ROWS, LANES), (1, LANES), (devices * share, LANES)
    part = functools.partial

    def wide(count):
        return (devices * count, LANES)

    inputs = (pair_map, cotangent, norm_gain, norm_shift)
    send, grad_sent, affine = call(
        part(first_kernel, table), [whole, whole, (SLOTS, LANES)], [whole, whole]
    )(*(pltpu.with_memory_space_constraint(v, pltpu.HBM) for v in inputs))
    x = exchange(send, devices)
    hidden, send = call(part(conv_one_kernel, devices), [whole, wide(SLOTS + 1)])(
        x, conv_one, grad_sent
    )
    grad_recv = exchange(send, devices)
    normed_one, inverse_one, active, second, send = call(
        part(conv_two_kernel, devices), [whole, line, whole, whole, wide(share + 2)], [rows]
    )(grad_recv, hidden, x, conv_two, affine)
    normed_recv = exchange(send, devices)
    normed_two, inverse_two, grad_sum, send = call(
        part(output_kernel, devices, share), [whole, line, whole, wide(SLOTS + 1)]
    )(normed_recv, second, x, grad_recv, affine)
    sym_recv = exchange(send, devices)
    cores = [(i, i ^ 1) for i in range(lax.axis_size("row"))]
    cost = pl.CostEstimate(flops=4 << 20, bytes_accessed=4 << 20, transcendentals=0)
    grad_before, total_two, sums, grad_second, give = call(
        part(back_two_kernel, devices), [whole, line, line, whole, rows]
    )(
        sym_recv, grad_sum, normed_two, inverse_two, active, normed_one, x, conv_two, affine
    )
    got = lax.ppermute(give, "row", cores)
    keep, normed_rows, constant, joined = call(
        part(keep_kernel, devices, share),
        [rows, (share, LANES), (share, LANES), (3 * LANES, 2 * LANES)],
        cost=cost,
    )(normed_recv, conv_one, grad_before, x, grad_second, active)
    (send,) = call(part(pair_kernel, devices, share), [wide(share + 1)])(
        keep, got, sums
    )
    recv = exchange(send, devices)
    total_one, send = call(
        part(back_one_kernel, devices, share, residues), [line, wide(share + SLOTS)]
    )(
        recv, grad_before, normed_one, inverse_one, grad_sum, joined, affine, normed_rows, constant
    )
    recv = exchange(send, devices)
    taps = conv_one.shape[0] * conv_one.shape[1]
    partner = lax.ppermute(recv, "row", cores)
    sym_out, grad_map, grad_gain, grad_shift = call(
        part(map_kernel, table, share, residues),
        [pair_map.shape, pair_map.shape, norm_gain.shape, norm_shift.shape],
        [whole, whole],
        cost,
    )(sym_recv, recv, total_one, total_two)
    grad_one, grad_two = call(
        part(grad_kernel, devices, share), [(taps, HALF, HALF)] * 2, [rows, rows]
    )(recv, partner)
    return (
        sym_out,
        grad_map,
        grad_one.reshape(conv_one.shape),
        grad_two.reshape(conv_two.shape),
        grad_gain,
        grad_shift,
    )


def body(pair_map, cotangent, conv_one, conv_two, norm_gain, norm_shift):
    devices = lax.axis_size("row") * lax.axis_size("col")
    fits = (
        conv_one.shape == (3, 3, HALF, HALF)
        and pair_map.shape == (DILATION_STEP, 2 * DILATION_STEP * HALF)
        and lax.axis_size("row") == SLOTS
        and lax.axis_size("col") == 4
    )
    plan = phase_body if fits else general_body
    return plan(pair_map, cotangent, conv_one, conv_two, norm_gain, norm_shift)


def solution(mesh):
    return jax.shard_map(
        body,
        mesh=mesh,
        in_specs=(P("row", "col"), P("row", "col"), P(), P(), P(), P()),
        out_specs=(P("row", "col"), P("row", "col"), P(), P(), P(), P()),
        check_vma=False,
    )
```

```python
import functools

import jax
import jax.numpy as jnp
from jax import lax
from jax.experimental import pallas as pl
from jax.experimental.pallas import tpu as pltpu
from jax.sharding import PartitionSpec as P

DILATION_STEP = 16


epsilon = 1e-05
highest = lax.Precision.HIGHEST


def extended_2(cells, sides, width):
    for axis, dim in sides:
        count = lax.axis_size(axis)
        ends = count - 1
        head = lax.slice_in_dim(cells, 0, width, axis=dim)
        tail = lax.slice_in_dim(cells, cells.shape[dim] - width, cells.shape[dim], axis=dim)
        cells = jnp.concatenate(
            [
                lax.ppermute(tail, axis, [(i, (i + 1) % count) for i in range(ends)]),
                cells,
                lax.ppermute(head, axis, [((i + 1) % count, i) for i in range(ends)]),
            ],
            axis=dim,
        )
    return cells


def extend(feature_field_patch):
    block_result = extended_2(feature_field_patch, (("row", 0), ("col", 1)), DILATION_STEP)
    return block_result


def tap_windows(extended, row_begin, column_starts, local_row_count, local_column_count):
    pieces = [
        extended[row_begin : row_begin + local_row_count, start : start + local_column_count]
        for start in column_starts
    ]
    joined = jnp.concatenate(pieces, axis=2)
    return joined.reshape(local_row_count * local_column_count, -1)


def dilated(extended, filter_weight, local_row_count, local_column_count):
    channels = filter_weight.shape[2]
    starts = [tap * DILATION_STEP for tap in range(3)]
    summed_taps = jnp.zeros(
        (local_row_count * local_column_count, filter_weight.shape[3]), jnp.float32
    )
    for filter_tap_row in range(3):
        window = tap_windows(
            extended, filter_tap_row * DILATION_STEP, starts, local_row_count, local_column_count
        )
        stacked = filter_weight[filter_tap_row].reshape(3 * channels, -1)
        summed_taps = summed_taps + jnp.dot(
            window, stacked, precision=highest, preferred_element_type=jnp.float32
        )
    return summed_taps.reshape(local_row_count, local_column_count, -1)


def dilated_back(grad_ext, filter_weight, local_row_count, local_column_count):
    channels = filter_weight.shape[3]
    starts = [(2 - tap) * DILATION_STEP for tap in range(3)]
    summed_taps = jnp.zeros(
        (local_row_count * local_column_count, filter_weight.shape[2]), jnp.float32
    )
    for filter_tap_row in range(3):
        window = tap_windows(
            grad_ext,
            (2 - filter_tap_row) * DILATION_STEP,
            starts,
            local_row_count,
            local_column_count,
        )
        stacked = jnp.transpose(filter_weight[filter_tap_row], (0, 2, 1)).reshape(3 * channels, -1)
        summed_taps = summed_taps + jnp.dot(
            window, stacked, precision=highest, preferred_element_type=jnp.float32
        )
    return summed_taps.reshape(local_row_count, local_column_count, -1)


def kernel_grad(extended, grad_tile, local_row_count, local_column_count):
    channels = extended.shape[2]
    starts = [tap * DILATION_STEP for tap in range(3)]
    grad_flat = grad_tile.reshape(-1, grad_tile.shape[2])
    tap_list = []
    for filter_tap_row in range(3):
        window = tap_windows(
            extended, filter_tap_row * DILATION_STEP, starts, local_row_count, local_column_count
        )
        product = lax.dot_general(
            window,
            grad_flat,
            (((0,), (0,)), ((), ())),
            precision=highest,
            preferred_element_type=jnp.float32,
        )
        tap_list.append(product.reshape(3, channels, -1))
    return jnp.stack(tap_list)


def normalize(hidden, cell_count):
    totals = lax.psum(jnp.sum(hidden, axis=(0, 1)), ("row", "col"))
    average = totals / cell_count
    centered = hidden - average
    spread = lax.psum(jnp.sum(centered * centered, axis=(0, 1)), ("row", "col"))
    variance = spread / cell_count
    inverse = lax.rsqrt(variance + epsilon)
    return ((hidden - average) * inverse, inverse)


def normalize_back(grad_normed, normed, inverse, gain_row, cell_count):
    shift_sum, gain_sum = lax.psum(
        (jnp.sum(grad_normed, axis=(0, 1)), jnp.sum(grad_normed * normed, axis=(0, 1))),
        ("row", "col"),
    )
    grad_scaled = grad_normed * gain_row
    grad_hidden = inverse * (
        grad_scaled
        - gain_row * shift_sum / cell_count
        - normed * (gain_row * gain_sum / cell_count)
    )
    return (grad_hidden, gain_sum, shift_sum)


def elu_slope(values):
    return jnp.where(values > 0, 1.0, jnp.exp(jnp.minimum(values, 0.0)))


def mirror_tile(tile_in):
    local_row_count, local_column_count, channels = tile_in.shape
    row_devices = lax.axis_size("row")
    col_devices = lax.axis_size("col")
    row_part = local_row_count // col_devices
    group = row_devices // col_devices
    sectioned = tile_in.reshape(col_devices, row_part, local_column_count, channels)
    sectioned = lax.all_to_all(sectioned, "col", split_axis=0, concat_axis=0, tiled=True)
    sectioned = (
        sectioned.reshape(col_devices, row_part, group, local_row_count, channels)
        .transpose(0, 2, 1, 3, 4)
        .reshape(row_devices, row_part, local_row_count, channels)
    )
    sectioned = lax.all_to_all(
        lax.all_to_all(sectioned, "row", split_axis=0, concat_axis=0, tiled=True),
        "col",
        split_axis=0,
        concat_axis=0,
        tiled=True,
    )
    sectioned = sectioned.reshape(
        col_devices, group, row_part, local_row_count, channels
    ).transpose(3, 1, 0, 2, 4)
    return sectioned.reshape(local_row_count, local_column_count, channels)


def general_body(pair_map, cotangent, conv_one, conv_two, norm_gain, norm_shift):
    channels = conv_one.shape[2]
    local_row_count = pair_map.shape[0]
    local_column_count = pair_map.shape[1] // channels
    residues = float(local_row_count * lax.axis_size("row"))
    cell_count = float(
        local_row_count * local_column_count * lax.axis_size("row") * lax.axis_size("col")
    )
    feature_field_patch = pair_map.reshape(local_row_count, local_column_count, channels)
    field_ext = extend(feature_field_patch)
    first_conv = dilated(field_ext, conv_one, local_row_count, local_column_count)
    normed_one, inverse_one = normalize(first_conv, cell_count)
    before_one = normed_one * norm_gain[0] + norm_shift[0]
    active = jax.nn.elu(before_one)
    active_ext = extend(active)
    second_conv = dilated(active_ext, conv_two, local_row_count, local_column_count)
    normed_two, inverse_two = normalize(second_conv, cell_count)
    summed = feature_field_patch + normed_two * norm_gain[1] + norm_shift[1]
    block_out = jax.nn.elu(summed)
    symmetric = 0.5 * (block_out + mirror_tile(block_out))
    grad_in = cotangent.reshape(local_row_count, local_column_count, channels)
    grad_out = 0.5 * (grad_in + mirror_tile(grad_in))
    grad_sum = grad_out * elu_slope(summed)
    grad_second, gain_two, shift_two = normalize_back(
        grad_sum, normed_two, inverse_two, norm_gain[1], cell_count
    )
    second_ext = extend(grad_second)
    grad_active = dilated_back(second_ext, conv_two, local_row_count, local_column_count)
    kernel_two = kernel_grad(active_ext, grad_second, local_row_count, local_column_count)
    grad_before = grad_active * elu_slope(before_one)
    grad_first, gain_one, shift_one = normalize_back(
        grad_before, normed_one, inverse_one, norm_gain[0], cell_count
    )
    first_ext = extend(grad_first)
    grad_field = grad_sum + dilated_back(first_ext, conv_one, local_row_count, local_column_count)
    kernel_one = kernel_grad(field_ext, grad_first, local_row_count, local_column_count)
    total_one, total_two = lax.psum((kernel_one, kernel_two), ("row", "col"))
    grad_gains = jnp.stack([gain_one, gain_two]) / residues
    grad_shifts = jnp.stack([shift_one, shift_two]) / residues
    return (
        symmetric.reshape(local_row_count, local_column_count * channels),
        grad_field.reshape(local_row_count, local_column_count * channels),
        total_one / residues,
        total_two / residues,
        grad_gains,
        grad_shifts,
    )


SLOTS = 8
LANES = 128
HALF = 64
ROWS = 256
AXES = ("row", "col")
VMEM_BYTES = 8 << 20
TAP_SOURCES = ((1, 2), (2, 3), (3, 0))


def phase_table(devices):
    pairs = [(r, s) for r in range(DILATION_STEP) for s in range(r + 1, DILATION_STEP)]
    table = []
    taken = 0
    diagonal = DILATION_STEP // 2
    for device in range(devices):
        count = SLOTS // 2 - (1 if device < diagonal else 0)
        upper = pairs[taken : taken + count]
        taken += count
        lower = [(s, r) for r, s in upper]
        if device < diagonal:
            upper = upper + [(2 * device, 2 * device)]
            lower = lower + [(2 * device + 1, 2 * device + 1)]
        table.append(upper + lower)
    return table


def device_index():
    return lax.axis_index("row") * lax.axis_size("col") + lax.axis_index("col")


def lane_low(shape):
    return lax.broadcasted_iota(jnp.int32, shape, len(shape) - 1) < HALF


def swap_halves(values):
    return pltpu.roll(values, HALF, values.ndim - 1)


def fold_halves(values):
    return values + swap_halves(values)


def twice(row):
    return jnp.concatenate([row, row], axis=1)


def two_parts(values):
    high = values.astype(jnp.bfloat16)
    return high, (values - high.astype(jnp.float32)).astype(jnp.bfloat16)


def close_dot(left, right, dims):
    if dims[0] == (0,):
        left, dims = left.T, ((1,), dims[1])
    left_high, left_low = two_parts(left)
    right_high, right_low = two_parts(right)
    return lax.dot_general(
        jnp.concatenate([left_high, left_high, left_low], axis=1),
        jnp.concatenate([right_high, right_low, right_high], axis=dims[1][0]),
        (dims, ((), ())),
        preferred_element_type=jnp.float32,
    )


def split_phases(tile_ref, scratch_ref):
    low = lane_low((DILATION_STEP, LANES))
    for t in range(DILATION_STEP // 2):
        first = tile_ref[:, t * LANES : (t + 1) * LANES]
        begin = DILATION_STEP * HALF + t * LANES
        second = tile_ref[:, begin : begin + LANES]
        row = 2 * t * DILATION_STEP
        scratch_ref[row : row + DILATION_STEP, :] = jnp.where(low, first, swap_halves(second))
        row += DILATION_STEP
        scratch_ref[row : row + DILATION_STEP, :] = jnp.where(low, swap_halves(first), second)


def join_phases(scratch_ref, tile_ref):
    low = lane_low((DILATION_STEP, LANES))
    for t in range(DILATION_STEP // 2):
        row = 2 * t * DILATION_STEP
        even = scratch_ref[row : row + DILATION_STEP, :]
        odd = scratch_ref[row + DILATION_STEP : row + 2 * DILATION_STEP, :]
        tile_ref[:, t * LANES : (t + 1) * LANES] = jnp.where(low, even, swap_halves(odd))
        begin = DILATION_STEP * HALF + t * LANES
        tile_ref[:, begin : begin + LANES] = jnp.where(low, swap_halves(even), odd)


def pack_rows(table, scratch_ref, send_ref, stride):
    for device, slots in enumerate(table):
        for k, (r, s) in enumerate(slots):
            source = s * DILATION_STEP + r
            target = device * stride + k
            send_ref[target : target + 1, :] = scratch_ref[source : source + 1, :]


def unpack_rows(table, recv_ref, scratch_ref, stride, offset):
    for device, slots in enumerate(table):
        for k, (r, s) in enumerate(slots):
            target = s * DILATION_STEP + r
            source = device * stride + offset + k
            scratch_ref[target : target + 1, :] = recv_ref[source : source + 1, :]


def slot_rows(ref, stride, devices):
    return jnp.concatenate(
        [ref[d * stride : d * stride + SLOTS, :] for d in range(devices)], axis=0
    )


def neighbours(values):
    zero = jnp.zeros((SLOTS, LANES), jnp.float32)
    ahead = jnp.concatenate([values[SLOTS:], zero], axis=0)
    behind = jnp.concatenate([zero, values[:-SLOTS]], axis=0)
    place = (lax.broadcasted_iota(jnp.int32, (ROWS, LANES), 0) >> 3) & 3
    low = lane_low((ROWS, LANES))
    side = jnp.where(low, jnp.where(place == 3, 0.0, ahead), jnp.where(place == 0, 0.0, behind))
    return jnp.concatenate([side, values], axis=1)


def forward_weight(weight_ref):
    zero = jnp.zeros((HALF, HALF), jnp.float32)
    taps = []
    for a in range(3):
        w = [weight_ref[a, b] for b in range(3)]
        blocks = [(zero, w[2]), (w[0], zero), (w[1], w[0]), (w[2], w[1])]
        taps.append(
            jnp.concatenate([jnp.concatenate(list(b), axis=1) for b in blocks], axis=0)
        )
    return jnp.concatenate(taps, axis=1)


def backward_weight(weight_ref):
    zero = jnp.zeros((HALF, HALF), jnp.float32)
    taps = []
    for a in range(3):
        w = [weight_ref[2 - a, 2 - b] for b in range(3)]
        taps.append(jnp.concatenate([zero, w[0], w[1], w[2]], axis=1))
        taps.append(jnp.concatenate([w[2], zero, w[0], w[1]], axis=1))
    return jnp.concatenate(taps, axis=0)


def shifted_sum(parts):
    step = 4 * SLOTS
    zero = jnp.zeros((step, LANES), jnp.float32)
    first, middle, last = (parts[:, a * LANES : (a + 1) * LANES] for a in range(3))
    return (
        middle
        + jnp.concatenate([zero, first[:-step]], axis=0)
        + jnp.concatenate([last[step:], zero], axis=0)
    )


def spread_shifts(values):
    step = 4 * SLOTS
    zero = jnp.zeros((step, LANES), jnp.float32)
    return jnp.concatenate(
        [
            jnp.concatenate([values[step:], zero], axis=0),
            values,
            jnp.concatenate([zero, values[:-step]], axis=0),
        ],
        axis=1,
    )


def tap_rows(product):
    quarter = HALF // 2
    low = lane_low((quarter, LANES))
    pieces = []
    for a in range(3):
        part = product[:, a * LANES : (a + 1) * LANES]
        for even, odd in TAP_SOURCES:
            first = part[even * HALF : (even + 1) * HALF]
            second = part[odd * HALF : (odd + 1) * HALF]
            kept = jnp.where(low, first[:quarter], second[quarter:])
            moved = jnp.where(low, first[quarter:], second[:quarter])
            pieces.append(kept + swap_halves(moved))
    return jnp.concatenate(pieces, axis=0)


def kernel_rows(joined, grad):
    return tap_rows(close_dot(joined, spread_shifts(grad), ((0,), (0,))))


def kernel_rows_and_sums(joined, grad, devices):
    row = lax.broadcasted_iota(jnp.int32, (ROWS, LANES), 0)
    tap = (lax.broadcasted_iota(jnp.int32, (ROWS, LANES), 1) & (HALF - 1)) >> 4
    step = 4 * SLOTS
    outside = ((tap == 0) & (row >= ROWS - step)) | ((tap == 2) & (row < step))
    ones = jnp.where(outside, 0.0, 1.0)
    product = close_dot(
        joined, jnp.concatenate([spread_shifts(grad), ones], axis=1), ((0,), (0,))
    )
    part = product[:, 3 * LANES :]
    quarter = HALF // 2
    low = lane_low((quarter, LANES))
    row = lax.broadcasted_iota(jnp.int32, (quarter, LANES), 0) & 15
    lane = lax.broadcasted_iota(jnp.int32, (quarter, LANES), 1) & (HALF - 1)
    pieces = []
    for even, odd in TAP_SOURCES:
        both = part[even * HALF : (even + 1) * HALF] + part[odd * HALF : (odd + 1) * HALF]
        pieces.append(jnp.where(low, both[:quarter], both[quarter:]))
    sums = jnp.concatenate(
        [jnp.where(lane - 16 * a == row, piece, 0.0) for a in range(3) for piece in pieces], axis=0
    )
    total = sums.shape[0]
    share = total // devices
    first = share * lax.broadcasted_iota(jnp.int32, (devices, total), 0)
    index = lax.broadcasted_iota(jnp.int32, (devices, total), 1)
    picked = jnp.where((index >= first) & (index < first + share), 1.0, 0.0)
    return tap_rows(product), close_dot(picked, sums, ((1,), (0,)))


def widen_sums(row, share):
    lane = lax.broadcasted_iota(jnp.int32, (share, LANES), 1)
    index = lax.broadcasted_iota(jnp.int32, (share, LANES), 0) + share * device_index()
    picked = jnp.where(lane & 15 == index & 15, row, 0.0)
    low = lane < HALF
    first = jnp.sum(jnp.where(low, picked, 0.0), axis=1, keepdims=True)
    second = jnp.sum(jnp.where(low, 0.0, picked), axis=1, keepdims=True)
    return jnp.where(low, first, second)


def local_stats(hidden):
    count = 2.0 * ROWS
    mean = fold_halves(jnp.sum(hidden, axis=0, keepdims=True)) / count
    centered = hidden - mean
    spread = fold_halves(jnp.sum(centered * centered, axis=0, keepdims=True))
    return jnp.where(lane_low((1, LANES)), mean, spread)


def combine_stats(rows, devices):
    low = lane_low((devices, LANES))
    means = jnp.where(low, rows, swap_halves(rows))
    spreads = jnp.where(low, swap_halves(rows), rows)
    mean = jnp.sum(means, axis=0, keepdims=True) / devices
    apart = means - mean
    total = jnp.sum(spreads + (2.0 * ROWS) * (apart * apart), axis=0, keepdims=True)
    return mean, lax.rsqrt(total / (2.0 * ROWS * devices) + epsilon)


def elu_value(values):
    return jnp.where(values > 0, values, jnp.exp(jnp.minimum(values, 0.0)) - 1.0)


def pair_sums(grad, normed):
    plain = fold_halves(jnp.sum(grad, axis=0, keepdims=True))
    scaled = fold_halves(jnp.sum(grad * normed, axis=0, keepdims=True))
    return jnp.where(lane_low((1, LANES)), plain, scaled)


def split_sums(rows):
    total = jnp.sum(rows, axis=0, keepdims=True)
    other = swap_halves(total)
    low = lane_low((1, LANES))
    return jnp.where(low, total, other), jnp.where(low, other, total)


def norm_back(grad, normed, inverse, gain, shift_sum, gain_sum, cells):
    return inverse * (gain * grad - gain * shift_sum / cells - normed * (gain * gain_sum / cells))


def mirrored(values, own_mask):
    low = lane_low((SLOTS, LANES))
    tiles = [values[i * SLOTS : (i + 1) * SLOTS] for i in range(ROWS // SLOTS)]
    pieces = []
    for p in range(SLOTS):
        for c in range(4):
            even = tiles[2 * c * 4 + p // 2]
            odd = tiles[(2 * c + 1) * 4 + p // 2]
            if p % 2 == 0:
                piece = jnp.where(low, even, swap_halves(odd))
            else:
                piece = jnp.where(low, swap_halves(even), odd)
            pieces.append(jnp.where(own_mask, piece, pltpu.roll(piece, 4, 0)))
    return jnp.concatenate(pieces, axis=0)


def own_mirrors():
    me = device_index()
    slot = lax.broadcasted_iota(jnp.int32, (SLOTS, LANES), 0)
    return (slot & 3 == 3) & (me < DILATION_STEP // 2)


def first_kernel(
    table, x_ref, g_ref, gain_ref, shift_ref, send_ref, grad_ref, affine_ref, scratch_ref, other_ref
):
    split_phases(x_ref, scratch_ref)
    pack_rows(table, scratch_ref, send_ref, SLOTS)
    split_phases(g_ref, other_ref)
    pack_rows(table, other_ref, grad_ref, SLOTS)
    affine_ref[...] = jnp.concatenate(
        [twice(gain_ref[...]), twice(shift_ref[...]), jnp.zeros((4, LANES), jnp.float32)], axis=0
    )


def conv_one_kernel(devices, x_ref, weight_ref, g_ref, hidden_ref, send_ref):
    stride = SLOTS + 1
    hidden = shifted_sum(
        close_dot(neighbours(x_ref[...]), forward_weight(weight_ref), ((1,), (0,)))
    )
    hidden_ref[...] = hidden
    stats = local_stats(hidden)
    for d in range(devices):
        send_ref[d * stride : d * stride + SLOTS, :] = g_ref[d * SLOTS : (d + 1) * SLOTS, :]
        send_ref[d * stride + SLOTS : (d + 1) * stride, :] = stats


def conv_two_kernel(
    devices, recv_ref, hidden_ref, x_ref, weight_ref, affine_ref,
    normed_ref, inverse_ref, active_ref, second_ref, send_ref, scratch_ref,
):
    mean, inverse = combine_stats(recv_ref[pl.ds(SLOTS, devices, stride=SLOTS + 1), :], devices)
    normed = (hidden_ref[...] - mean) * inverse
    normed_ref[...] = normed
    inverse_ref[...] = inverse
    active = elu_value(normed * affine_ref[0:1, :] + affine_ref[2:3, :])
    active_ref[...] = active
    second = shifted_sum(
        close_dot(neighbours(active), forward_weight(weight_ref), ((1,), (0,)))
    )
    second_ref[...] = second
    stats = local_stats(second)
    rows, sums = kernel_rows_and_sums(neighbours(x_ref[...]), normed, devices)
    scratch_ref[...] = rows
    share = rows.shape[0] // devices
    stride = share + 2
    for d in range(devices):
        begin = d * stride
        send_ref[begin : begin + share, :] = scratch_ref[d * share : (d + 1) * share, :]
        send_ref[begin + share : begin + share + 1, :] = sums[d : d + 1, :]
        send_ref[begin + share + 1 : begin + stride, :] = stats


def output_kernel(
    devices, share, recv_ref, second_ref, x_ref, grad_ref, affine_ref,
    normed_ref, inverse_ref, sum_ref, send_ref,
):
    stride = SLOTS + 1
    mean, inverse = combine_stats(
        recv_ref[pl.ds(share + 1, devices, stride=share + 2), :], devices
    )
    normed = (second_ref[...] - mean) * inverse
    normed_ref[...] = normed
    inverse_ref[...] = inverse
    summed = x_ref[...] + normed * affine_ref[1:2, :] + affine_ref[3:4, :]
    slope = jnp.exp(jnp.minimum(summed, 0.0))
    out = jnp.where(summed > 0, summed, slope - 1.0)
    own = own_mirrors()
    symmetric = 0.5 * (out + mirrored(out, own))
    for d in range(devices):
        send_ref[d * stride : d * stride + SLOTS, :] = symmetric[d * SLOTS : (d + 1) * SLOTS]
    grad_in = slot_rows(grad_ref, stride, devices)
    grad_out = 0.5 * (grad_in + mirrored(grad_in, own))
    grad_sum = grad_out * jnp.where(summed > 0, 1.0, slope)
    sum_ref[...] = grad_sum
    sums = pair_sums(grad_sum, normed)
    for d in range(devices):
        send_ref[d * stride + SLOTS : (d + 1) * stride, :] = sums


def back_two_kernel(
    devices, recv_ref, sum_ref, normed_two_ref, inverse_two_ref, active_ref, normed_ref,
    x_ref, weight_ref, affine_ref, before_ref, total_ref, sums_ref, second_ref, give_ref,
):
    cells = 2.0 * ROWS * devices
    shift_sum, gain_sum = split_sums(recv_ref[pl.ds(SLOTS, devices, stride=SLOTS + 1), :])
    total_ref[...] = jnp.where(lane_low((1, LANES)), shift_sum, gain_sum)
    grad_second = norm_back(
        sum_ref[...], normed_two_ref[...], inverse_two_ref[...], affine_ref[1:2, :],
        shift_sum, gain_sum, cells,
    )
    grad_active = shifted_sum(
        close_dot(neighbours(grad_second), backward_weight(weight_ref), ((1,), (1,)))
    )
    normed = normed_ref[...]
    before = normed * affine_ref[0:1, :] + affine_ref[2:3, :]
    grad_before = grad_active * jnp.where(before > 0, 1.0, jnp.exp(jnp.minimum(before, 0.0)))
    before_ref[...] = grad_before
    sums_ref[...] = pair_sums(grad_before, normed)
    second_ref[...] = grad_second
    even = first_core()
    give_ref[...] = kernel_rows(
        neighbours(jnp.where(even, active_ref[...], x_ref[...])),
        jnp.where(even, grad_second, grad_before),
    )


def first_core():
    return lax.axis_index("row") & 1 == 0


def pair_kernel(devices, share, keep_ref, got_ref, sums_ref, send_ref):
    stride = share + 1
    sums = sums_ref[...]
    for d in range(devices):
        rows = slice(d * share, (d + 1) * share)
        send_ref[d * stride : d * stride + share, :] = keep_ref[rows, :] + got_ref[rows, :]
        send_ref[d * stride + share : (d + 1) * stride, :] = sums


def keep_kernel(
    devices, share, recv_ref, weight_ref, before_ref, x_ref, second_ref, active_ref,
    keep_ref, rows_ref, constant_ref, joined_ref,
):
    even = first_core()
    keep_ref[...] = kernel_rows(
        neighbours(jnp.where(even, x_ref[...], active_ref[...])),
        jnp.where(even, before_ref[...], second_ref[...]),
    )
    rows = reduce_share(recv_ref, range(devices), 0, share + 1, share + 2)
    rows_ref[...] = rows[:share]
    constant_ref[...] = widen_sums(rows[share : share + 1], share)
    joined_ref[...] = backward_weight(weight_ref)


def reduce_share(ref, sources, begin, size, stride):
    total = None
    for d in sources:
        rows = ref[d * stride + begin : d * stride + begin + size, :]
        total = rows if total is None else total + rows
    return total


def owner_core(device):
    return device // 4 % 2


def back_one_kernel(
    devices, share, residues, recv_ref, before_ref, normed_ref, inverse_ref, sum_ref, joined_ref,
    affine_ref, rows_ref, constant_ref, total_ref, send_ref,
):
    cells = 2.0 * ROWS * devices
    stride = share + 1
    shift_sum, gain_sum = split_sums(recv_ref[pl.ds(share, devices, stride=stride), :])
    total_ref[...] = jnp.where(lane_low((1, LANES)), shift_sum, gain_sum)
    gain, inverse = affine_ref[0:1, :], inverse_ref[...]
    grad_first = norm_back(
        before_ref[...], normed_ref[...], inverse, gain, shift_sum, gain_sum, cells
    )
    field = sum_ref[...] + shifted_sum(
        close_dot(neighbours(grad_first), joined_ref[...], ((1,), (1,)))
    )
    sources = range(devices)
    one = reduce_share(recv_ref, [d for d in sources if not owner_core(d)], 0, share, stride)
    two = reduce_share(recv_ref, [d for d in sources if owner_core(d)], 0, share, stride)
    one = (inverse * gain) * (
        one - constant_ref[...] * (shift_sum / cells) - rows_ref[...] * (gain_sum / cells)
    )
    one, two = one / residues, two / residues
    stride = share + SLOTS
    for d in range(devices):
        begin = d * stride
        send_ref[begin : begin + SLOTS, :] = field[d * SLOTS : (d + 1) * SLOTS]
        send_ref[begin + SLOTS : begin + stride, :] = two if owner_core(d) else one


def pick_kernel(devices, share, recv_ref, rows_ref):
    for d in range(devices):
        begin = d * (share + SLOTS) + SLOTS
        rows_ref[d * share : (d + 1) * share, :] = recv_ref[begin : begin + share, :]


def write_taps(rows_ref, taps_ref, first, one_ref, two_ref, sem):
    for tap in range(9):
        block = rows_ref[tap * HALF // 2 : (tap + 1) * HALF // 2, :]
        taps_ref[tap, : HALF // 2, :] = block[:, :HALF]
        taps_ref[tap, HALF // 2 :, :] = swap_halves(block)[:, :HALF]

    @pl.when(first)
    def _():
        pltpu.make_async_copy(taps_ref, one_ref, sem).start()

    @pl.when(jnp.logical_not(first))
    def _():
        pltpu.make_async_copy(taps_ref, two_ref, sem).start()

    return pltpu.make_async_copy(taps_ref, one_ref, sem)


def map_kernel(
    table, share, residues, sym_recv_ref, recv_ref, rows_ref, total_one_ref, total_two_ref,
    sym_ref, map_ref, gain_ref, shift_ref, one_ref, two_ref,
    scratch_ref, other_ref, taps_ref, sem,
):
    copy = write_taps(rows_ref, taps_ref, first_core(), one_ref, two_ref, sem)
    unpack_rows(table, sym_recv_ref, scratch_ref, SLOTS + 1, 0)
    join_phases(scratch_ref, sym_ref)
    unpack_rows(table, recv_ref, other_ref, share + SLOTS, 0)
    join_phases(other_ref, map_ref)
    for index, total_ref in ((0, total_one_ref), (1, total_two_ref)):
        total = total_ref[...] / residues
        shift_ref[index : index + 1, :] = total[:, :HALF]
        gain_ref[index : index + 1, :] = swap_halves(total)[:, :HALF]
    copy.wait()


def grad_kernel(rows_ref, own_one_ref, own_two_ref, one_ref, two_ref, taps_ref, sem):
    del own_one_ref, own_two_ref
    write_taps(
        rows_ref, taps_ref, jnp.logical_not(first_core()), one_ref, two_ref, sem
    ).wait()


def call(body, shapes, scratch=(), cost=None):
    return pl.pallas_call(
        body,
        out_shape=[jax.ShapeDtypeStruct(s, jnp.float32) for s in shapes],
        scratch_shapes=[pltpu.VMEM(s, jnp.float32) for s in scratch],
        compiler_params=pltpu.CompilerParams(vmem_limit_bytes=VMEM_BYTES),
        cost_estimate=cost,
    )


def exchange(rows, devices):
    sent = rows.reshape(devices, 1, -1)
    received = lax.all_to_all(sent, AXES, split_axis=0, concat_axis=0, tiled=True)
    return received.reshape(-1, LANES)


def phase_body(pair_map, cotangent, conv_one, conv_two, norm_gain, norm_shift):
    devices = lax.axis_size("row") * lax.axis_size("col")
    residues = float(pair_map.shape[0] * lax.axis_size("row"))
    table = phase_table(devices)
    share = ROWS * 9 // 8 // devices
    whole, line, rows = (ROWS, LANES), (1, LANES), (devices * share, LANES)
    part = functools.partial

    def wide(count):
        return (devices * count, LANES)

    inputs = (pair_map, cotangent, norm_gain, norm_shift)
    send, grad_sent, affine = call(
        part(first_kernel, table), [whole, whole, (SLOTS, LANES)], [whole, whole]
    )(*(pltpu.with_memory_space_constraint(v, pltpu.HBM) for v in inputs))
    x = exchange(send, devices)
    hidden, send = call(part(conv_one_kernel, devices), [whole, wide(SLOTS + 1)])(
        x, conv_one, grad_sent
    )
    grad_recv = exchange(send, devices)
    normed_one, inverse_one, active, second, send = call(
        part(conv_two_kernel, devices), [whole, line, whole, whole, wide(share + 2)], [rows]
    )(grad_recv, hidden, x, conv_two, affine)
    normed_recv = exchange(send, devices)
    normed_two, inverse_two, grad_sum, send = call(
        part(output_kernel, devices, share), [whole, line, whole, wide(SLOTS + 1)]
    )(normed_recv, second, x, grad_recv, affine)
    sym_recv = exchange(send, devices)
    cores = [(i, i ^ 1) for i in range(lax.axis_size("row"))]
    cost = pl.CostEstimate(flops=4 << 20, bytes_accessed=4 << 20, transcendentals=0)
    grad_before, total_two, sums, grad_second, give = call(
        part(back_two_kernel, devices), [whole, line, line, whole, rows]
    )(
        sym_recv, grad_sum, normed_two, inverse_two, active, normed_one, x, conv_two, affine
    )
    got = lax.ppermute(give, "row", cores)
    keep, normed_rows, constant, joined = call(
        part(keep_kernel, devices, share),
        [rows, (share, LANES), (share, LANES), (3 * LANES, 2 * LANES)],
        cost=cost,
    )(normed_recv, conv_one, grad_before, x, grad_second, active)
    (send,) = call(part(pair_kernel, devices, share), [wide(share + 1)])(
        keep, got, sums
    )
    recv = exchange(send, devices)
    total_one, send = call(
        part(back_one_kernel, devices, share, residues), [line, wide(share + SLOTS)]
    )(
        recv, grad_before, normed_one, inverse_one, grad_sum, joined, affine, normed_rows, constant
    )
    recv = exchange(send, devices)
    taps = conv_one.shape[0] * conv_one.shape[1]
    (collected,) = call(part(pick_kernel, devices, share), [rows])(recv)
    partner = lax.ppermute(collected, "row", cores)
    blocks = jax.ShapeDtypeStruct((taps, HALF, HALF), jnp.float32)
    in_vmem = pl.BlockSpec(memory_space=pltpu.VMEM)
    in_hbm = pl.BlockSpec(memory_space=pl.ANY)
    taps_scratch = [pltpu.VMEM(blocks.shape, jnp.float32), pltpu.SemaphoreType.DMA]
    params = pltpu.CompilerParams(vmem_limit_bytes=VMEM_BYTES)
    sym_out, grad_map, grad_gain, grad_shift, own_one, own_two = pl.pallas_call(
        part(map_kernel, table, share, residues),
        out_shape=[
            jax.ShapeDtypeStruct(v.shape, jnp.float32)
            for v in (pair_map, pair_map, norm_gain, norm_shift)
        ]
        + [blocks] * 2,
        out_specs=[in_vmem] * 4 + [in_hbm] * 2,
        scratch_shapes=[pltpu.VMEM(whole, jnp.float32)] * 2 + taps_scratch,
        compiler_params=params,
        cost_estimate=cost,
    )(sym_recv, recv, collected, total_one, total_two)
    grad_one, grad_two = pl.pallas_call(
        grad_kernel,
        out_shape=[blocks] * 2,
        in_specs=[in_vmem] + [in_hbm] * 2,
        out_specs=[in_hbm] * 2,
        input_output_aliases={1: 0, 2: 1},
        scratch_shapes=taps_scratch,
        compiler_params=params,
    )(partner, own_one, own_two)
    return (
        sym_out,
        grad_map,
        grad_one.reshape(conv_one.shape),
        grad_two.reshape(conv_two.shape),
        grad_gain,
        grad_shift,
    )


def body(pair_map, cotangent, conv_one, conv_two, norm_gain, norm_shift):
    devices = lax.axis_size("row") * lax.axis_size("col")
    fits = (
        conv_one.shape == (3, 3, HALF, HALF)
        and pair_map.shape == (DILATION_STEP, 2 * DILATION_STEP * HALF)
        and lax.axis_size("row") == SLOTS
        and lax.axis_size("col") == 4
    )
    plan = phase_body if fits else general_body
    return plan(pair_map, cotangent, conv_one, conv_two, norm_gain, norm_shift)


def solution(mesh):
    return jax.shard_map(
        body,
        mesh=mesh,
        in_specs=(P("row", "col"), P("row", "col"), P(), P(), P(), P()),
        out_specs=(P("row", "col"), P("row", "col"), P(), P(), P(), P()),
        check_vma=False,
    )
```

```python
import functools

import jax
import jax.numpy as jnp
from jax import lax
from jax.experimental import pallas as pl
from jax.experimental.pallas import tpu as pltpu
from jax.sharding import PartitionSpec as P

DILATION_STEP = 16


epsilon = 1e-05
highest = lax.Precision.HIGHEST


def extended_2(cells, sides, width):
    for axis, dim in sides:
        count = lax.axis_size(axis)
        ends = count - 1
        head = lax.slice_in_dim(cells, 0, width, axis=dim)
        tail = lax.slice_in_dim(cells, cells.shape[dim] - width, cells.shape[dim], axis=dim)
        cells = jnp.concatenate(
            [
                lax.ppermute(tail, axis, [(i, (i + 1) % count) for i in range(ends)]),
                cells,
                lax.ppermute(head, axis, [((i + 1) % count, i) for i in range(ends)]),
            ],
            axis=dim,
        )
    return cells


def extend(feature_field_patch):
    block_result = extended_2(feature_field_patch, (("row", 0), ("col", 1)), DILATION_STEP)
    return block_result


def tap_windows(extended, row_begin, column_starts, local_row_count, local_column_count):
    pieces = [
        extended[row_begin : row_begin + local_row_count, start : start + local_column_count]
        for start in column_starts
    ]
    joined = jnp.concatenate(pieces, axis=2)
    return joined.reshape(local_row_count * local_column_count, -1)


def dilated(extended, filter_weight, local_row_count, local_column_count):
    channels = filter_weight.shape[2]
    starts = [tap * DILATION_STEP for tap in range(3)]
    summed_taps = jnp.zeros(
        (local_row_count * local_column_count, filter_weight.shape[3]), jnp.float32
    )
    for filter_tap_row in range(3):
        window = tap_windows(
            extended, filter_tap_row * DILATION_STEP, starts, local_row_count, local_column_count
        )
        stacked = filter_weight[filter_tap_row].reshape(3 * channels, -1)
        summed_taps = summed_taps + jnp.dot(
            window, stacked, precision=highest, preferred_element_type=jnp.float32
        )
    return summed_taps.reshape(local_row_count, local_column_count, -1)


def dilated_back(grad_ext, filter_weight, local_row_count, local_column_count):
    channels = filter_weight.shape[3]
    starts = [(2 - tap) * DILATION_STEP for tap in range(3)]
    summed_taps = jnp.zeros(
        (local_row_count * local_column_count, filter_weight.shape[2]), jnp.float32
    )
    for filter_tap_row in range(3):
        window = tap_windows(
            grad_ext,
            (2 - filter_tap_row) * DILATION_STEP,
            starts,
            local_row_count,
            local_column_count,
        )
        stacked = jnp.transpose(filter_weight[filter_tap_row], (0, 2, 1)).reshape(3 * channels, -1)
        summed_taps = summed_taps + jnp.dot(
            window, stacked, precision=highest, preferred_element_type=jnp.float32
        )
    return summed_taps.reshape(local_row_count, local_column_count, -1)


def kernel_grad(extended, grad_tile, local_row_count, local_column_count):
    channels = extended.shape[2]
    starts = [tap * DILATION_STEP for tap in range(3)]
    grad_flat = grad_tile.reshape(-1, grad_tile.shape[2])
    tap_list = []
    for filter_tap_row in range(3):
        window = tap_windows(
            extended, filter_tap_row * DILATION_STEP, starts, local_row_count, local_column_count
        )
        product = lax.dot_general(
            window,
            grad_flat,
            (((0,), (0,)), ((), ())),
            precision=highest,
            preferred_element_type=jnp.float32,
        )
        tap_list.append(product.reshape(3, channels, -1))
    return jnp.stack(tap_list)


def normalize(hidden, cell_count):
    totals = lax.psum(jnp.sum(hidden, axis=(0, 1)), ("row", "col"))
    average = totals / cell_count
    centered = hidden - average
    spread = lax.psum(jnp.sum(centered * centered, axis=(0, 1)), ("row", "col"))
    variance = spread / cell_count
    inverse = lax.rsqrt(variance + epsilon)
    return ((hidden - average) * inverse, inverse)


def normalize_back(grad_normed, normed, inverse, gain_row, cell_count):
    shift_sum, gain_sum = lax.psum(
        (jnp.sum(grad_normed, axis=(0, 1)), jnp.sum(grad_normed * normed, axis=(0, 1))),
        ("row", "col"),
    )
    grad_scaled = grad_normed * gain_row
    grad_hidden = inverse * (
        grad_scaled
        - gain_row * shift_sum / cell_count
        - normed * (gain_row * gain_sum / cell_count)
    )
    return (grad_hidden, gain_sum, shift_sum)


def elu_slope(values):
    return jnp.where(values > 0, 1.0, jnp.exp(jnp.minimum(values, 0.0)))


def mirror_tile(tile_in):
    local_row_count, local_column_count, channels = tile_in.shape
    row_devices = lax.axis_size("row")
    col_devices = lax.axis_size("col")
    row_part = local_row_count // col_devices
    group = row_devices // col_devices
    sectioned = tile_in.reshape(col_devices, row_part, local_column_count, channels)
    sectioned = lax.all_to_all(sectioned, "col", split_axis=0, concat_axis=0, tiled=True)
    sectioned = (
        sectioned.reshape(col_devices, row_part, group, local_row_count, channels)
        .transpose(0, 2, 1, 3, 4)
        .reshape(row_devices, row_part, local_row_count, channels)
    )
    sectioned = lax.all_to_all(
        lax.all_to_all(sectioned, "row", split_axis=0, concat_axis=0, tiled=True),
        "col",
        split_axis=0,
        concat_axis=0,
        tiled=True,
    )
    sectioned = sectioned.reshape(
        col_devices, group, row_part, local_row_count, channels
    ).transpose(3, 1, 0, 2, 4)
    return sectioned.reshape(local_row_count, local_column_count, channels)


def general_body(pair_map, cotangent, conv_one, conv_two, norm_gain, norm_shift):
    channels = conv_one.shape[2]
    local_row_count = pair_map.shape[0]
    local_column_count = pair_map.shape[1] // channels
    residues = float(local_row_count * lax.axis_size("row"))
    cell_count = float(
        local_row_count * local_column_count * lax.axis_size("row") * lax.axis_size("col")
    )
    feature_field_patch = pair_map.reshape(local_row_count, local_column_count, channels)
    field_ext = extend(feature_field_patch)
    first_conv = dilated(field_ext, conv_one, local_row_count, local_column_count)
    normed_one, inverse_one = normalize(first_conv, cell_count)
    before_one = normed_one * norm_gain[0] + norm_shift[0]
    active = jax.nn.elu(before_one)
    active_ext = extend(active)
    second_conv = dilated(active_ext, conv_two, local_row_count, local_column_count)
    normed_two, inverse_two = normalize(second_conv, cell_count)
    summed = feature_field_patch + normed_two * norm_gain[1] + norm_shift[1]
    block_out = jax.nn.elu(summed)
    symmetric = 0.5 * (block_out + mirror_tile(block_out))
    grad_in = cotangent.reshape(local_row_count, local_column_count, channels)
    grad_out = 0.5 * (grad_in + mirror_tile(grad_in))
    grad_sum = grad_out * elu_slope(summed)
    grad_second, gain_two, shift_two = normalize_back(
        grad_sum, normed_two, inverse_two, norm_gain[1], cell_count
    )
    second_ext = extend(grad_second)
    grad_active = dilated_back(second_ext, conv_two, local_row_count, local_column_count)
    kernel_two = kernel_grad(active_ext, grad_second, local_row_count, local_column_count)
    grad_before = grad_active * elu_slope(before_one)
    grad_first, gain_one, shift_one = normalize_back(
        grad_before, normed_one, inverse_one, norm_gain[0], cell_count
    )
    first_ext = extend(grad_first)
    grad_field = grad_sum + dilated_back(first_ext, conv_one, local_row_count, local_column_count)
    kernel_one = kernel_grad(field_ext, grad_first, local_row_count, local_column_count)
    total_one, total_two = lax.psum((kernel_one, kernel_two), ("row", "col"))
    grad_gains = jnp.stack([gain_one, gain_two]) / residues
    grad_shifts = jnp.stack([shift_one, shift_two]) / residues
    return (
        symmetric.reshape(local_row_count, local_column_count * channels),
        grad_field.reshape(local_row_count, local_column_count * channels),
        total_one / residues,
        total_two / residues,
        grad_gains,
        grad_shifts,
    )


SLOTS = 8
LANES = 128
HALF = 64
ROWS = 256
AXES = ("row", "col")
VMEM_BYTES = 8 << 20
TAP_SOURCES = ((1, 2), (2, 3), (3, 0))


def phase_table(devices):
    pairs = [(r, s) for r in range(DILATION_STEP) for s in range(r + 1, DILATION_STEP)]
    table = []
    taken = 0
    diagonal = DILATION_STEP // 2
    for device in range(devices):
        count = SLOTS // 2 - (1 if device < diagonal else 0)
        upper = pairs[taken : taken + count]
        taken += count
        lower = [(s, r) for r, s in upper]
        if device < diagonal:
            upper = upper + [(2 * device, 2 * device)]
            lower = lower + [(2 * device + 1, 2 * device + 1)]
        table.append(upper + lower)
    return table


def device_index():
    return lax.axis_index("row") * lax.axis_size("col") + lax.axis_index("col")


def lane_low(shape):
    return lax.broadcasted_iota(jnp.int32, shape, len(shape) - 1) < HALF


def swap_halves(values):
    return pltpu.roll(values, HALF, values.ndim - 1)


def fold_halves(values):
    return values + swap_halves(values)


def twice(row):
    return jnp.concatenate([row, row], axis=1)


def two_parts(values):
    high = values.astype(jnp.bfloat16)
    return high, (values - high.astype(jnp.float32)).astype(jnp.bfloat16)


def close_dot(left, right, dims):
    if dims[0] == (0,):
        left, dims = left.T, ((1,), dims[1])
    left_high, left_low = two_parts(left)
    right_high, right_low = two_parts(right)
    return lax.dot_general(
        jnp.concatenate([left_high, left_high, left_low], axis=1),
        jnp.concatenate([right_high, right_low, right_high], axis=dims[1][0]),
        (dims, ((), ())),
        preferred_element_type=jnp.float32,
    )


def split_phases(tile_ref, scratch_ref):
    low = lane_low((DILATION_STEP, LANES))
    for t in range(DILATION_STEP // 2):
        first = tile_ref[:, t * LANES : (t + 1) * LANES]
        begin = DILATION_STEP * HALF + t * LANES
        second = tile_ref[:, begin : begin + LANES]
        row = 2 * t * DILATION_STEP
        scratch_ref[row : row + DILATION_STEP, :] = jnp.where(low, first, swap_halves(second))
        row += DILATION_STEP
        scratch_ref[row : row + DILATION_STEP, :] = jnp.where(low, swap_halves(first), second)


def join_phases(scratch_ref, tile_ref):
    low = lane_low((DILATION_STEP, LANES))
    for t in range(DILATION_STEP // 2):
        row = 2 * t * DILATION_STEP
        even = scratch_ref[row : row + DILATION_STEP, :]
        odd = scratch_ref[row + DILATION_STEP : row + 2 * DILATION_STEP, :]
        tile_ref[:, t * LANES : (t + 1) * LANES] = jnp.where(low, even, swap_halves(odd))
        begin = DILATION_STEP * HALF + t * LANES
        tile_ref[:, begin : begin + LANES] = jnp.where(low, swap_halves(even), odd)


def pack_rows(table, scratch_ref, send_ref, stride):
    for device, slots in enumerate(table):
        for k, (r, s) in enumerate(slots):
            source = s * DILATION_STEP + r
            target = device * stride + k
            send_ref[target : target + 1, :] = scratch_ref[source : source + 1, :]


def unpack_rows(table, recv_ref, scratch_ref, stride, offset):
    for device, slots in enumerate(table):
        for k, (r, s) in enumerate(slots):
            target = s * DILATION_STEP + r
            source = device * stride + offset + k
            scratch_ref[target : target + 1, :] = recv_ref[source : source + 1, :]


def slot_rows(ref, stride, devices):
    return jnp.concatenate(
        [ref[d * stride : d * stride + SLOTS, :] for d in range(devices)], axis=0
    )


def neighbours(values):
    zero = jnp.zeros((SLOTS, LANES), jnp.float32)
    ahead = jnp.concatenate([values[SLOTS:], zero], axis=0)
    behind = jnp.concatenate([zero, values[:-SLOTS]], axis=0)
    place = (lax.broadcasted_iota(jnp.int32, (ROWS, LANES), 0) >> 3) & 3
    low = lane_low((ROWS, LANES))
    side = jnp.where(low, jnp.where(place == 3, 0.0, ahead), jnp.where(place == 0, 0.0, behind))
    return jnp.concatenate([side, values], axis=1)


def forward_weight(weight_ref):
    zero = jnp.zeros((HALF, HALF), jnp.float32)
    taps = []
    for a in range(3):
        w = [weight_ref[a, b] for b in range(3)]
        blocks = [(zero, w[2]), (w[0], zero), (w[1], w[0]), (w[2], w[1])]
        taps.append(
            jnp.concatenate([jnp.concatenate(list(b), axis=1) for b in blocks], axis=0)
        )
    return jnp.concatenate(taps, axis=1)


def backward_weight(weight_ref):
    zero = jnp.zeros((HALF, HALF), jnp.float32)
    taps = []
    for a in range(3):
        w = [weight_ref[2 - a, 2 - b] for b in range(3)]
        taps.append(jnp.concatenate([zero, w[0], w[1], w[2]], axis=1))
        taps.append(jnp.concatenate([w[2], zero, w[0], w[1]], axis=1))
    return jnp.concatenate(taps, axis=0)


def shifted_sum(parts):
    step = 4 * SLOTS
    zero = jnp.zeros((step, LANES), jnp.float32)
    first, middle, last = (parts[:, a * LANES : (a + 1) * LANES] for a in range(3))
    return (
        middle
        + jnp.concatenate([zero, first[:-step]], axis=0)
        + jnp.concatenate([last[step:], zero], axis=0)
    )


def spread_shifts(values):
    step = 4 * SLOTS
    zero = jnp.zeros((step, LANES), jnp.float32)
    return jnp.concatenate(
        [
            jnp.concatenate([values[step:], zero], axis=0),
            values,
            jnp.concatenate([zero, values[:-step]], axis=0),
        ],
        axis=1,
    )


def tap_rows(product):
    quarter = HALF // 2
    low = lane_low((quarter, LANES))
    pieces = []
    for a in range(3):
        part = product[:, a * LANES : (a + 1) * LANES]
        for even, odd in TAP_SOURCES:
            first = part[even * HALF : (even + 1) * HALF]
            second = part[odd * HALF : (odd + 1) * HALF]
            kept = jnp.where(low, first[:quarter], second[quarter:])
            moved = jnp.where(low, first[quarter:], second[:quarter])
            pieces.append(kept + swap_halves(moved))
    return jnp.concatenate(pieces, axis=0)


def kernel_rows(joined, grad):
    return tap_rows(close_dot(joined, spread_shifts(grad), ((0,), (0,))))


def kernel_rows_and_sums(joined, grad, devices):
    row = lax.broadcasted_iota(jnp.int32, (ROWS, LANES), 0)
    tap = (lax.broadcasted_iota(jnp.int32, (ROWS, LANES), 1) & (HALF - 1)) >> 4
    step = 4 * SLOTS
    outside = ((tap == 0) & (row >= ROWS - step)) | ((tap == 2) & (row < step))
    ones = jnp.where(outside, 0.0, 1.0)
    product = close_dot(
        joined, jnp.concatenate([spread_shifts(grad), ones], axis=1), ((0,), (0,))
    )
    part = product[:, 3 * LANES :]
    quarter = HALF // 2
    low = lane_low((quarter, LANES))
    row = lax.broadcasted_iota(jnp.int32, (quarter, LANES), 0) & 15
    lane = lax.broadcasted_iota(jnp.int32, (quarter, LANES), 1) & (HALF - 1)
    pieces = []
    for even, odd in TAP_SOURCES:
        both = part[even * HALF : (even + 1) * HALF] + part[odd * HALF : (odd + 1) * HALF]
        pieces.append(jnp.where(low, both[:quarter], both[quarter:]))
    sums = jnp.concatenate(
        [jnp.where(lane - 16 * a == row, piece, 0.0) for a in range(3) for piece in pieces], axis=0
    )
    total = sums.shape[0]
    share = total // devices
    first = share * lax.broadcasted_iota(jnp.int32, (devices, total), 0)
    index = lax.broadcasted_iota(jnp.int32, (devices, total), 1)
    picked = jnp.where((index >= first) & (index < first + share), 1.0, 0.0)
    return tap_rows(product), close_dot(picked, sums, ((1,), (0,)))


def widen_sums(row, share):
    lane = lax.broadcasted_iota(jnp.int32, (share, LANES), 1)
    index = lax.broadcasted_iota(jnp.int32, (share, LANES), 0) + share * device_index()
    picked = jnp.where(lane & 15 == index & 15, row, 0.0)
    low = lane < HALF
    first = jnp.sum(jnp.where(low, picked, 0.0), axis=1, keepdims=True)
    second = jnp.sum(jnp.where(low, 0.0, picked), axis=1, keepdims=True)
    return jnp.where(low, first, second)


def local_stats(hidden):
    count = 2.0 * ROWS
    mean = fold_halves(jnp.sum(hidden, axis=0, keepdims=True)) / count
    centered = hidden - mean
    spread = fold_halves(jnp.sum(centered * centered, axis=0, keepdims=True))
    return jnp.where(lane_low((1, LANES)), mean, spread)


def combine_stats(rows, devices):
    low = lane_low((devices, LANES))
    means = jnp.where(low, rows, swap_halves(rows))
    spreads = jnp.where(low, swap_halves(rows), rows)
    mean = jnp.sum(means, axis=0, keepdims=True) / devices
    apart = means - mean
    total = jnp.sum(spreads + (2.0 * ROWS) * (apart * apart), axis=0, keepdims=True)
    return mean, lax.rsqrt(total / (2.0 * ROWS * devices) + epsilon)


def elu_value(values):
    return jnp.where(values > 0, values, jnp.exp(jnp.minimum(values, 0.0)) - 1.0)


def pair_sums(grad, normed):
    plain = fold_halves(jnp.sum(grad, axis=0, keepdims=True))
    scaled = fold_halves(jnp.sum(grad * normed, axis=0, keepdims=True))
    return jnp.where(lane_low((1, LANES)), plain, scaled)


def split_sums(rows):
    total = jnp.sum(rows, axis=0, keepdims=True)
    other = swap_halves(total)
    low = lane_low((1, LANES))
    return jnp.where(low, total, other), jnp.where(low, other, total)


def norm_back(grad, normed, inverse, gain, shift_sum, gain_sum, cells):
    return inverse * (gain * grad - gain * shift_sum / cells - normed * (gain * gain_sum / cells))


def mirrored(values, own_mask):
    low = lane_low((SLOTS, LANES))
    tiles = [values[i * SLOTS : (i + 1) * SLOTS] for i in range(ROWS // SLOTS)]
    pieces = []
    for p in range(SLOTS):
        for c in range(4):
            even = tiles[2 * c * 4 + p // 2]
            odd = tiles[(2 * c + 1) * 4 + p // 2]
            if p % 2 == 0:
                piece = jnp.where(low, even, swap_halves(odd))
            else:
                piece = jnp.where(low, swap_halves(even), odd)
            pieces.append(jnp.where(own_mask, piece, pltpu.roll(piece, 4, 0)))
    return jnp.concatenate(pieces, axis=0)


def own_mirrors():
    me = device_index()
    slot = lax.broadcasted_iota(jnp.int32, (SLOTS, LANES), 0)
    return (slot & 3 == 3) & (me < DILATION_STEP // 2)


def first_kernel(
    table, x_ref, g_ref, gain_ref, shift_ref, send_ref, grad_ref, affine_ref, scratch_ref, other_ref
):
    split_phases(x_ref, scratch_ref)
    pack_rows(table, scratch_ref, send_ref, SLOTS)
    split_phases(g_ref, other_ref)
    pack_rows(table, other_ref, grad_ref, SLOTS)
    affine_ref[...] = jnp.concatenate(
        [twice(gain_ref[...]), twice(shift_ref[...]), jnp.zeros((4, LANES), jnp.float32)], axis=0
    )


def conv_one_kernel(devices, x_ref, weight_ref, g_ref, hidden_ref, send_ref):
    stride = SLOTS + 1
    hidden = shifted_sum(
        close_dot(neighbours(x_ref[...]), forward_weight(weight_ref), ((1,), (0,)))
    )
    hidden_ref[...] = hidden
    stats = local_stats(hidden)
    for d in range(devices):
        send_ref[d * stride : d * stride + SLOTS, :] = g_ref[d * SLOTS : (d + 1) * SLOTS, :]
        send_ref[d * stride + SLOTS : (d + 1) * stride, :] = stats


def conv_two_kernel(
    devices, recv_ref, hidden_ref, x_ref, weight_ref, affine_ref,
    normed_ref, inverse_ref, active_ref, second_ref, send_ref, scratch_ref,
):
    mean, inverse = combine_stats(recv_ref[pl.ds(SLOTS, devices, stride=SLOTS + 1), :], devices)
    normed = (hidden_ref[...] - mean) * inverse
    normed_ref[...] = normed
    inverse_ref[...] = inverse
    active = elu_value(normed * affine_ref[0:1, :] + affine_ref[2:3, :])
    active_ref[...] = active
    second = shifted_sum(
        close_dot(neighbours(active), forward_weight(weight_ref), ((1,), (0,)))
    )
    second_ref[...] = second
    stats = local_stats(second)
    rows, sums = kernel_rows_and_sums(neighbours(x_ref[...]), normed, devices)
    scratch_ref[...] = rows
    share = rows.shape[0] // devices
    stride = share + 2
    for d in range(devices):
        begin = d * stride
        send_ref[begin : begin + share, :] = scratch_ref[d * share : (d + 1) * share, :]
        send_ref[begin + share : begin + share + 1, :] = sums[d : d + 1, :]
        send_ref[begin + share + 1 : begin + stride, :] = stats


def output_kernel(
    devices, share, recv_ref, second_ref, x_ref, grad_ref, affine_ref,
    normed_ref, inverse_ref, sum_ref, send_ref,
):
    stride = SLOTS + 1
    mean, inverse = combine_stats(
        recv_ref[pl.ds(share + 1, devices, stride=share + 2), :], devices
    )
    normed = (second_ref[...] - mean) * inverse
    normed_ref[...] = normed
    inverse_ref[...] = inverse
    summed = x_ref[...] + normed * affine_ref[1:2, :] + affine_ref[3:4, :]
    slope = jnp.exp(jnp.minimum(summed, 0.0))
    out = jnp.where(summed > 0, summed, slope - 1.0)
    own = own_mirrors()
    symmetric = 0.5 * (out + mirrored(out, own))
    for d in range(devices):
        send_ref[d * stride : d * stride + SLOTS, :] = symmetric[d * SLOTS : (d + 1) * SLOTS]
    grad_in = slot_rows(grad_ref, stride, devices)
    grad_out = 0.5 * (grad_in + mirrored(grad_in, own))
    grad_sum = grad_out * jnp.where(summed > 0, 1.0, slope)
    sum_ref[...] = grad_sum
    sums = pair_sums(grad_sum, normed)
    for d in range(devices):
        send_ref[d * stride + SLOTS : (d + 1) * stride, :] = sums


def back_two_kernel(
    devices, recv_ref, sum_ref, normed_two_ref, inverse_two_ref, active_ref, normed_ref,
    x_ref, weight_ref, affine_ref, before_ref, total_ref, sums_ref, second_ref, give_ref,
):
    cells = 2.0 * ROWS * devices
    shift_sum, gain_sum = split_sums(recv_ref[pl.ds(SLOTS, devices, stride=SLOTS + 1), :])
    total_ref[...] = jnp.where(lane_low((1, LANES)), shift_sum, gain_sum)
    grad_second = norm_back(
        sum_ref[...], normed_two_ref[...], inverse_two_ref[...], affine_ref[1:2, :],
        shift_sum, gain_sum, cells,
    )
    grad_active = shifted_sum(
        close_dot(neighbours(grad_second), backward_weight(weight_ref), ((1,), (1,)))
    )
    normed = normed_ref[...]
    before = normed * affine_ref[0:1, :] + affine_ref[2:3, :]
    grad_before = grad_active * jnp.where(before > 0, 1.0, jnp.exp(jnp.minimum(before, 0.0)))
    before_ref[...] = grad_before
    sums_ref[...] = pair_sums(grad_before, normed)
    second_ref[...] = grad_second
    even = first_core()
    give_ref[...] = kernel_rows(
        neighbours(jnp.where(even, active_ref[...], x_ref[...])),
        jnp.where(even, grad_second, grad_before),
    )


def first_core():
    return lax.axis_index("row") & 1 == 0


def pair_kernel(devices, share, keep_ref, got_ref, sums_ref, send_ref):
    stride = share + 1
    sums = sums_ref[...]
    for d in range(devices):
        rows = slice(d * share, (d + 1) * share)
        send_ref[d * stride : d * stride + share, :] = keep_ref[rows, :] + got_ref[rows, :]
        send_ref[d * stride + share : (d + 1) * stride, :] = sums


def keep_kernel(
    devices, share, recv_ref, weight_ref, before_ref, x_ref, second_ref, active_ref,
    keep_ref, rows_ref, constant_ref, joined_ref,
):
    even = first_core()
    keep_ref[...] = kernel_rows(
        neighbours(jnp.where(even, x_ref[...], active_ref[...])),
        jnp.where(even, before_ref[...], second_ref[...]),
    )
    rows = reduce_share(recv_ref, range(devices), 0, share + 1, share + 2)
    rows_ref[...] = rows[:share]
    constant_ref[...] = widen_sums(rows[share : share + 1], share)
    joined_ref[...] = backward_weight(weight_ref)


def reduce_share(ref, sources, begin, size, stride):
    total = None
    for d in sources:
        rows = ref[d * stride + begin : d * stride + begin + size, :]
        total = rows if total is None else total + rows
    return total


def owner_core(device):
    return device // 4 % 2


def back_one_kernel(
    devices, share, residues, recv_ref, before_ref, normed_ref, inverse_ref, sum_ref, joined_ref,
    affine_ref, rows_ref, constant_ref, total_ref, send_ref,
):
    cells = 2.0 * ROWS * devices
    stride = share + 1
    shift_sum, gain_sum = split_sums(recv_ref[pl.ds(share, devices, stride=stride), :])
    total_ref[...] = jnp.where(lane_low((1, LANES)), shift_sum, gain_sum)
    gain, inverse = affine_ref[0:1, :], inverse_ref[...]
    grad_first = norm_back(
        before_ref[...], normed_ref[...], inverse, gain, shift_sum, gain_sum, cells
    )
    field = sum_ref[...] + shifted_sum(
        close_dot(neighbours(grad_first), joined_ref[...], ((1,), (1,)))
    )
    sources = range(devices)
    one = reduce_share(recv_ref, [d for d in sources if not owner_core(d)], 0, share, stride)
    two = reduce_share(recv_ref, [d for d in sources if owner_core(d)], 0, share, stride)
    one = (inverse * gain) * (
        one - constant_ref[...] * (shift_sum / cells) - rows_ref[...] * (gain_sum / cells)
    )
    one, two = one / residues, two / residues
    stride = share + SLOTS
    for d in range(devices):
        begin = d * stride
        send_ref[begin : begin + SLOTS, :] = field[d * SLOTS : (d + 1) * SLOTS]
        send_ref[begin + SLOTS : begin + stride, :] = two if owner_core(d) else one


def pick_kernel(devices, share, recv_ref, rows_ref):
    for d in range(devices):
        begin = d * (share + SLOTS) + SLOTS
        rows_ref[d * share : (d + 1) * share, :] = recv_ref[begin : begin + share, :]


def write_taps(rows_ref, taps_ref, first, one_ref, two_ref, sems):
    copies = []
    for a in range(3):
        part = pl.ds(3 * a, 3)
        for tap in range(3 * a, 3 * a + 3):
            block = rows_ref[tap * HALF // 2 : (tap + 1) * HALF // 2, :]
            taps_ref[tap, : HALF // 2, :] = block[:, :HALF]
            taps_ref[tap, HALF // 2 :, :] = swap_halves(block)[:, :HALF]
        to_one = pltpu.make_async_copy(taps_ref.at[part], one_ref.at[part], sems.at[a])
        to_two = pltpu.make_async_copy(taps_ref.at[part], two_ref.at[part], sems.at[a])
        pl.when(first)(to_one.start)
        pl.when(jnp.logical_not(first))(to_two.start)
        copies.append(to_one)
    return copies


def map_kernel(
    table, share, residues, sym_recv_ref, recv_ref, rows_ref, total_one_ref, total_two_ref,
    gain_ref, shift_ref, sym_ref, map_ref, one_ref, two_ref,
    scratch_ref, other_ref, gains_ref, shifts_ref, sym_tile_ref, map_tile_ref, taps_ref,
    tile_sems, sems,
):
    copies = write_taps(rows_ref, taps_ref, first_core(), one_ref, two_ref, sems)
    for index, total_ref in ((0, total_one_ref), (1, total_two_ref)):
        total = total_ref[...] / residues
        shifts_ref[index : index + 1, :] = total[:, :HALF]
        gains_ref[index : index + 1, :] = swap_halves(total)[:, :HALF]
    copies.append(pltpu.make_async_copy(gains_ref, gain_ref, tile_sems.at[2]))
    copies[-1].start()
    copies.append(pltpu.make_async_copy(shifts_ref, shift_ref, tile_sems.at[3]))
    copies[-1].start()
    unpack_rows(table, sym_recv_ref, scratch_ref, SLOTS + 1, 0)
    join_phases(scratch_ref, sym_tile_ref)
    copies.append(pltpu.make_async_copy(sym_tile_ref, sym_ref, tile_sems.at[0]))
    copies[-1].start()
    unpack_rows(table, recv_ref, other_ref, share + SLOTS, 0)
    join_phases(other_ref, map_tile_ref)
    copies.append(pltpu.make_async_copy(map_tile_ref, map_ref, tile_sems.at[1]))
    copies[-1].start()
    for copy in copies:
        copy.wait()


def grad_kernel(rows_ref, own_one_ref, own_two_ref, one_ref, two_ref, taps_ref, sems):
    del own_one_ref, own_two_ref
    second = jnp.logical_not(first_core())
    for copy in write_taps(rows_ref, taps_ref, second, one_ref, two_ref, sems):
        copy.wait()


def call(body, shapes, scratch=(), cost=None):
    return pl.pallas_call(
        body,
        out_shape=[jax.ShapeDtypeStruct(s, jnp.float32) for s in shapes],
        scratch_shapes=[pltpu.VMEM(s, jnp.float32) for s in scratch],
        compiler_params=pltpu.CompilerParams(vmem_limit_bytes=VMEM_BYTES),
        cost_estimate=cost,
    )


def exchange(rows, devices):
    sent = rows.reshape(devices, 1, -1)
    received = lax.all_to_all(sent, AXES, split_axis=0, concat_axis=0, tiled=True)
    return received.reshape(-1, LANES)


def phase_body(pair_map, cotangent, conv_one, conv_two, norm_gain, norm_shift):
    devices = lax.axis_size("row") * lax.axis_size("col")
    residues = float(pair_map.shape[0] * lax.axis_size("row"))
    table = phase_table(devices)
    share = ROWS * 9 // 8 // devices
    whole, line, rows = (ROWS, LANES), (1, LANES), (devices * share, LANES)
    part = functools.partial

    def wide(count):
        return (devices * count, LANES)

    inputs = (pair_map, cotangent, norm_gain, norm_shift)
    send, grad_sent, affine = call(
        part(first_kernel, table), [whole, whole, (SLOTS, LANES)], [whole, whole]
    )(*(pltpu.with_memory_space_constraint(v, pltpu.HBM) for v in inputs))
    x = exchange(send, devices)
    hidden, send = call(part(conv_one_kernel, devices), [whole, wide(SLOTS + 1)])(
        x, conv_one, grad_sent
    )
    grad_recv = exchange(send, devices)
    normed_one, inverse_one, active, second, send = call(
        part(conv_two_kernel, devices), [whole, line, whole, whole, wide(share + 2)], [rows]
    )(grad_recv, hidden, x, conv_two, affine)
    normed_recv = exchange(send, devices)
    normed_two, inverse_two, grad_sum, send = call(
        part(output_kernel, devices, share), [whole, line, whole, wide(SLOTS + 1)]
    )(normed_recv, second, x, grad_recv, affine)
    sym_recv = exchange(send, devices)
    cores = [(i, i ^ 1) for i in range(lax.axis_size("row"))]
    cost = pl.CostEstimate(flops=4 << 20, bytes_accessed=4 << 20, transcendentals=0)
    grad_before, total_two, sums, grad_second, give = call(
        part(back_two_kernel, devices), [whole, line, line, whole, rows]
    )(
        sym_recv, grad_sum, normed_two, inverse_two, active, normed_one, x, conv_two, affine
    )
    got = lax.ppermute(give, "row", cores)
    keep, normed_rows, constant, joined = call(
        part(keep_kernel, devices, share),
        [rows, (share, LANES), (share, LANES), (3 * LANES, 2 * LANES)],
        cost=cost,
    )(normed_recv, conv_one, grad_before, x, grad_second, active)
    (send,) = call(part(pair_kernel, devices, share), [wide(share + 1)])(
        keep, got, sums
    )
    recv = exchange(send, devices)
    total_one, send = call(
        part(back_one_kernel, devices, share, residues), [line, wide(share + SLOTS)]
    )(
        recv, grad_before, normed_one, inverse_one, grad_sum, joined, affine, normed_rows, constant
    )
    recv = exchange(send, devices)
    taps = conv_one.shape[0] * conv_one.shape[1]
    (collected,) = call(part(pick_kernel, devices, share), [rows])(recv)
    partner = lax.ppermute(collected, "row", cores)
    blocks = jax.ShapeDtypeStruct((taps, HALF, HALF), jnp.float32)
    in_vmem = pl.BlockSpec(memory_space=pltpu.VMEM)
    in_hbm = pl.BlockSpec(memory_space=pl.ANY)
    taps_scratch = [pltpu.VMEM(blocks.shape, jnp.float32), pltpu.SemaphoreType.DMA((3,))]
    params = pltpu.CompilerParams(vmem_limit_bytes=VMEM_BYTES)
    outs = (norm_gain, norm_shift, pair_map, pair_map)
    tiles = [pltpu.VMEM(v.shape, jnp.float32) for v in outs]
    grad_gain, grad_shift, sym_out, grad_map, own_one, own_two = pl.pallas_call(
        part(map_kernel, table, share, residues),
        out_shape=[jax.ShapeDtypeStruct(v.shape, jnp.float32) for v in outs] + [blocks] * 2,
        out_specs=[in_hbm] * 6,
        scratch_shapes=[pltpu.VMEM(whole, jnp.float32)] * 2
        + tiles
        + taps_scratch[:1]
        + [pltpu.SemaphoreType.DMA((4,))]
        + taps_scratch[1:],
        compiler_params=params,
        cost_estimate=cost,
    )(sym_recv, recv, collected, total_one, total_two)
    grad_one, grad_two = pl.pallas_call(
        grad_kernel,
        out_shape=[blocks] * 2,
        in_specs=[in_vmem] + [in_hbm] * 2,
        out_specs=[in_hbm] * 2,
        input_output_aliases={1: 0, 2: 1},
        scratch_shapes=taps_scratch,
        compiler_params=params,
    )(partner, own_one, own_two)
    return (
        sym_out,
        grad_map,
        grad_one.reshape(conv_one.shape),
        grad_two.reshape(conv_two.shape),
        grad_gain,
        grad_shift,
    )


def body(pair_map, cotangent, conv_one, conv_two, norm_gain, norm_shift):
    devices = lax.axis_size("row") * lax.axis_size("col")
    fits = (
        conv_one.shape == (3, 3, HALF, HALF)
        and pair_map.shape == (DILATION_STEP, 2 * DILATION_STEP * HALF)
        and lax.axis_size("row") == SLOTS
        and lax.axis_size("col") == 4
    )
    plan = phase_body if fits else general_body
    return plan(pair_map, cotangent, conv_one, conv_two, norm_gain, norm_shift)


def solution(mesh):
    return jax.shard_map(
        body,
        mesh=mesh,
        in_specs=(P("row", "col"), P("row", "col"), P(), P(), P(), P()),
        out_specs=(P("row", "col"), P("row", "col"), P(), P(), P(), P()),
        check_vma=False,
    )
```
